128 devices in a mesh: tile: 16 (over x, z_lo, core), col: 8 (over y, z_hi).
Axes of the slice: x: 4, y: 4, z: 4 (z_hi: 2, z_lo: 2; z = z_hi * 2 + z_lo), core: 2. Of those that a mesh axis runs over, the one named last changes fastest.
Arguments:
- u_velocity: float32 [8192, 4096], P('tile', 'col'), may hold values from -12 to 12
- v_velocity: float32 [8192, 4096], P('tile', 'col'), may hold values from -12 to 12
- ocean_mask: int32 [64, 32], P('tile', 'col'), may hold values from 0 to 1, as said below
- tile_owner: int32 [64, 32], P('tile', 'col'), may hold values from 0 to 15, as said below
- lower_edge_quarter_turns: int32 [16], replicated, may hold values from 0 to 3
Outputs:
- library: float32 [16, 8, 16, 16, 1024], P('tile', 'col')
- gram: float32 [16, 16], replicated
The draws below stay inside these ranges and needn't reach their ends.
Inputs may be any that keep to these rules, and one draw needn't show every extreme that they name: `ocean_mask`: in every column of devices (4 x 4 tile blocks), at least one device has only ocean tiles. `tile_owner`: among the ocean tiles of one device at most 1 share an owner; the ocean tiles of one column of devices are spread over its 16 owners so that the owners' counts differ by at most one. Land tiles carry an owner that is not used.
All inputs are finite; a program needn't handle non-finite values.
Results may differ from the reference program's by a relative error of at most 0.00014.
Values sent between devices are 32-bit elements; how exact they have to be, the bound alone decides.
No kernel may reach another device: no remote copies, remote signals or barrier semaphores. Data moves between devices by JAX's collectives and lax.ppermute only.
A program may use at most 192 MiB of HBM per device.

```python
import math
import jax
import jax.numpy as jnp
from jax import lax

CX = 512
CY = 512
PASSES = 8
TS = 32
TERMS = 16
NX = 8192
NY = 4096
GX = 4
GY = 4
TPD = 16
CAP = 1
TC = 1024
N_TILE = 16
N_COL = 8


def rescaled_forcing_field(key):
    key_scale, key_block, key_noise = jax.random.split(key, 3)
    scale = 0.3 * jnp.exp(jax.random.uniform(key_scale, (NX // 32, NY // 32), jnp.float32, 0.0, math.log(10.0)))
    scale = jnp.repeat(jnp.repeat(scale, 32, axis=0), 32, axis=1)
    block = jnp.clip(jax.random.normal(key_block, (NX // 4, NY // 4), jnp.float32), -2.5, 2.5)
    noise = jnp.clip(jax.random.normal(key_noise, (NX, NY), jnp.float32), -2.5, 2.5)
    block = jnp.repeat(jnp.repeat(block, 4, axis=0), 4, axis=1)
    return scale * (block + 0.5 * noise)


def draw_u_velocity(key, part):
    return rescaled_forcing_field(jax.random.fold_in(key, 11))


def draw_v_velocity(key, part):
    return rescaled_forcing_field(jax.random.fold_in(key, 12))


def ocean_tables(key):
    root_random_key = jax.random.fold_in(key, 21)
    level_random_key, key_full, key_roll, key_perm, key_land = jax.random.split(root_random_key, 5)
    level = jax.random.randint(level_random_key, (N_TILE, N_COL), 40, 101)
    full_row = jax.random.randint(key_full, (N_COL,), 0, N_TILE)
    rows_index = jnp.arange(N_TILE, dtype=jnp.int32)
    level = jnp.where(rows_index[:, None] == full_row[None, :], 100, level)
    rolled = jax.random.randint(key_roll, (N_TILE, GX, N_COL, GY), 0, 100)
    mask = (rolled < level[:, None, :, None]).astype(jnp.int32)
    ordered = jnp.transpose(mask, (2, 0, 1, 3)).reshape(N_COL, N_TILE * GX * GY)
    rank = jnp.cumsum(ordered, axis=1) - ordered
    perms = jax.vmap(lambda one: jax.random.permutation(one, N_TILE))(jax.random.split(key_perm, N_COL))
    ocean_owner = jnp.take_along_axis(perms, rank % N_TILE, axis=1)
    land_owner = jax.random.randint(key_land, (N_COL, N_TILE * GX * GY), 0, N_TILE)
    owner = jnp.where(ordered == 1, ocean_owner, land_owner).astype(jnp.int32)
    owner = jnp.transpose(owner.reshape(N_COL, N_TILE, GX, GY), (1, 2, 0, 3)).reshape(N_TILE * GX, N_COL * GY)
    mask = mask.reshape(N_TILE * GX, N_COL * GY)
    return (mask, owner)


def draw_ocean_mask(key, part):
    return ocean_tables(key)[0]


def draw_tile_owner(key, part):
    return ocean_tables(key)[1]


def with_ends(result, own_key, low, top_value):
    longest = result.shape.index(max(result.shape))
    spots = []
    for shift in (0, 1):
        where = [jax.random.randint(jax.random.fold_in(own_key, axis), (), 0, length) for axis, length in enumerate(result.shape)]
        where[longest] = (where[longest] + shift) % result.shape[longest]
        spots.append(tuple(where))
    return result.at[spots[0]].set(low).at[spots[1]].set(top_value)


def setup_inputs(seed: int = 0) -> dict:
    splits = jax.random.split(jax.random.key(seed), 6)
    u_velocity = draw_u_velocity(jax.random.fold_in(splits[5], 71), 0)
    v_velocity = draw_v_velocity(jax.random.fold_in(splits[5], 71), 0)
    ocean_mask = draw_ocean_mask(jax.random.fold_in(splits[5], 71), 0)
    tile_owner = draw_tile_owner(jax.random.fold_in(splits[5], 71), 0)
    lower_edge_quarter_turns = with_ends(jax.random.randint(splits[4], (N_TILE,), 0, 4), jax.random.fold_in(splits[4], 1), 0, 3).astype(jnp.int32)
    return {"u_velocity": u_velocity, "v_velocity": v_velocity, "ocean_mask": ocean_mask, "tile_owner": tile_owner, "lower_edge_quarter_turns": lower_edge_quarter_turns}


KAPPA = 0.2


def quarter(first, second, turns):
    cosine = jnp.where(turns == 0, 1.0, jnp.where(turns == 2, -1.0, 0.0)).astype(first.dtype)
    sine = jnp.where(turns == 1, 1.0, jnp.where(turns == 3, -1.0, 0.0)).astype(first.dtype)
    return cosine * first - sine * second, sine * first + cosine * second


def neighbours(u_field, v_field, lower_edge_quarter_turns, block_rows):
    total = u_field.shape[0]
    index = jnp.arange(total, dtype=jnp.int32)
    block = index // block_rows
    blocks = total // block_rows
    zero_turn = jnp.zeros((total,), jnp.int32)
    k_up = jnp.where(index % block_rows == 0, lower_edge_quarter_turns[block], zero_turn)[:, None]
    k_down = jnp.where(index % block_rows == block_rows - 1, (4 - lower_edge_quarter_turns[(block + 1) % blocks]) % 4, zero_turn)[:, None]
    above = quarter(jnp.roll(u_field, 1, 0), jnp.roll(v_field, 1, 0), k_up)
    below = quarter(jnp.roll(u_field, -1, 0), jnp.roll(v_field, -1, 0), k_down)
    left_pair = (jnp.roll(u_field, 1, 1), jnp.roll(v_field, 1, 1))
    right_pair = (jnp.roll(u_field, -1, 1), jnp.roll(v_field, -1, 1))
    return above, below, left_pair, right_pair


def make_terms(u_part, v_part, vort, strain, stretch):
    listed = [u_part, v_part, vort, strain, stretch, vort * vort, vort * strain, vort * stretch,
              strain * strain, stretch * stretch, strain * stretch, u_part * vort, v_part * vort,
              u_part * strain, v_part * stretch, u_part * v_part]
    return jnp.stack(listed, axis=-2)


def tiled(field):
    shaped = field.reshape(N_TILE, GX, TS, N_COL, GY, TS)
    shaped = jnp.transpose(shaped, (0, 3, 1, 4, 2, 5))
    return shaped.reshape(N_TILE, N_COL, TPD, TC)


def reference(u_velocity, v_velocity, ocean_mask, tile_owner, lower_edge_quarter_turns):
    u_field, v_field = u_velocity, v_velocity
    for step in range(PASSES):
        above, below, left_pair, right_pair = neighbours(u_field, v_field, lower_edge_quarter_turns, CX)
        following_u_velocity = u_field + KAPPA * (above[0] + below[0] + left_pair[0] + right_pair[0] - 4.0 * u_field)
        v_next = v_field + KAPPA * (above[1] + below[1] + left_pair[1] + right_pair[1] - 4.0 * v_field)
        u_field, v_field = following_u_velocity, v_next
    coarse_u = u_field.reshape(NX // 4, 4, NY // 4, 4).mean(axis=(1, 3))
    coarse_v = v_field.reshape(NX // 4, 4, NY // 4, 4).mean(axis=(1, 3))
    above, below, left_pair, right_pair = neighbours(coarse_u, coarse_v, lower_edge_quarter_turns, CX // 4)
    u_dx = (right_pair[0] - left_pair[0]) * 0.5
    u_dy = (below[0] - above[0]) * 0.5
    v_dx = (right_pair[1] - left_pair[1]) * 0.5
    v_dy = (below[1] - above[1]) * 0.5
    vort = v_dx - u_dy
    strain = u_dy + v_dx
    stretch = u_dx - v_dy
    terms = make_terms(tiled(coarse_u), tiled(coarse_v), tiled(vort), tiled(strain), tiled(stretch))
    mask_tiles = jnp.transpose(ocean_mask.reshape(N_TILE, GX, N_COL, GY), (0, 2, 1, 3)).reshape(N_TILE, N_COL, TPD)
    owner_tiles = jnp.transpose(tile_owner.reshape(N_TILE, GX, N_COL, GY), (0, 2, 1, 3)).reshape(N_TILE, N_COL, TPD)
    live = mask_tiles == 1
    local = jnp.arange(TPD, dtype=jnp.int32)
    same = (owner_tiles[..., :, None] == owner_tiles[..., None, :]) & live[..., None, :] & (local[None, :] < local[:, None])
    slot = jnp.sum(same.astype(jnp.int32), axis=-1)
    owners_all = jnp.arange(N_TILE, dtype=jnp.int32)
    slots_all = jnp.arange(CAP, dtype=jnp.int32)
    chosen_terms = (live[..., None, None] & (owner_tiles[..., None, None] == owners_all[:, None])
              & (slot[..., None, None] == slots_all[None, :])).astype(jnp.float32)
    library = jnp.einsum('sclop,sclnx->ocspnx', chosen_terms, terms, precision=lax.Precision.HIGHEST)
    library = library.reshape(N_TILE, N_COL, N_TILE * CAP, TERMS, TC)
    masked = terms * live.astype(jnp.float32)[..., None, None]
    gram = jnp.einsum('sclnx,sclmx->nm', masked, terms, precision=lax.Precision.HIGHEST)
    gram = gram / ((CX // 4) * (CY // 4))
    return library, gram
```

```python
import math

import jax
import jax.numpy as jnp
import ml_dtypes
import numpy as np
from jax import lax
from jax.experimental import pallas as pl
from jax.experimental.pallas import tpu as pltpu
from jax.sharding import PartitionSpec as P

PASSES = 8
KAPPA = 0.2
POOL = 4
CELLS = 128
HALO = 12
SIDE = 32
TERMS = 16
PAD = 8
FULL = CELLS + 2 * PAD
LANES = 128
BASES = 5
BLOCK_ROWS = 48
F32 = jnp.float32
BF16 = jnp.bfloat16

EDGE_COLS = (-1, -2, CELLS + 1, CELLS)
SCALE = KAPPA**PASSES / (POOL * POOL)


def across(power, fine, coarse):
    total = 0
    for inner in range(POOL):
        offset = fine - (POOL * coarse + inner)
        if abs(offset) <= power and (power + offset) % 2 == 0:
            total += math.comb(power, (power + offset) // 2)
    return total


def column_weights():
    fine = CELLS * POOL
    weights = np.zeros((fine, 10 * LANES), np.float32)
    for j in range(PASSES + 1):
        block = PASSES - j
        for coarse in range(CELLS):
            for f in range(max(0, POOL * coarse - 8), min(fine, POOL * coarse + 12)):
                weights[f, block * LANES + coarse] = math.comb(PASSES, j) * across(PASSES - j, f, coarse)
        for place, coarse in enumerate(EDGE_COLS):
            for f in range(max(0, POOL * coarse - 8), min(fine, POOL * coarse + 12)):
                weights[f, 9 * LANES + 4 * j + place] = math.comb(PASSES, j) * across(PASSES - j, f, coarse)
    out = weights.astype(ml_dtypes.bfloat16)
    assert (out.astype(np.float32) == weights).all()
    return out


def send_selectors():
    sel = np.zeros((2, 16, 6 * LANES), np.float32)
    spots = ((0, 1, 1), (1, 1, 0), (2, 0, 0), (8, 0, CELLS - 1), (9, 1, 3), (10, 1, 2))
    for f in range(2):
        for row, source, lane in spots:
            for piece in range(3):
                sel[f, row + 3 * f, (source * 3 + piece) * LANES + lane] = 1.0
    return sel.astype(ml_dtypes.bfloat16)


def place_matrix():
    place = np.zeros((3, 16, 4 * LANES), np.float32)
    for f in range(2):
        add, rim = 2 * f * LANES, (2 * f + 1) * LANES
        place[:, 3 * f + 0, rim + 0] = 1.0
        place[:, 3 * f + 1, add + 0] = 1.0
        place[:, 3 * f + 2, add + 1] = 1.0
        place[:, 8 + 3 * f + 0, add + CELLS - 2] = 1.0
        place[:, 8 + 3 * f + 1, add + CELLS - 1] = 1.0
        place[:, 8 + 3 * f + 2, rim + CELLS - 1] = 1.0
    return place.reshape(48, 4 * LANES).astype(ml_dtypes.bfloat16)


def head(x):
    scaled = x * 65537.0
    return scaled - (scaled - x)


def two_parts(x):
    high = head(x)
    return high.astype(BF16), (x - high).astype(BF16)


def three_parts(x):
    high = head(x)
    rest = x - high
    mid = head(rest)
    return high.astype(BF16), mid.astype(BF16), (rest - mid).astype(BF16)


def dot(a, b, dims=(((1,), (0,)), ((), ()))):
    return lax.dot_general(a, b, dims, preferred_element_type=F32)


def three_rows(t):
    rows = t[0].shape[0]
    up = pltpu.roll(t[3], 1, 0)
    down = pltpu.roll(t[0], rows - 1, 0)
    left, middle, right = t[0] + t[1], t[1] + t[2], t[2] + t[3]
    return [left + up, t[0] + middle, middle + t[3], right + down]


def own_kernel(*refs):
    w_ref, main_ref, edge_ref, high_ref, low_ref, sum_ref, first_ref, last_ref = refs[8:]
    for f in range(2):
        for c in range(4):
            for p in range(POOL):
                high, low = two_parts(refs[4 * f + c][pl.ds(p, CELLS, stride=POOL), :])
                spot = pl.ds((f * POOL + p) * CELLS, CELLS)
                high_ref[spot, c * LANES : (c + 1) * LANES] = high
                low_ref[spot, c * LANES : (c + 1) * LANES] = low
    for t in range(5):
        w = w_ref[:, 2 * t * LANES : 2 * (t + 1) * LANES]
        z = dot(high_ref[...], w) + dot(low_ref[...], w)
        for half in range(2):
            part = z[:, half * LANES : (half + 1) * LANES]
            stage = 2 * t + half
            for f in range(2):
                for_phase = [part[(f * POOL + p) * CELLS : (f * POOL + p + 1) * CELLS] for p in range(POOL)]
                if stage in (0, 9):
                    into = (sum_ref if stage == 0 else first_ref).at[f]
                    for p in range(POOL):
                        into[p, :PAD] = jnp.zeros((PAD, LANES), F32)
                        into[p, PAD:] = for_phase[p]
                else:
                    new = three_rows([sum_ref[f, p] for p in range(POOL)])
                    for p in range(POOL):
                        sum_ref[f, p, :PAD] = new[p][:PAD]
                        sum_ref[f, p, PAD:] = new[p][PAD:] + for_phase[p]
    for f in range(2):
        for p in range(POOL):
            last_ref[f, p] = first_ref[f, p]

    @pl.loop(0, PASSES)
    def _(step):
        for f in range(2):
            new = three_rows([pltpu.roll(last_ref[f, p], LANES - 4, 1) for p in range(POOL)])
            for p in range(POOL):
                last_ref[f, p] = new[p] + first_ref[f, p]

    for f in range(2):
        for from_ref, to_ref in ((sum_ref, main_ref), (last_ref, edge_ref)):
            pooled = ((from_ref[f, 0] + from_ref[f, 1]) + (from_ref[f, 2] + from_ref[f, 3])) * SCALE
            to_ref[f, : PAD + CELLS] = pooled
            to_ref[f, PAD + CELLS :] = pooled[:PAD]


def turn(first, second, k):
    cosine = jnp.where(k == 0, 1.0, jnp.where(k == 2, -1.0, 0.0)).astype(F32)
    sine = jnp.where(k == 1, 1.0, jnp.where(k == 3, -1.0, 0.0)).astype(F32)
    return cosine * first - sine * second, sine * first + cosine * second


def strip_kernel(turns_ref, above_ref, below_ref, w_ref, sel_ref, main_in, edge_in, main_ref, edge_ref, left_ref,
                 right_ref, rows_ref, strip_ref):
    tiles = turns_ref.shape[0] - 1
    here = turns_ref[tiles]
    k_top = turns_ref[here]
    k_bottom = lax.rem(4 - turns_ref[lax.rem(here + 1, tiles)], 4)
    strip_ref[...] = jnp.zeros_like(strip_ref)
    for s, (x_ref, k, start) in enumerate(((above_ref, k_top, 1), (below_ref, k_bottom, 4))):
        turned = turn(x_ref[:HALO], x_ref[HALO:], k)
        for f in range(2):
            for c in range(4):
                cut = slice(c * LANES, (c + 1) * LANES)
                rows_ref[s, f, c, :HALO] = turned[f][:, cut]
                for p in range(POOL):
                    spot = ((f * 2 + s) * POOL + p) * 8 + start
                    strip_ref[spot : spot + 3, cut] = rows_ref[s, f, c, pl.ds(p, 3, stride=POOL), :]
    high, low = two_parts(strip_ref[...])
    main_ref[...] = main_in[...]
    edge_ref[...] = edge_in[...]
    sums = [None] * 4
    for t in range(5):
        w = w_ref[:, 2 * t * LANES : 2 * (t + 1) * LANES]
        z = dot(high, w) + dot(low, w)
        for half in range(2):
            part = z[:, half * LANES : (half + 1) * LANES]
            stage = 2 * t + half
            for g in range(4):
                own = [part[(g * POOL + p) * 8 : (g * POOL + p + 1) * 8] for p in range(POOL)]
                if stage == 0:
                    sums[g] = own
                elif stage < 9:
                    sums[g] = [a + b for a, b in zip(three_rows(sums[g]), own)]
                else:
                    last = own
                    for _ in range(PASSES):
                        last = [a + b for a, b in zip(three_rows([pltpu.roll(x, LANES - 4, 1) for x in last]), own)]
                    f, s = g // 2, g % 2
                    spot, cut = ((7, 3), (PAD + CELLS - 2, 2))[s]
                    for to_ref, x in ((main_ref, sums[g]), (edge_ref, last)):
                        pooled = ((x[0] + x[1]) + (x[2] + x[3])) * SCALE
                        to_ref[f, spot : spot + 3] = to_ref[f, spot : spot + 3] + pooled[cut : cut + 3]
    out = jnp.zeros((16, FULL), F32)
    for f in range(2):
        parts = jnp.concatenate(three_parts(main_ref[f]) + three_parts(edge_ref[f]), axis=1)
        out = out + dot(sel_ref[f], parts, (((1,), (1,)), ((), ())))
    left_ref[...] = out[:8]
    right_ref[...] = out[8:]


def base_kernel(mask_ref, owner_ref, main_ref, edge_ref, from_left_ref, from_right_ref, place_ref, out_ref, field_ref,
                base_ref, term_ref, gram_ref):
    lane = lax.broadcasted_iota(jnp.int32, (1, LANES), 1)
    received = jnp.concatenate([from_left_ref[...], from_right_ref[...]], axis=0)
    placed = dot(jnp.concatenate(three_parts(received), axis=0), place_ref[...], (((0,), (0,)), ((), ())))
    inner = slice(PAD, PAD + CELLS)
    slopes = []
    for f in range(2):
        full = main_ref[f] + placed[:, 2 * f * LANES : (2 * f + 1) * LANES]
        field_ref[f] = full
        edge = edge_ref[f, inner]
        rim = placed[inner, (2 * f + 1) * LANES : (2 * f + 2) * LANES]
        rim = rim + jnp.where(lane == 0, edge, pltpu.roll(edge, LANES - 4, 1))
        centre = full[inner]
        left = jnp.where(lane == 0, rim, pltpu.roll(centre, 1, 1))
        right = jnp.where(lane == LANES - 1, rim, pltpu.roll(centre, LANES - 1, 1))
        dx = (right - left) * 0.5
        dy = (field_ref[f, PAD + 1 : PAD + 1 + CELLS] - field_ref[f, PAD - 1 : PAD - 1 + CELLS]) * 0.5
        slopes.append((centre, dx, dy))
    (u, u_dx, u_dy), (v, v_dx, v_dy) = slopes
    grid = CELLS // SIDE
    rows = []
    for a in range(grid):
        row = jnp.zeros((1, LANES), F32)
        for e in range(grid):
            row = jnp.where(lane // SIDE == e, (mask_ref[a, e] == 1).astype(F32), row)
        rows.append(jnp.broadcast_to(row, (SIDE, LANES)))
    live = jnp.concatenate(rows, axis=0) > 0.5
    for n, x in enumerate((u, v, v_dx - u_dy, u_dy + v_dx, u_dx - v_dy)):
        base_ref[n] = jnp.where(live, x, 0.0)
    for n, x in enumerate(terms_of([base_ref[n] for n in range(BASES)])):
        term_ref[n] = x
    for n in range(TERMS):
        first = term_ref[n]
        for m in range(n, TERMS):
            product = (first * term_ref[m]).reshape(CELLS // 8, 8, LANES)
            total = jnp.sum(jnp.sum(product, axis=0), axis=0, keepdims=True)
            gram_ref[n * TERMS + m : n * TERMS + m + 1] = total
            if m > n:
                gram_ref[m * TERMS + n : m * TERMS + n + 1] = total
    sums = jnp.concatenate(three_parts(gram_ref[...]), axis=1)
    gram = dot(jnp.ones((8, 3 * LANES), BF16), sums, (((1,), (1,)), ((), ())))
    owners = out_ref.shape[0]
    out_ref[...] = jnp.zeros_like(out_ref)
    for o in range(owners):
        for half in range(2):
            out_ref[o, 40 + half : 41 + half] = gram[:1, half * LANES : (half + 1) * LANES]
    for a in range(grid):
        for e in range(grid):

            @pl.when(mask_ref[a, e] == 1)
            def _():
                owner = owner_ref[a, e]
                for n in range(BASES):
                    block = None
                    for q in range(LANES // SIDE):
                        x = base_ref[n, pl.ds(a * SIDE + q, 8, stride=4), :]
                        x = pltpu.roll(x, (q - e) % 4 * SIDE, 1) if q != e else x
                        block = x if block is None else jnp.where(lane // SIDE == q, x, block)
                    out_ref[owner, 8 * n : 8 * n + 8] = block


def terms_of(base):
    u, v, vort, strain, stretch = base
    return [u, v, vort, strain, stretch, vort * vort, vort * strain, vort * stretch, strain * strain, stretch * stretch,
            strain * stretch, u * vort, v * vort, u * strain, v * stretch, u * v]


def library_kernel(x_ref, out_ref, gram_ref):
    slots = x_ref.shape[0] // BLOCK_ROWS
    k = pl.program_id(0)
    base = [x_ref[pl.ds(8 * n + k, slots, stride=BLOCK_ROWS), :] for n in range(BASES)]
    for n, x in enumerate(terms_of(base)):
        out_ref[pl.ds(n, slots, stride=TERMS), :] = x

    @pl.when(k == 0)
    def _():
        for half in range(2):
            rows = x_ref[pl.ds(40 + half, slots, stride=BLOCK_ROWS), :]
            total = jnp.sum(rows, axis=0, keepdims=True)
            for c in range(gram_ref.shape[0]):
                gram_ref[c, half : half + 1] = total


VMEM = pl.BlockSpec(memory_space=pltpu.VMEM)
SMEM = pl.BlockSpec(memory_space=pltpu.SMEM)
PARAMS = pltpu.CompilerParams(vmem_limit_bytes=48 << 20)


def struct(*shape):
    return jax.ShapeDtypeStruct(shape, F32)


def per_device(u_velocity, v_velocity, ocean_mask, tile_owner, lower_edge_quarter_turns):
    tiles, columns = lax.axis_size("tile"), lax.axis_size("col")
    onward = lambda count: [(i, (i + 1) % count) for i in range(count)]
    back = lambda count: [((i + 1) % count, i) for i in range(count)]
    weights = jnp.asarray(column_weights())
    here = lax.axis_index("tile").astype(jnp.int32)
    turns = jnp.concatenate([lower_edge_quarter_turns, here[None]])

    above = lax.ppermute(jnp.concatenate([u_velocity[-HALO:], v_velocity[-HALO:]]), "tile", onward(tiles))
    below = lax.ppermute(jnp.concatenate([u_velocity[:HALO], v_velocity[:HALO]]), "tile", back(tiles))
    main, edge = pl.pallas_call(
        own_kernel,
        out_shape=[struct(2, FULL, LANES)] * 2,
        grid=(1,),
        in_specs=[pl.BlockSpec((POOL * CELLS, LANES), lambda i, c=c: (0, c)) for c in range(4)] * 2 + [VMEM],
        out_specs=[VMEM] * 2,
        scratch_shapes=[pltpu.VMEM((2 * POOL * CELLS, POOL * CELLS), BF16)] * 2
        + [pltpu.VMEM((2, POOL, PAD + CELLS, LANES), F32)] * 3,
        compiler_params=PARAMS,
        name="own_rows",
    )(*[u_velocity] * 4, *[v_velocity] * 4, weights)
    main, edge, to_left, to_right = pl.pallas_call(
        strip_kernel,
        out_shape=[struct(2, FULL, LANES)] * 2 + [struct(8, FULL)] * 2,
        in_specs=[SMEM] + [VMEM] * 6,
        out_specs=[VMEM] * 4,
        scratch_shapes=[pltpu.VMEM((2, 2, 4, 16, LANES), F32), pltpu.VMEM((128, POOL * CELLS), F32)],
        compiler_params=PARAMS,
        name="row_strips",
    )(turns, above, below, weights, jnp.asarray(send_selectors()), main, edge)
    from_right = lax.ppermute(to_left, "col", back(columns))
    from_left = lax.ppermute(to_right, "col", onward(columns))
    blocks = pl.pallas_call(
        base_kernel,
        out_shape=struct(tiles, BLOCK_ROWS, LANES),
        in_specs=[SMEM] * 2 + [VMEM] * 5,
        out_specs=VMEM,
        scratch_shapes=[pltpu.VMEM((2, FULL, LANES), F32), pltpu.VMEM((BASES, CELLS, LANES), F32),
                        pltpu.VMEM((TERMS, CELLS, LANES), F32), pltpu.VMEM((TERMS * TERMS, LANES), F32)],
        compiler_params=PARAMS,
        name="base_fields",
    )(ocean_mask, tile_owner, main, edge, from_left, from_right, jnp.asarray(place_matrix()))
    blocks = lax.all_to_all(blocks, "tile", split_axis=0, concat_axis=0, tiled=True)
    library, gram = pl.pallas_call(
        library_kernel,
        out_shape=[struct(tiles * TERMS, SIDE * SIDE), struct(columns, 2, LANES)],
        grid=(8,),
        in_specs=[pl.BlockSpec((tiles * BLOCK_ROWS, LANES), lambda k: (0, 0))],
        out_specs=[pl.BlockSpec((tiles * TERMS, LANES), lambda k: (0, k)),
                   pl.BlockSpec((columns, 2, LANES), lambda k: (0, 0, 0))],
        compiler_params=PARAMS,
        name="library_terms",
    )(blocks.reshape(tiles * BLOCK_ROWS, LANES))
    gram = lax.all_to_all(gram, "col", split_axis=0, concat_axis=0, tiled=True)
    gram = jnp.sum(gram, axis=0).reshape(TERMS, TERMS) / (CELLS * CELLS)
    return library.reshape(1, 1, tiles, TERMS, SIDE * SIDE), gram


def solution(mesh):
    in_specs = (P("tile", "col"), P("tile", "col"), P("tile", "col"), P("tile", "col"), P())
    out_specs = (P("tile", "col", None, None, None), P())
    return jax.shard_map(
        per_device, mesh=mesh, in_specs=in_specs, out_specs=out_specs, check_vma=False
    )
```

```python
import math

import jax
import jax.numpy as jnp
import ml_dtypes
import numpy as np
from jax import lax
from jax.experimental import pallas as pl
from jax.experimental.pallas import tpu as pltpu
from jax.sharding import PartitionSpec as P

PASSES = 8
KAPPA = 0.2
POOL = 4
CELLS = 128
HALO = 12
SIDE = 32
TERMS = 16
PAD = 8
FULL = CELLS + 2 * PAD
LANES = 128
BASES = 5
BLOCK_ROWS = 48
F32 = jnp.float32
BF16 = jnp.bfloat16

HALF = CELLS // 2
EDGE_COLS = (HALF, HALF + 1, -2, -1)
EDGE_LANE = {CELLS: 0, CELLS + 1: 1, -2: HALF + 2, -1: HALF + 3}
SCALE = KAPPA**PASSES / (POOL * POOL)


def across(power, fine, coarse):
    total = 0
    for inner in range(POOL):
        offset = fine - (POOL * coarse + inner)
        if abs(offset) <= power and (power + offset) % 2 == 0:
            total += math.comb(power, (power + offset) // 2)
    return total


def column_weights():
    fine = HALF * POOL
    weights = np.zeros((fine, 5 * LANES), np.float32)

    def fill(column, j, coarse):
        for f in range(max(0, POOL * coarse - PASSES), min(fine, POOL * coarse + POOL + PASSES)):
            weights[f, column] = math.comb(PASSES, j) * across(PASSES - j, f, coarse)

    for j in range(PASSES + 1):
        for coarse in range(HALF):
            fill((PASSES - j) * HALF + coarse, j, coarse)
        for place, coarse in enumerate(EDGE_COLS):
            fill(9 * HALF + 4 * j + place, j, coarse)
    out = weights.astype(ml_dtypes.bfloat16)
    assert (out.astype(np.float32) == weights).all()
    return out


def send_selectors():
    sel = np.zeros((2, 16, 6 * LANES), np.float32)
    spots = ((0, 1, EDGE_LANE[-2]), (1, 1, EDGE_LANE[-1]), (2, 0, 0),
             (8, 0, CELLS - 1), (9, 1, EDGE_LANE[CELLS]), (10, 1, EDGE_LANE[CELLS + 1]))
    for f in range(2):
        for row, source, lane in spots:
            for piece in range(3):
                sel[f, row + 3 * f, (source * 3 + piece) * LANES + lane] = 1.0
    return sel.astype(ml_dtypes.bfloat16)


def place_matrix():
    place = np.zeros((3, 16, 4 * LANES), np.float32)
    for f in range(2):
        add, rim = 2 * f * LANES, (2 * f + 1) * LANES
        place[:, 3 * f + 0, rim + 0] = 1.0
        place[:, 3 * f + 1, add + 0] = 1.0
        place[:, 3 * f + 2, add + 1] = 1.0
        place[:, 8 + 3 * f + 0, add + CELLS - 2] = 1.0
        place[:, 8 + 3 * f + 1, add + CELLS - 1] = 1.0
        place[:, 8 + 3 * f + 2, rim + CELLS - 1] = 1.0
    return place.reshape(48, 4 * LANES).astype(ml_dtypes.bfloat16)


def head(x):
    scaled = x * 65537.0
    return scaled - (scaled - x)


def two_parts(x):
    high = head(x)
    return high.astype(BF16), (x - high).astype(BF16)


def three_parts(x):
    high = head(x)
    rest = x - high
    mid = head(rest)
    return high.astype(BF16), mid.astype(BF16), (rest - mid).astype(BF16)


def dot(a, b, dims=(((1,), (0,)), ((), ()))):
    return lax.dot_general(a, b, dims, preferred_element_type=F32)


def three_rows(t):
    rows = t[0].shape[0]
    up = pltpu.roll(t[3], 1, 0)
    down = pltpu.roll(t[0], rows - 1, 0)
    left, middle, right = t[0] + t[1], t[1] + t[2], t[2] + t[3]
    return [left + up, t[0] + middle, middle + t[3], right + down]


def halves(z, rows, tile):
    cut = slice(tile * LANES, (tile + 1) * LANES)
    low_lanes = lax.broadcasted_iota(jnp.int32, (1, LANES), 1) < HALF
    first, second = z[:rows, cut], z[rows:, cut]
    turned = pltpu.roll(second, HALF, 1)
    return jnp.where(low_lanes, first, turned), (first, second, turned, low_lanes)


def other_half(parts):
    first, second, _, low_lanes = parts
    return jnp.where(low_lanes, pltpu.roll(first, HALF, 1), second)


def edge_half(parts):
    first, _, turned, low_lanes = parts
    return jnp.where(low_lanes, turned, first)


def join(main, edge):
    lane = lax.broadcasted_iota(jnp.int32, (1, LANES), 1)
    main = main + jnp.where((lane == HALF) | (lane == HALF + 1), edge, 0.0)
    return main + jnp.where((lane == HALF - 1) | (lane == HALF - 2), pltpu.roll(edge, HALF - 4, 1), 0.0)


def own_kernel(u_hbm, v_hbm, w_hbm, main_ref, edge_ref, x_ref, w_ref, parts_ref, sum_ref, first_ref, last_ref, x_sem,
               w_sem):
    fine = HALF * POOL
    x_copies = [[pltpu.make_async_copy(hbm.at[:, pl.ds(c * LANES, LANES)], x_ref.at[f, c], x_sem.at[f, c])
                 for c in range(4)] for f, hbm in enumerate((u_hbm, v_hbm))]
    w_copies = [pltpu.make_async_copy(w_hbm, w_ref.at[pl.ds(part * fine, fine)], w_sem.at[part]) for part in range(2)]
    for copy in (*x_copies[0], *x_copies[1], *w_copies):
        copy.start()
    rows = 2 * POOL * CELLS
    for f in range(2):
        for c in range(4):
            x_copies[f][c].wait()
            for p in range(POOL):
                high, low = two_parts(x_ref[f, c, pl.ds(p, CELLS, stride=POOL), :])
                spot = pl.ds(c // 2 * rows + (f * POOL + p) * CELLS, CELLS)
                lane = c % 2 * LANES
                parts_ref[spot, lane : lane + LANES] = high
                parts_ref[spot, fine + lane : fine + lane + LANES] = low
    for copy in w_copies:
        copy.wait()
    for f in range(2):
        for p in range(POOL):
            sum_ref[f, p, :PAD] = jnp.zeros((PAD, LANES), F32)
            first_ref[f, p, :PAD] = jnp.zeros((PAD, LANES), F32)

    def step(part):
        for f in range(2):
            new = three_rows([sum_ref[f, p] for p in range(POOL)])
            for p in range(POOL):
                block = (f * POOL + p) * CELLS
                sum_ref[f, p, :PAD] = new[p][:PAD]
                sum_ref[f, p, PAD:] = new[p][PAD:] + part[block : block + CELLS]

    def store(to_ref, part):
        for f in range(2):
            for p in range(POOL):
                block = (f * POOL + p) * CELLS
                to_ref[f, p, PAD:] = part[block : block + CELLS]

    for start in (0, 2, 4):
        wide = min(2, 5 - start)
        z = dot(parts_ref[...], w_ref[:, start * LANES : (start + wide) * LANES])
        for tile in range(wide):
            part, both = halves(z, rows, tile)
            if start + tile == 0:
                store(sum_ref, part)
            else:
                step(part)
            if start + tile < 4:
                step(other_half(both))
            else:
                store(first_ref, edge_half(both))
    for f in range(2):
        for p in range(POOL):
            last_ref[f, p] = first_ref[f, p]

    @pl.loop(0, PASSES)
    def _(count):
        for f in range(2):
            new = three_rows([pltpu.roll(last_ref[f, p], LANES - 4, 1) for p in range(POOL)])
            for p in range(POOL):
                last_ref[f, p] = new[p] + first_ref[f, p]

    for f in range(2):
        main, edge = [((x[f, 0] + x[f, 1]) + (x[f, 2] + x[f, 3])) * SCALE for x in (sum_ref, last_ref)]
        for to_ref, pooled in ((main_ref, join(main, edge)), (edge_ref, edge)):
            to_ref[f, : PAD + CELLS] = pooled
            to_ref[f, PAD + CELLS :] = pooled[:PAD]


def turn(first, second, k):
    cosine = jnp.where(k == 0, 1.0, jnp.where(k == 2, -1.0, 0.0)).astype(F32)
    sine = jnp.where(k == 1, 1.0, jnp.where(k == 3, -1.0, 0.0)).astype(F32)
    return cosine * first - sine * second, sine * first + cosine * second


def strip_kernel(here_ref, turns_ref, above_ref, below_ref, w_ref, sel_ref, main_in, edge_in, main_ref, edge_ref, left_ref,
                 right_ref, rows_ref, strip_ref):
    tiles = turns_ref.shape[0]
    here = here_ref[0]
    k_top = turns_ref[here]
    k_bottom = lax.rem(4 - turns_ref[lax.rem(here + 1, tiles)], 4)
    strip_ref[...] = jnp.zeros_like(strip_ref)
    for s, (x_ref, k, start) in enumerate(((above_ref, k_top, 1), (below_ref, k_bottom, 4))):
        turned = turn(x_ref[:HALO], x_ref[HALO:], k)
        for f in range(2):
            for c in range(4):
                rows_ref[s, f, c, :HALO] = turned[f][:, c * LANES : (c + 1) * LANES]
                cut = slice(c % 2 * LANES, (c % 2 + 1) * LANES)
                for p in range(POOL):
                    spot = c // 2 * 128 + ((f * 2 + s) * POOL + p) * 8 + start
                    strip_ref[spot : spot + 3, cut] = rows_ref[s, f, c, pl.ds(p, 3, stride=POOL), :]
    parts = jnp.concatenate(two_parts(strip_ref[...]), axis=1)
    main_ref[...] = main_in[...]
    edge_ref[...] = edge_in[...]
    w = jnp.concatenate([w_ref[...]] * 2, axis=0)
    z = dot(parts, w)
    own = []
    for tile in range(5):
        part, both = halves(z, 128, tile)
        own += [part, other_half(both) if tile < 4 else edge_half(both)]
    for g in range(4):
        f, s = g // 2, g % 2
        cut = [[x[(g * POOL + p) * 8 : (g * POOL + p + 1) * 8] for p in range(POOL)] for x in own]
        total, last = cut[0], cut[9]
        for stage in range(1, 9):
            total = [a + b for a, b in zip(three_rows(total), cut[stage])]
            last = [a + b for a, b in zip(three_rows([pltpu.roll(x, LANES - 4, 1) for x in last]), cut[9])]
        main, edge = [((x[0] + x[1]) + (x[2] + x[3])) * SCALE for x in (total, last)]
        spot, start = ((7, 3), (PAD + CELLS - 2, 2))[s]
        for to_ref, x in ((main_ref, join(main, edge)), (edge_ref, edge)):
            to_ref[f, spot : spot + 3] = to_ref[f, spot : spot + 3] + x[start : start + 3]
    out = jnp.zeros((16, FULL), F32)
    for f in range(2):
        parts = jnp.concatenate(three_parts(main_ref[f]) + three_parts(edge_ref[f]), axis=1)
        out = out + dot(sel_ref[f], parts, (((1,), (1,)), ((), ())))
    left_ref[...] = out[:8]
    right_ref[...] = out[8:]


def base_kernel(mask_ref, owner_ref, main_ref, edge_ref, from_left_ref, from_right_ref, place_ref, out_ref, field_ref,
                base_ref, term_ref, gram_ref):
    lane = lax.broadcasted_iota(jnp.int32, (1, LANES), 1)
    received = jnp.concatenate([from_left_ref[...], from_right_ref[...]], axis=0)
    placed = dot(jnp.concatenate(three_parts(received), axis=0), place_ref[...], (((0,), (0,)), ((), ())))
    inner = slice(PAD, PAD + CELLS)
    slopes = []
    for f in range(2):
        full = main_ref[f] + placed[:, 2 * f * LANES : (2 * f + 1) * LANES]
        field_ref[f] = full
        edge = edge_ref[f, inner]
        rim = placed[inner, (2 * f + 1) * LANES : (2 * f + 2) * LANES]
        to_first, to_last = LANES - EDGE_LANE[-1], LANES - 1 - EDGE_LANE[CELLS]
        rim = rim + jnp.where(lane == 0, pltpu.roll(edge, to_first, 1), pltpu.roll(edge, to_last, 1))
        centre = full[inner]
        left = jnp.where(lane == 0, rim, pltpu.roll(centre, 1, 1))
        right = jnp.where(lane == LANES - 1, rim, pltpu.roll(centre, LANES - 1, 1))
        dx = (right - left) * 0.5
        dy = (field_ref[f, PAD + 1 : PAD + 1 + CELLS] - field_ref[f, PAD - 1 : PAD - 1 + CELLS]) * 0.5
        slopes.append((centre, dx, dy))
    (u, u_dx, u_dy), (v, v_dx, v_dy) = slopes
    grid = CELLS // SIDE
    rows = []
    for a in range(grid):
        row = jnp.zeros((1, LANES), F32)
        for e in range(grid):
            row = jnp.where(lane // SIDE == e, (mask_ref[a, e] == 1).astype(F32), row)
        rows.append(jnp.broadcast_to(row, (SIDE, LANES)))
    live = jnp.concatenate(rows, axis=0) > 0.5
    for n, x in enumerate((u, v, v_dx - u_dy, u_dy + v_dx, u_dx - v_dy)):
        base_ref[n] = jnp.where(live, x, 0.0)
    for n, x in enumerate(terms_of([base_ref[n] for n in range(BASES)])):
        term_ref[n] = x
    for n in range(TERMS):
        first = term_ref[n]
        for m in range(n, TERMS):
            product = (first * term_ref[m]).reshape(CELLS // 8, 8, LANES)
            total = jnp.sum(jnp.sum(product, axis=0), axis=0, keepdims=True)
            gram_ref[n * TERMS + m : n * TERMS + m + 1] = total
            if m > n:
                gram_ref[m * TERMS + n : m * TERMS + n + 1] = total
    sums = jnp.concatenate(three_parts(gram_ref[...]), axis=1)
    gram = dot(jnp.ones((8, 3 * LANES), BF16), sums, (((1,), (1,)), ((), ())))
    owners = out_ref.shape[0]
    out_ref[...] = jnp.zeros_like(out_ref)
    for o in range(owners):
        for half in range(2):
            out_ref[o, 40 + half : 41 + half] = gram[:1, half * LANES : (half + 1) * LANES]
    for a in range(grid):
        for e in range(grid):

            @pl.when(mask_ref[a, e] == 1)
            def _():
                owner = owner_ref[a, e]
                for n in range(BASES):
                    block = None
                    for q in range(LANES // SIDE):
                        x = base_ref[n, pl.ds(a * SIDE + q, 8, stride=4), :]
                        x = pltpu.roll(x, (q - e) % 4 * SIDE, 1) if q != e else x
                        block = x if block is None else jnp.where(lane // SIDE == q, x, block)
                    out_ref[owner, 8 * n : 8 * n + 8] = block


def terms_of(base):
    u, v, vort, strain, stretch = base
    return [u, v, vort, strain, stretch, vort * vort, vort * strain, vort * stretch, strain * strain, stretch * stretch,
            strain * stretch, u * vort, v * vort, u * strain, v * stretch, u * v]


def library_kernel(x_ref, out_hbm, gram_ref, out_ref, sem):
    slots = x_ref.shape[0] // BLOCK_ROWS
    copies = []
    for k in range(8):
        base = [x_ref[pl.ds(8 * n + k, slots, stride=BLOCK_ROWS), :] for n in range(BASES)]
        for n, x in enumerate(terms_of(base)):
            out_ref[k, pl.ds(n, slots, stride=TERMS), :] = x
        copies.append(pltpu.make_async_copy(out_ref.at[k], out_hbm.at[:, pl.ds(k * LANES, LANES)], sem.at[k]))
        copies[k].start()
    totals = [jnp.sum(x_ref[pl.ds(40 + half, slots, stride=BLOCK_ROWS), :], axis=0, keepdims=True) for half in range(2)]
    for n in range(TERMS):
        row = totals[n // 8]
        row = pltpu.roll(row, LANES - n % 8 * TERMS, 1) if n % 8 else row
        for c in range(gram_ref.shape[0]):
            gram_ref[c, n : n + 1] = row
    for copy in copies:
        copy.wait()


VMEM = pl.BlockSpec(memory_space=pltpu.VMEM)
HBM = pl.BlockSpec(memory_space=pltpu.HBM)
SMEM = pl.BlockSpec(memory_space=pltpu.SMEM)
PARAMS = pltpu.CompilerParams(vmem_limit_bytes=48 << 20)


def struct(*shape):
    return jax.ShapeDtypeStruct(shape, F32)


def per_device(u_velocity, v_velocity, ocean_mask, tile_owner, lower_edge_quarter_turns):
    tiles, columns = lax.axis_size("tile"), lax.axis_size("col")
    onward = lambda count: [(i, (i + 1) % count) for i in range(count)]
    back = lambda count: [((i + 1) % count, i) for i in range(count)]
    weights = jnp.asarray(column_weights())
    here = lax.axis_index("tile").astype(jnp.int32)[None]

    above = lax.ppermute(jnp.concatenate([u_velocity[-HALO:], v_velocity[-HALO:]]), "tile", onward(tiles))
    below = lax.ppermute(jnp.concatenate([u_velocity[:HALO], v_velocity[:HALO]]), "tile", back(tiles))
    main, edge = pl.pallas_call(
        own_kernel,
        out_shape=[struct(2, FULL, LANES)] * 2,
        in_specs=[HBM] * 3,
        out_specs=[VMEM] * 2,
        scratch_shapes=[pltpu.VMEM((2, 4, POOL * CELLS, LANES), F32), pltpu.VMEM((POOL * CELLS, 5 * LANES), BF16),
                        pltpu.VMEM((4 * POOL * CELLS, POOL * CELLS), BF16)]
        + [pltpu.VMEM((2, POOL, PAD + CELLS, LANES), F32)] * 3
        + [pltpu.SemaphoreType.DMA((2, 4)), pltpu.SemaphoreType.DMA((2,))],
        compiler_params=PARAMS,
        name="own_rows",
    )(*[pltpu.with_memory_space_constraint(x, pltpu.HBM) for x in (u_velocity, v_velocity, weights)])
    main, edge, to_left, to_right = pl.pallas_call(
        strip_kernel,
        out_shape=[struct(2, FULL, LANES)] * 2 + [struct(8, FULL)] * 2,
        in_specs=[SMEM] * 2 + [VMEM] * 6,
        out_specs=[VMEM] * 4,
        scratch_shapes=[pltpu.VMEM((2, 2, 4, 16, LANES), F32), pltpu.VMEM((256, 2 * LANES), F32)],
        compiler_params=PARAMS,
        name="row_strips",
    )(here, lower_edge_quarter_turns, above, below, weights, jnp.asarray(send_selectors()), main, edge)
    from_right = lax.ppermute(to_left, "col", back(columns))
    from_left = lax.ppermute(to_right, "col", onward(columns))
    blocks = pl.pallas_call(
        base_kernel,
        out_shape=struct(tiles, BLOCK_ROWS, LANES),
        in_specs=[SMEM] * 2 + [VMEM] * 5,
        out_specs=VMEM,
        scratch_shapes=[pltpu.VMEM((2, FULL, LANES), F32), pltpu.VMEM((BASES, CELLS, LANES), F32),
                        pltpu.VMEM((TERMS, CELLS, LANES), F32), pltpu.VMEM((TERMS * TERMS, LANES), F32)],
        compiler_params=PARAMS,
        name="base_fields",
    )(ocean_mask, tile_owner, main, edge, from_left, from_right, jnp.asarray(place_matrix()))
    blocks = lax.all_to_all(blocks, "tile", split_axis=0, concat_axis=0, tiled=True)
    library, gram = pl.pallas_call(
        library_kernel,
        out_shape=[struct(tiles * TERMS, SIDE * SIDE), struct(columns, TERMS, LANES)],
        in_specs=[VMEM],
        out_specs=[HBM, VMEM],
        scratch_shapes=[pltpu.VMEM((8, tiles * TERMS, LANES), F32), pltpu.SemaphoreType.DMA((8,))],
        compiler_params=PARAMS,
        name="library_terms",
    )(blocks.reshape(tiles * BLOCK_ROWS, LANES))
    gram = lax.all_to_all(gram, "col", split_axis=0, concat_axis=0, tiled=True)
    gram = jnp.sum(gram, axis=0)[:, :TERMS] / (CELLS * CELLS)
    return library.reshape(1, 1, tiles, TERMS, SIDE * SIDE), gram


def solution(mesh):
    in_specs = (P("tile", "col"), P("tile", "col"), P("tile", "col"), P("tile", "col"), P())
    out_specs = (P("tile", "col", None, None, None), P())
    return jax.shard_map(
        per_device, mesh=mesh, in_specs=in_specs, out_specs=out_specs, check_vma=False
    )
```

```python
import math

import jax
import jax.numpy as jnp
import ml_dtypes
import numpy as np
from jax import lax
from jax.experimental import pallas as pl
from jax.experimental.pallas import tpu as pltpu
from jax.sharding import PartitionSpec as P

PASSES = 8
KAPPA = 0.2
POOL = 4
CELLS = 128
HALO = 12
SIDE = 32
TERMS = 16
PAD = 8
FULL = CELLS + 2 * PAD
LANES = 128
BASES = 5
BLOCK_ROWS = 48
F32 = jnp.float32
BF16 = jnp.bfloat16

SCALE = KAPPA**PASSES / (POOL * POOL)
RIM_COLS = (-2, -1, 0, CELLS - 1, CELLS, CELLS + 1)


def across(power, fine, coarse):
    total = 0
    for inner in range(POOL):
        offset = fine - (POOL * coarse + inner)
        if abs(offset) <= power and (power + offset) % 2 == 0:
            total += math.comb(power, (power + offset) // 2)
    return total


def column_weights():
    fine = CELLS * POOL
    main = np.zeros((fine, 9 * LANES), np.float32)
    rim = np.zeros((fine, LANES), np.float32)
    for j in range(PASSES + 1):
        for coarse in range(-2, CELLS + 2):
            for f in range(max(0, POOL * coarse - PASSES), min(fine, POOL * coarse + POOL + PASSES)):
                value = math.comb(PASSES, j) * across(PASSES - j, f, coarse)
                if 0 <= coarse < CELLS:
                    main[f, (PASSES - j) * LANES + coarse] = value
                if coarse in RIM_COLS:
                    rim[f, 6 * j + RIM_COLS.index(coarse)] = value
    assert not rim[64 : fine - 64].any()
    rim[LANES - 64 : LANES] = rim[fine - 64 :]
    rim[LANES : 2 * LANES] = rim[:LANES]
    weights = np.concatenate([main, rim], axis=1)
    out = weights.astype(ml_dtypes.bfloat16)
    assert (out.astype(np.float32) == weights).all()
    return out


def rim_selector():
    row = lax.broadcasted_iota(jnp.int32, (32, 1), 0)
    source = jnp.full((32, 1), -1, jnp.int32)
    for f in range(2):
        for c in range(3):
            source = jnp.where(row == 3 * f + c, 64 * f + c, source)
            source = jnp.where(row == 8 + 3 * f + c, 64 * f + 3 + c, source)
        source = jnp.where(row == 16 + 2 * f, 64 * f + 1, source)
        source = jnp.where(row == 17 + 2 * f, 64 * f + 4, source)
    lane = lax.broadcasted_iota(jnp.int32, (32, 3 * LANES), 1) % LANES
    return jnp.where(lane == source, 1.0, 0.0).astype(BF16)


def place_matrix():
    place = np.zeros((3, 32, 4 * LANES), np.float32)
    for f in range(2):
        add, rim = 2 * f * LANES, (2 * f + 1) * LANES
        place[:, 3 * f + 0, rim + 0] = 1.0
        place[:, 3 * f + 1, add + 0] = 1.0
        place[:, 3 * f + 2, add + 1] = 1.0
        place[:, 8 + 3 * f + 0, add + CELLS - 2] = 1.0
        place[:, 8 + 3 * f + 1, add + CELLS - 1] = 1.0
        place[:, 8 + 3 * f + 2, rim + CELLS - 1] = 1.0
        place[:, 16 + 2 * f, rim + 0] = 1.0
        place[:, 17 + 2 * f, rim + CELLS - 1] = 1.0
    return place.reshape(96, 4 * LANES).astype(ml_dtypes.bfloat16)


def head(x):
    scaled = x * 65537.0
    return scaled - (scaled - x)


def two_parts(x):
    high = head(x)
    return high.astype(BF16), (x - high).astype(BF16)


def three_parts(x):
    high = head(x)
    rest = x - high
    mid = head(rest)
    return high.astype(BF16), mid.astype(BF16), (rest - mid).astype(BF16)


def dot(a, b, dims=(((1,), (0,)), ((), ()))):
    return lax.dot_general(a, b, dims, preferred_element_type=F32)


def three_rows(t):
    rows = t[0].shape[0]
    up = pltpu.roll(t[3], 1, 0)
    down = pltpu.roll(t[0], rows - 1, 0)
    left, middle, right = t[0] + t[1], t[1] + t[2], t[2] + t[3]
    return [left + up, t[0] + middle, middle + t[3], right + down]


def turn(first, second, k):
    cosine = jnp.where(k == 0, 1.0, jnp.where(k == 2, -1.0, 0.0)).astype(F32)
    sine = jnp.where(k == 1, 1.0, jnp.where(k == 3, -1.0, 0.0)).astype(F32)
    return cosine * first - sine * second, sine * first + cosine * second


def send_kernel(here_ref, turns_hbm, u_hbm, v_hbm, up_ref, down_ref, x_ref, turns_ref, sem, turns_sem):
    rows = u_hbm.shape[0]
    copies = [pltpu.make_async_copy(hbm.at[pl.ds(start, 16)], x_ref.at[side, f], sem.at[side, f])
              for side, start in enumerate((0, rows - 16)) for f, hbm in enumerate((u_hbm, v_hbm))]
    table = pltpu.make_async_copy(turns_hbm, turns_ref, turns_sem)
    table.start()
    for copy in copies:
        copy.start()
    table.wait()
    tiles = turns_ref.shape[0]
    here = here_ref[0]
    k_up = lax.rem(4 - turns_ref[here], 4)
    k_down = turns_ref[lax.rem(here + 1, tiles)]
    for copy in copies:
        copy.wait()
    for side, (to_ref, k, start) in enumerate(((up_ref, k_up, 0), (down_ref, k_down, 16 - HALO))):
        for f, x in enumerate(turn(x_ref[side, 0], x_ref[side, 1], k)):
            to_ref[f * HALO : (f + 1) * HALO] = x[start : start + HALO]


def phase_rows(p, own, above_ref, below_ref, f, cut, strip_ref):
    strip_ref[...] = jnp.zeros_like(strip_ref)
    for m in range(3):
        strip_ref[5 + m : 6 + m] = above_ref[f * HALO + 4 * m + p : f * HALO + 4 * m + p + 1, cut]
        strip_ref[8 + m : 9 + m] = below_ref[f * HALO + 4 * m + p : f * HALO + 4 * m + p + 1, cut]
    return jnp.concatenate([strip_ref[:8], own, strip_ref[8:]], axis=0)


def rim_kernel(u_first, u_last, v_first, v_last, above_ref, below_ref, w_ref, left_ref, right_ref, own_ref,
               parts_ref, first_ref, last_ref, strip_ref):
    lane = lax.broadcasted_iota(jnp.int32, (1, LANES), 1)
    for f, (head_ref, tail_ref) in enumerate(((u_first, u_last), (v_first, v_last))):
        for p in range(POOL):
            spot = pl.ds(p, CELLS, stride=POOL)
            ends = [phase_rows(p, ref[spot, :], above_ref, below_ref, f, slice(c * LANES, (c + 1) * LANES), strip_ref)
                    for c, ref in ((0, head_ref), (3, tail_ref))]
            parts = jnp.concatenate(two_parts(jnp.where(lane < 64, *ends)), axis=1)
            parts_ref[(f * POOL + p) * FULL : (f * POOL + p + 1) * FULL] = parts
    z = dot(parts_ref[...], w_ref[...])
    for p in range(POOL):
        u, v = [z[(f * POOL + p) * FULL : (f * POOL + p + 1) * FULL] for f in range(2)]
        both = jnp.where(lane < 64, u, pltpu.roll(v, 64, 1))
        first_ref[p] = both
        last_ref[p] = both
    for _ in range(PASSES):
        new = three_rows([pltpu.roll(last_ref[p], LANES - 6, 1) for p in range(POOL)])
        for p in range(POOL):
            last_ref[p] = new[p] + first_ref[p]
    pooled = ((last_ref[0] + last_ref[1]) + (last_ref[2] + last_ref[3])) * SCALE
    out = dot(rim_selector(), jnp.concatenate(three_parts(pooled), axis=1), (((1,), (1,)), ((), ())))
    left_ref[...] = out[:8]
    right_ref[...] = out[8:16]
    own_ref[...] = out[16:]


def main_kernel(*refs):
    above_ref, below_ref, w_ref, _, main_ref, parts_ref, sum_ref, strip_ref = refs[8:]
    fine = POOL * CELLS
    for f in range(2):
        for c in range(4):
            cut = slice(c * LANES, (c + 1) * LANES)
            for p in range(POOL):
                own = refs[4 * f + c][pl.ds(p, CELLS, stride=POOL), :]
                high, low = two_parts(phase_rows(p, own, above_ref, below_ref, f, cut, strip_ref))
                spot = slice((f * POOL + p) * FULL, (f * POOL + p + 1) * FULL)
                parts_ref[spot, cut] = high
                parts_ref[spot, fine + c * LANES : fine + (c + 1) * LANES] = low
    for start in range(0, 9, 2):
        wide = min(2, 9 - start)
        w = w_ref[:, start * LANES : (start + wide) * LANES]
        z = dot(parts_ref[:, :fine], w) + dot(parts_ref[:, fine:], w)
        for stage in range(start, start + wide):
            part = z[:, (stage - start) * LANES : (stage - start + 1) * LANES]
            for f in range(2):
                own = [part[(f * POOL + p) * FULL : (f * POOL + p + 1) * FULL] for p in range(POOL)]
                if stage:
                    own = [a + b for a, b in zip(three_rows([sum_ref[f, p] for p in range(POOL)]), own)]
                for p in range(POOL):
                    sum_ref[f, p] = own[p]
    for f in range(2):
        main_ref[f] = ((sum_ref[f, 0] + sum_ref[f, 1]) + (sum_ref[f, 2] + sum_ref[f, 3])) * SCALE


def base_kernel(mask_ref, owner_ref, main_ref, own_ref, from_left_ref, from_right_ref, place_ref, out_ref, field_ref,
                base_ref, term_ref, gram_ref):
    lane = lax.broadcasted_iota(jnp.int32, (1, LANES), 1)
    received = jnp.concatenate([from_left_ref[...], from_right_ref[...], own_ref[...]], axis=0)
    placed = dot(jnp.concatenate(three_parts(received), axis=0), place_ref[...], (((0,), (0,)), ((), ())))
    inner = slice(PAD, PAD + CELLS)
    slopes = []
    for f in range(2):
        full = main_ref[f] + placed[:, 2 * f * LANES : (2 * f + 1) * LANES]
        field_ref[f] = full
        rim = placed[inner, (2 * f + 1) * LANES : (2 * f + 2) * LANES]
        centre = full[inner]
        left = jnp.where(lane == 0, rim, pltpu.roll(centre, 1, 1))
        right = jnp.where(lane == LANES - 1, rim, pltpu.roll(centre, LANES - 1, 1))
        dx = (right - left) * 0.5
        dy = (field_ref[f, PAD + 1 : PAD + 1 + CELLS] - field_ref[f, PAD - 1 : PAD - 1 + CELLS]) * 0.5
        slopes.append((centre, dx, dy))
    (u, u_dx, u_dy), (v, v_dx, v_dy) = slopes
    grid = CELLS // SIDE
    rows = []
    for a in range(grid):
        row = jnp.zeros((1, LANES), F32)
        for e in range(grid):
            row = jnp.where(lane // SIDE == e, (mask_ref[a, e] == 1).astype(F32), row)
        rows.append(jnp.broadcast_to(row, (SIDE, LANES)))
    live = jnp.concatenate(rows, axis=0) > 0.5
    for n, x in enumerate((u, v, v_dx - u_dy, u_dy + v_dx, u_dx - v_dy)):
        base_ref[n] = jnp.where(live, x, 0.0)
    for n, x in enumerate(terms_of([base_ref[n] for n in range(BASES)])):
        term_ref[n] = x
    for n in range(TERMS):
        first = term_ref[n]
        for m in range(n, TERMS):
            product = (first * term_ref[m]).reshape(CELLS // 8, 8, LANES)
            total = jnp.sum(jnp.sum(product, axis=0), axis=0, keepdims=True)
            gram_ref[n * TERMS + m : n * TERMS + m + 1] = total
            if m > n:
                gram_ref[m * TERMS + n : m * TERMS + n + 1] = total
    sums = jnp.concatenate(three_parts(gram_ref[...]), axis=1)
    gram = dot(jnp.ones((8, 3 * LANES), BF16), sums, (((1,), (1,)), ((), ())))
    owners = out_ref.shape[0]
    out_ref[...] = jnp.zeros_like(out_ref)
    for o in range(owners):
        for half in range(2):
            out_ref[o, 40 + half : 41 + half] = gram[:1, half * LANES : (half + 1) * LANES]
    for a in range(grid):
        for e in range(grid):

            @pl.when(mask_ref[a, e] == 1)
            def _():
                owner = owner_ref[a, e]
                for n in range(BASES):
                    block = None
                    for q in range(LANES // SIDE):
                        x = base_ref[n, pl.ds(a * SIDE + q, 8, stride=4), :]
                        x = pltpu.roll(x, (q - e) % 4 * SIDE, 1) if q != e else x
                        block = x if block is None else jnp.where(lane // SIDE == q, x, block)
                    out_ref[owner, 8 * n : 8 * n + 8] = block


def terms_of(base):
    u, v, vort, strain, stretch = base
    return [u, v, vort, strain, stretch, vort * vort, vort * strain, vort * stretch, strain * strain, stretch * stretch,
            strain * stretch, u * vort, v * vort, u * strain, v * stretch, u * v]


def library_kernel(x_ref, out_hbm, gram_ref, out_ref, sem):
    slots = x_ref.shape[0] // BLOCK_ROWS
    copies = []
    for k in range(8):
        base = [x_ref[pl.ds(8 * n + k, slots, stride=BLOCK_ROWS), :] for n in range(BASES)]
        for n, x in enumerate(terms_of(base)):
            out_ref[k, pl.ds(n, slots, stride=TERMS), :] = x
        copies.append(pltpu.make_async_copy(out_ref.at[k], out_hbm.at[:, pl.ds(k * LANES, LANES)], sem.at[k]))
        copies[k].start()
    totals = [jnp.sum(x_ref[pl.ds(40 + half, slots, stride=BLOCK_ROWS), :], axis=0, keepdims=True) for half in range(2)]
    for n in range(TERMS):
        row = totals[n // 8]
        row = pltpu.roll(row, LANES - n % 8 * TERMS, 1) if n % 8 else row
        for c in range(gram_ref.shape[0]):
            gram_ref[c, n : n + 1] = row
    for copy in copies:
        copy.wait()


VMEM = pl.BlockSpec(memory_space=pltpu.VMEM)
HBM = pl.BlockSpec(memory_space=pltpu.HBM)
SMEM = pl.BlockSpec(memory_space=pltpu.SMEM)
PARAMS = pltpu.CompilerParams(vmem_limit_bytes=48 << 20)


def struct(*shape):
    return jax.ShapeDtypeStruct(shape, F32)


def per_device(u_velocity, v_velocity, ocean_mask, tile_owner, lower_edge_quarter_turns):
    tiles, columns = lax.axis_size("tile"), lax.axis_size("col")
    onward = lambda count: [(i, (i + 1) % count) for i in range(count)]
    back = lambda count: [((i + 1) % count, i) for i in range(count)]
    here = lax.axis_index("tile").astype(jnp.int32)[None]
    in_hbm = lambda x: pltpu.with_memory_space_constraint(x, pltpu.HBM)
    up, down = pl.pallas_call(
        send_kernel,
        out_shape=[struct(2 * HALO, POOL * CELLS)] * 2,
        in_specs=[SMEM] + [HBM] * 3,
        out_specs=[VMEM] * 2,
        scratch_shapes=[pltpu.VMEM((2, 2, 16, POOL * CELLS), F32), pltpu.SMEM((tiles,), jnp.int32),
                        pltpu.SemaphoreType.DMA((2, 2)), pltpu.SemaphoreType.DMA],
        compiler_params=PARAMS,
        name="send_rows",
    )(here, *[in_hbm(x) for x in (lower_edge_quarter_turns, u_velocity, v_velocity)])
    up, down, u_velocity, v_velocity = lax.optimization_barrier((up, down, u_velocity, v_velocity))
    above = lax.ppermute(down, "tile", onward(tiles))
    below = lax.ppermute(up, "tile", back(tiles))
    weights = jnp.asarray(column_weights())
    column = lambda c: pl.BlockSpec((POOL * CELLS, LANES), lambda i: (0, c))
    whole = lambda *shape: pl.BlockSpec(shape, lambda i: (0,) * len(shape))
    halo = whole(2 * HALO, POOL * CELLS)
    to_left, to_right, own = pl.pallas_call(
        rim_kernel,
        out_shape=[struct(8, FULL), struct(8, FULL), struct(16, FULL)],
        grid=(1,),
        in_specs=[column(0), column(3)] * 2 + [halo] * 2 + [pl.BlockSpec((2 * LANES, LANES), lambda i: (0, 9))],
        out_specs=[whole(8, FULL), whole(8, FULL), whole(16, FULL)],
        scratch_shapes=[pltpu.VMEM((2 * POOL * FULL, 2 * LANES), BF16), pltpu.VMEM((POOL, FULL, LANES), F32),
                        pltpu.VMEM((POOL, FULL, LANES), F32), pltpu.VMEM((16, LANES), F32)],
        compiler_params=PARAMS,
        name="rim_columns",
    )(u_velocity, u_velocity, v_velocity, v_velocity, above, below, weights)
    from_right = lax.ppermute(to_left, "col", back(columns))
    from_left = lax.ppermute(to_right, "col", onward(columns))
    main = pl.pallas_call(
        main_kernel,
        out_shape=struct(2, FULL, LANES),
        grid=(1,),
        in_specs=[column(c) for c in range(4)] * 2 + [halo] * 2 + [whole(POOL * CELLS, 10 * LANES), whole(16, FULL)],
        out_specs=whole(2, FULL, LANES),
        scratch_shapes=[pltpu.VMEM((2 * POOL * FULL, 2 * POOL * CELLS), BF16), pltpu.VMEM((2, POOL, FULL, LANES), F32),
                        pltpu.VMEM((16, LANES), F32)],
        compiler_params=PARAMS,
        name="main_columns",
    )(*[u_velocity] * 4, *[v_velocity] * 4, above, below, weights, own)
    blocks = pl.pallas_call(
        base_kernel,
        out_shape=struct(tiles, BLOCK_ROWS, LANES),
        in_specs=[SMEM] * 2 + [VMEM] * 5,
        out_specs=VMEM,
        scratch_shapes=[pltpu.VMEM((2, FULL, LANES), F32), pltpu.VMEM((BASES, CELLS, LANES), F32),
                        pltpu.VMEM((TERMS, CELLS, LANES), F32), pltpu.VMEM((TERMS * TERMS, LANES), F32)],
        compiler_params=PARAMS,
        name="base_fields",
    )(ocean_mask, tile_owner, main, own, from_left, from_right, jnp.asarray(place_matrix()))
    blocks = lax.all_to_all(blocks, "tile", split_axis=0, concat_axis=0, tiled=True)
    library, gram = pl.pallas_call(
        library_kernel,
        out_shape=[struct(tiles * TERMS, SIDE * SIDE), struct(columns, TERMS, LANES)],
        in_specs=[VMEM],
        out_specs=[HBM, VMEM],
        scratch_shapes=[pltpu.VMEM((8, tiles * TERMS, LANES), F32), pltpu.SemaphoreType.DMA((8,))],
        compiler_params=PARAMS,
        name="library_terms",
    )(blocks.reshape(tiles * BLOCK_ROWS, LANES))
    gram = lax.all_to_all(gram, "col", split_axis=0, concat_axis=0, tiled=True)
    gram = jnp.sum(gram, axis=0)[:, :TERMS] / (CELLS * CELLS)
    return library.reshape(1, 1, tiles, TERMS, SIDE * SIDE), gram


def solution(mesh):
    in_specs = (P("tile", "col"), P("tile", "col"), P("tile", "col"), P("tile", "col"), P())
    out_specs = (P("tile", "col", None, None, None), P())
    return jax.shard_map(
        per_device, mesh=mesh, in_specs=in_specs, out_specs=out_specs, check_vma=False
    )
```

```python
import math

import jax
import jax.numpy as jnp
import ml_dtypes
import numpy as np
from jax import lax
from jax.experimental import pallas as pl
from jax.experimental.pallas import tpu as pltpu
from jax.sharding import PartitionSpec as P

PASSES = 8
KAPPA = 0.2
POOL = 4
CELLS = 128
HALO = 12
SIDE = 32
TERMS = 16
PAD = 8
FULL = CELLS + 2 * PAD
LANES = 128
BASES = 5
BLOCK_ROWS = 48
F32 = jnp.float32
BF16 = jnp.bfloat16

SCALE = KAPPA**PASSES / (POOL * POOL)
RIM_COLS = (-2, -1, 0, CELLS - 1, CELLS, CELLS + 1)


def across(power, fine, coarse):
    total = 0
    for inner in range(POOL):
        offset = fine - (POOL * coarse + inner)
        if abs(offset) <= power and (power + offset) % 2 == 0:
            total += math.comb(power, (power + offset) // 2)
    return total


def column_weights():
    fine = CELLS * POOL
    main = np.zeros((fine, 9 * LANES), np.float32)
    rim = np.zeros((fine, LANES), np.float32)
    for j in range(PASSES + 1):
        for coarse in range(-2, CELLS + 2):
            for f in range(max(0, POOL * coarse - PASSES), min(fine, POOL * coarse + POOL + PASSES)):
                value = math.comb(PASSES, j) * across(PASSES - j, f, coarse)
                if 0 <= coarse < CELLS:
                    main[f, (PASSES - j) * LANES + coarse] = value
                if coarse in RIM_COLS:
                    rim[f, 6 * j + RIM_COLS.index(coarse)] = value
    assert not rim[64 : fine - 64].any()
    rim[LANES - 64 : LANES] = rim[fine - 64 :]
    rim[LANES : 2 * LANES] = rim[:LANES]
    weights = np.concatenate([main, rim], axis=1)
    out = weights.astype(ml_dtypes.bfloat16)
    assert (out.astype(np.float32) == weights).all()
    return out


def rim_selector():
    row = lax.broadcasted_iota(jnp.int32, (32, 1), 0)
    source = jnp.full((32, 1), -1, jnp.int32)
    for f in range(2):
        for c in range(3):
            source = jnp.where(row == 3 * f + c, 64 * f + c, source)
            source = jnp.where(row == 8 + 3 * f + c, 64 * f + 3 + c, source)
        source = jnp.where(row == 16 + 2 * f, 64 * f + 1, source)
        source = jnp.where(row == 17 + 2 * f, 64 * f + 4, source)
    lane = lax.broadcasted_iota(jnp.int32, (32, 3 * LANES), 1) % LANES
    return jnp.where(lane == source, 1.0, 0.0).astype(BF16)


def place_matrix():
    place = np.zeros((3, 32, 4 * LANES), np.float32)
    for f in range(2):
        add, rim = 2 * f * LANES, (2 * f + 1) * LANES
        place[:, 3 * f + 0, rim + 0] = 1.0
        place[:, 3 * f + 1, add + 0] = 1.0
        place[:, 3 * f + 2, add + 1] = 1.0
        place[:, 8 + 3 * f + 0, add + CELLS - 2] = 1.0
        place[:, 8 + 3 * f + 1, add + CELLS - 1] = 1.0
        place[:, 8 + 3 * f + 2, rim + CELLS - 1] = 1.0
        place[:, 16 + 2 * f, rim + 0] = 1.0
        place[:, 17 + 2 * f, rim + CELLS - 1] = 1.0
    return place.reshape(96, 4 * LANES).astype(ml_dtypes.bfloat16)


def head(x):
    scaled = x * 65537.0
    return scaled - (scaled - x)


def two_parts(x):
    high = head(x)
    return high.astype(BF16), (x - high).astype(BF16)


def three_parts(x):
    high = head(x)
    rest = x - high
    mid = head(rest)
    return high.astype(BF16), mid.astype(BF16), (rest - mid).astype(BF16)


def dot(a, b, dims=(((1,), (0,)), ((), ()))):
    return lax.dot_general(a, b, dims, preferred_element_type=F32)


def three_rows(t):
    rows = t[0].shape[0]
    up = pltpu.roll(t[3], 1, 0)
    down = pltpu.roll(t[0], rows - 1, 0)
    left, middle, right = t[0] + t[1], t[1] + t[2], t[2] + t[3]
    return [left + up, t[0] + middle, middle + t[3], right + down]


def turn(first, second, k):
    cosine = jnp.where(k == 0, 1.0, jnp.where(k == 2, -1.0, 0.0)).astype(F32)
    sine = jnp.where(k == 1, 1.0, jnp.where(k == 3, -1.0, 0.0)).astype(F32)
    return cosine * first - sine * second, sine * first + cosine * second


def send_kernel(here_ref, turns_hbm, u_hbm, v_hbm, up_ref, down_ref, x_ref, turns_ref, sem, turns_sem):
    rows = u_hbm.shape[0]
    copies = [pltpu.make_async_copy(hbm.at[pl.ds(start, 16)], x_ref.at[side, f], sem.at[side, f])
              for side, start in enumerate((0, rows - 16)) for f, hbm in enumerate((u_hbm, v_hbm))]
    table = pltpu.make_async_copy(turns_hbm, turns_ref, turns_sem)
    table.start()
    for copy in copies:
        copy.start()
    table.wait()
    tiles = turns_ref.shape[0]
    here = here_ref[0]
    k_up = lax.rem(4 - turns_ref[here], 4)
    k_down = turns_ref[lax.rem(here + 1, tiles)]
    for copy in copies:
        copy.wait()
    for side, (to_ref, k, start) in enumerate(((up_ref, k_up, 0), (down_ref, k_down, 16 - HALO))):
        for f, x in enumerate(turn(x_ref[side, 0], x_ref[side, 1], k)):
            to_ref[f * HALO : (f + 1) * HALO] = x[start : start + HALO]


EARLY = 4


def prepare_kernel(*refs):
    w_hbm, parts_ref, w_out, rim_ref, early_ref, rim_parts_ref, first_ref, last_ref, sem = refs[8:]
    copy = pltpu.make_async_copy(w_hbm, w_out, sem)
    copy.start()
    lane = lax.broadcasted_iota(jnp.int32, (1, LANES), 1)
    fine = POOL * CELLS
    for f in range(2):
        for p in range(POOL):
            spot = slice((f * POOL + p) * CELLS, (f * POOL + p + 1) * CELLS)
            pieces = [two_parts(refs[4 * f + c][pl.ds(p, CELLS, stride=POOL), :]) for c in range(4)]
            for part in range(2):
                for c in range(4):
                    parts_ref[spot, part * fine + c * LANES : part * fine + (c + 1) * LANES] = pieces[c][part]
                rim_parts_ref[spot, part * LANES : (part + 1) * LANES] = jnp.where(
                    lane < 64, pieces[0][part], pieces[3][part])
    copy.wait()
    z = dot(rim_parts_ref[...], w_out[: 2 * LANES, 9 * LANES :])
    for p in range(POOL):
        u, v = [z[(f * POOL + p) * CELLS : (f * POOL + p + 1) * CELLS] for f in range(2)]
        both = jnp.where(lane < 64, u, pltpu.roll(v, 64, 1))
        for to_ref in (first_ref, last_ref):
            to_ref[p, :PAD] = jnp.zeros((PAD, LANES), F32)
            to_ref[p, PAD:] = both
    for _ in range(PASSES):
        new = three_rows([pltpu.roll(last_ref[p], LANES - 6, 1) for p in range(POOL)])
        for p in range(POOL):
            last_ref[p] = new[p] + first_ref[p]
    pooled = ((last_ref[0] + last_ref[1]) + (last_ref[2] + last_ref[3])) * SCALE
    rim_ref[: PAD + CELLS] = pooled
    rim_ref[PAD + CELLS :] = pooled[:PAD]
    for start in range(0, EARLY, 2):
        cut = slice(start * LANES, (start + 2) * LANES)
        early_ref[:, cut] = dot(parts_ref[:, :fine], w_out[:, cut]) + dot(parts_ref[:, fine:], w_out[:, cut])


def rim_kernel(above_ref, below_ref, w_ref, rim_in, left_ref, right_ref, own_ref, rows_ref, strip_ref, rim_ref):
    lane = lax.broadcasted_iota(jnp.int32, (1, LANES), 1)
    strip_ref[...] = jnp.zeros_like(strip_ref)
    for s, (x_ref, start) in enumerate(((above_ref, 1), (below_ref, 4))):
        ends = jnp.where(lane < 64, x_ref[:, :LANES], x_ref[:, 3 * LANES :])
        rows_ref[s] = ends
        for f in range(2):
            for p in range(POOL):
                spot = ((f * 2 + s) * POOL + p) * 8 + start
                strip_ref[spot : spot + 3] = rows_ref[s, pl.ds(f * HALO + p, 3, stride=POOL), :]
    z = dot(jnp.concatenate(two_parts(strip_ref[...]), axis=1), w_ref[...])
    rim_ref[...] = rim_in[...]
    for s, (spot, start) in enumerate(((7, 3), (PAD + CELLS - 2, 2))):
        first = []
        for p in range(POOL):
            u, v = [z[((f * 2 + s) * POOL + p) * 8 : ((f * 2 + s) * POOL + p + 1) * 8] for f in range(2)]
            first.append(jnp.where(lane < 64, u, pltpu.roll(v, 64, 1)))
        last = first
        for _ in range(PASSES):
            last = [a + b for a, b in zip(three_rows([pltpu.roll(x, LANES - 6, 1) for x in last]), first)]
        pooled = ((last[0] + last[1]) + (last[2] + last[3])) * SCALE
        rim_ref[spot : spot + 3] = rim_ref[spot : spot + 3] + pooled[start : start + 3]
    turned = jnp.transpose(rim_ref[...])
    for to_ref, columns in ((left_ref, (0, 1, 2)), (right_ref, (3, 4, 5)), (own_ref, (1, 4))):
        to_ref[...] = jnp.zeros_like(to_ref)
        for f in range(2):
            for place, c in enumerate(columns):
                spot = len(columns) * f + place
                to_ref[spot : spot + 1] = turned[64 * f + c : 64 * f + c + 1]


def main_kernel(parts_ref, early_ref, w_ref, above_ref, below_ref, _, main_ref, rows_ref, strip_ref, sum_ref):
    strip_ref[...] = jnp.zeros_like(strip_ref)
    for s, (x_ref, start) in enumerate(((above_ref, 5), (below_ref, 8))):
        for c in range(4):
            cut = slice(c * LANES, (c + 1) * LANES)
            rows_ref[s, c] = x_ref[:, cut]
            for f in range(2):
                for p in range(POOL):
                    spot = (f * POOL + p) * 16 + start
                    strip_ref[spot : spot + 3, cut] = rows_ref[s, c, pl.ds(f * HALO + p, 3, stride=POOL), :]
    strips = jnp.concatenate(two_parts(strip_ref[...]), axis=1)
    fine = POOL * CELLS
    for start in range(0, 9, 2):
        wide = min(2, 9 - start)
        w = w_ref[:, start * LANES : (start + wide) * LANES]
        if start < EARLY:
            z = early_ref[:, start * LANES : (start + wide) * LANES]
        else:
            z = dot(parts_ref[:, :fine], w) + dot(parts_ref[:, fine:], w)
        z_strip = dot(strips[:, :fine], w) + dot(strips[:, fine:], w)
        for stage in range(start, start + wide):
            cut = slice((stage - start) * LANES, (stage - start + 1) * LANES)
            for f in range(2):
                own = []
                for p in range(POOL):
                    block = f * POOL + p
                    own.append(jnp.concatenate([
                        z_strip[block * 16 : block * 16 + 8, cut], z[block * CELLS : (block + 1) * CELLS, cut],
                        z_strip[block * 16 + 8 : block * 16 + 16, cut]], axis=0))
                if stage:
                    own = [a + b for a, b in zip(three_rows([sum_ref[f, p] for p in range(POOL)]), own)]
                for p in range(POOL):
                    sum_ref[f, p] = own[p]
    for f in range(2):
        main_ref[f] = ((sum_ref[f, 0] + sum_ref[f, 1]) + (sum_ref[f, 2] + sum_ref[f, 3])) * SCALE


def base_kernel(mask_ref, owner_ref, main_ref, own_ref, from_left_ref, from_right_ref, place_ref, out_ref, field_ref,
                base_ref, term_ref, gram_ref, pack_ref, tile_ref):
    lane = lax.broadcasted_iota(jnp.int32, (1, LANES), 1)
    received = jnp.concatenate([from_left_ref[...], from_right_ref[...], own_ref[...]], axis=0)
    placed = dot(jnp.concatenate(three_parts(received), axis=0), place_ref[...], (((0,), (0,)), ((), ())))
    inner = slice(PAD, PAD + CELLS)
    slopes = []
    for f in range(2):
        full = main_ref[f] + placed[:, 2 * f * LANES : (2 * f + 1) * LANES]
        field_ref[f] = full
        rim = placed[inner, (2 * f + 1) * LANES : (2 * f + 2) * LANES]
        centre = full[inner]
        left = jnp.where(lane == 0, rim, pltpu.roll(centre, 1, 1))
        right = jnp.where(lane == LANES - 1, rim, pltpu.roll(centre, LANES - 1, 1))
        dx = (right - left) * 0.5
        dy = (field_ref[f, PAD + 1 : PAD + 1 + CELLS] - field_ref[f, PAD - 1 : PAD - 1 + CELLS]) * 0.5
        slopes.append((centre, dx, dy))
    (u, u_dx, u_dy), (v, v_dx, v_dy) = slopes
    grid = CELLS // SIDE
    rows = []
    for a in range(grid):
        row = jnp.zeros((1, LANES), F32)
        for e in range(grid):
            row = jnp.where(lane // SIDE == e, (mask_ref[a, e] == 1).astype(F32), row)
        rows.append(jnp.broadcast_to(row, (SIDE, LANES)))
    live = jnp.concatenate(rows, axis=0) > 0.5
    for n, x in enumerate((u, v, v_dx - u_dy, u_dy + v_dx, u_dx - v_dy)):
        base_ref[n] = jnp.where(live, x, 0.0)
    for n, x in enumerate(terms_of([base_ref[n] for n in range(BASES)])):
        term_ref[n] = x
    for n in range(TERMS):
        first = term_ref[n]
        for m in range(n, TERMS):
            product = (first * term_ref[m]).reshape(CELLS // 8, 8, LANES)
            total = jnp.sum(jnp.sum(product, axis=0), axis=0, keepdims=True)
            gram_ref[n * TERMS + m : n * TERMS + m + 1] = total
            if m > n:
                gram_ref[m * TERMS + n : m * TERMS + n + 1] = total
    totals = jnp.sum(gram_ref[...], axis=1, keepdims=True)
    row = lax.broadcasted_iota(jnp.int32, (TERMS * TERMS, 1), 0)
    spread = jnp.where(row % LANES == lane, totals, 0.0)
    halves = [jnp.sum(spread[h * LANES : (h + 1) * LANES], axis=0, keepdims=True) for h in range(2)]
    owners = out_ref.shape[0]
    nothing = grid * grid
    for o in range(owners + 1):
        tile_ref[o] = nothing
    for a in range(grid):
        for e in range(grid):
            tile_ref[jnp.where(mask_ref[a, e] == 1, owner_ref[a, e], owners)] = a * grid + e
    pack_ref[nothing] = jnp.zeros((8 * BASES, LANES), F32)
    for a in range(grid):
        for n in range(BASES):
            pieces = [base_ref[n, pl.ds(a * SIDE + q, 8, stride=4), :] for q in range(grid)]
            for e in range(grid):
                block = None
                for q in range(grid):
                    x = pltpu.roll(pieces[q], (q - e) % grid * SIDE, 1) if q != e else pieces[q]
                    block = x if block is None else jnp.where(lane // SIDE == q, x, block)
                pack_ref[a * grid + e, 8 * n : 8 * n + 8] = block
    for o in range(owners):
        out_ref[o, : 8 * BASES] = pack_ref[tile_ref[o]]
        for h in range(2):
            out_ref[o, 8 * BASES + h : 8 * BASES + h + 1] = halves[h]


def terms_of(base):
    u, v, vort, strain, stretch = base
    return [u, v, vort, strain, stretch, vort * vort, vort * strain, vort * stretch, strain * strain, stretch * stretch,
            strain * stretch, u * vort, v * vort, u * strain, v * stretch, u * v]


def library_kernel(x_ref, out_hbm, gram_ref, out_ref, sem):
    slots = x_ref.shape[0] // BLOCK_ROWS
    copies = []
    for k in range(8):
        base = [x_ref[pl.ds(8 * n + k, slots, stride=BLOCK_ROWS), :] for n in range(BASES)]
        for n, x in enumerate(terms_of(base)):
            out_ref[k, pl.ds(n, slots, stride=TERMS), :] = x
        copies.append(pltpu.make_async_copy(out_ref.at[k], out_hbm.at[:, pl.ds(k * LANES, LANES)], sem.at[k]))
        copies[k].start()
    totals = [jnp.sum(x_ref[pl.ds(40 + half, slots, stride=BLOCK_ROWS), :], axis=0, keepdims=True) for half in range(2)]
    for n in range(TERMS):
        row = totals[n // 8]
        row = pltpu.roll(row, LANES - n % 8 * TERMS, 1) if n % 8 else row
        for c in range(gram_ref.shape[0]):
            gram_ref[c, n : n + 1] = row
    for copy in copies:
        copy.wait()


VMEM = pl.BlockSpec(memory_space=pltpu.VMEM)
HBM = pl.BlockSpec(memory_space=pltpu.HBM)
SMEM = pl.BlockSpec(memory_space=pltpu.SMEM)
PARAMS = pltpu.CompilerParams(vmem_limit_bytes=24 << 20)


def struct(*shape):
    return jax.ShapeDtypeStruct(shape, F32)


def per_device(u_velocity, v_velocity, ocean_mask, tile_owner, lower_edge_quarter_turns):
    tiles, columns = lax.axis_size("tile"), lax.axis_size("col")
    onward = lambda count: [(i, (i + 1) % count) for i in range(count)]
    back = lambda count: [((i + 1) % count, i) for i in range(count)]
    here = lax.axis_index("tile").astype(jnp.int32)[None]
    in_hbm = lambda x: pltpu.with_memory_space_constraint(x, pltpu.HBM)
    up, down = pl.pallas_call(
        send_kernel,
        out_shape=[struct(2 * HALO, POOL * CELLS)] * 2,
        in_specs=[SMEM] + [HBM] * 3,
        out_specs=[VMEM] * 2,
        scratch_shapes=[pltpu.VMEM((2, 2, 16, POOL * CELLS), F32), pltpu.SMEM((tiles,), jnp.int32),
                        pltpu.SemaphoreType.DMA((2, 2)), pltpu.SemaphoreType.DMA],
        compiler_params=PARAMS,
        name="send_rows",
    )(here, *[in_hbm(x) for x in (lower_edge_quarter_turns, u_velocity, v_velocity)])
    up, down, u_velocity, v_velocity = lax.optimization_barrier((up, down, u_velocity, v_velocity))
    above = lax.ppermute(down, "tile", onward(tiles))
    below = lax.ppermute(up, "tile", back(tiles))
    column = lambda c: pl.BlockSpec((POOL * CELLS, LANES), lambda i: (0, c))
    whole = lambda *shape: pl.BlockSpec(shape, lambda i: (0,) * len(shape))
    halo = whole(2 * HALO, POOL * CELLS)
    rows = 2 * POOL * CELLS
    parts, weights, rim, early = pl.pallas_call(
        prepare_kernel,
        out_shape=[jax.ShapeDtypeStruct((rows, 2 * POOL * CELLS), BF16),
                   jax.ShapeDtypeStruct((POOL * CELLS, 10 * LANES), BF16), struct(FULL, LANES),
                   struct(rows, EARLY * LANES)],
        grid=(1,),
        in_specs=[column(c) for c in range(4)] * 2 + [HBM],
        out_specs=[VMEM] * 4,
        scratch_shapes=[pltpu.VMEM((rows, 2 * LANES), BF16)] + [pltpu.VMEM((POOL, PAD + CELLS, LANES), F32)] * 2
        + [pltpu.SemaphoreType.DMA],
        compiler_params=PARAMS,
        name="prepare_rows",
    )(*[u_velocity] * 4, *[v_velocity] * 4, in_hbm(jnp.asarray(column_weights())))
    to_left, to_right, own = pl.pallas_call(
        rim_kernel,
        out_shape=[struct(8, FULL), struct(8, FULL), struct(16, FULL)],
        grid=(1,),
        in_specs=[halo] * 2 + [pl.BlockSpec((2 * LANES, LANES), lambda i: (0, 9)), whole(FULL, LANES)],
        out_specs=[whole(8, FULL), whole(8, FULL), whole(16, FULL)],
        scratch_shapes=[pltpu.VMEM((2, 2 * HALO, LANES), F32), pltpu.VMEM((2 * 2 * POOL * 8, LANES), F32),
                        pltpu.VMEM((FULL, LANES), F32)],
        compiler_params=PARAMS,
        name="rim_columns",
    )(above, below, weights, rim)
    from_right = lax.ppermute(to_left, "col", back(columns))
    from_left = lax.ppermute(to_right, "col", onward(columns))
    main = pl.pallas_call(
        main_kernel,
        out_shape=struct(2, FULL, LANES),
        in_specs=[VMEM] * 6,
        out_specs=VMEM,
        scratch_shapes=[pltpu.VMEM((2, 4, 2 * HALO, LANES), F32), pltpu.VMEM((2 * POOL * 16, POOL * CELLS), F32),
                        pltpu.VMEM((2, POOL, FULL, LANES), F32)],
        compiler_params=PARAMS,
        name="main_columns",
    )(parts, early, weights, above, below, own)
    blocks = pl.pallas_call(
        base_kernel,
        out_shape=struct(tiles, BLOCK_ROWS, LANES),
        in_specs=[SMEM] * 2 + [VMEM] * 5,
        out_specs=VMEM,
        scratch_shapes=[pltpu.VMEM((2, FULL, LANES), F32), pltpu.VMEM((BASES, CELLS, LANES), F32),
                        pltpu.VMEM((TERMS, CELLS, LANES), F32), pltpu.VMEM((TERMS * TERMS, LANES), F32),
                        pltpu.VMEM((17, 8 * BASES, LANES), F32), pltpu.SMEM((tiles + 1,), jnp.int32)],
        compiler_params=PARAMS,
        name="base_fields",
    )(ocean_mask, tile_owner, main, own, from_left, from_right, jnp.asarray(place_matrix()))
    blocks = lax.all_to_all(blocks, "tile", split_axis=0, concat_axis=0, tiled=True)
    library, gram = pl.pallas_call(
        library_kernel,
        out_shape=[struct(tiles * TERMS, SIDE * SIDE), struct(columns, TERMS, LANES)],
        in_specs=[VMEM],
        out_specs=[HBM, VMEM],
        scratch_shapes=[pltpu.VMEM((8, tiles * TERMS, LANES), F32), pltpu.SemaphoreType.DMA((8,))],
        compiler_params=PARAMS,
        name="library_terms",
    )(blocks.reshape(tiles * BLOCK_ROWS, LANES))
    gram = lax.all_to_all(gram, "col", split_axis=0, concat_axis=0, tiled=True)
    gram = jnp.sum(gram, axis=0)[:, :TERMS] / (CELLS * CELLS)
    return library.reshape(1, 1, tiles, TERMS, SIDE * SIDE), gram


def solution(mesh):
    in_specs = (P("tile", "col"), P("tile", "col"), P("tile", "col"), P("tile", "col"), P())
    out_specs = (P("tile", "col", None, None, None), P())
    return jax.shard_map(
        per_device, mesh=mesh, in_specs=in_specs, out_specs=out_specs, check_vma=False
    )
```

```python
import math

import jax
import jax.numpy as jnp
import ml_dtypes
import numpy as np
from jax import lax
from jax.experimental import pallas as pl
from jax.experimental.pallas import tpu as pltpu
from jax.sharding import PartitionSpec as P

PASSES = 8
KAPPA = 0.2
POOL = 4
CELLS = 128
HALO = 12
SIDE = 32
TERMS = 16
PAD = 8
FULL = CELLS + 2 * PAD
LANES = 128
BASES = 5
BLOCK_ROWS = 24
SIDES, ENDS, GRAM = 16, 17, 18
F32 = jnp.float32
BF16 = jnp.bfloat16

SCALE = KAPPA**PASSES / (POOL * POOL)
RIM_COLS = (-2, -1, 0, CELLS - 1, CELLS, CELLS + 1)


def across(power, fine, coarse):
    total = 0
    for inner in range(POOL):
        offset = fine - (POOL * coarse + inner)
        if abs(offset) <= power and (power + offset) % 2 == 0:
            total += math.comb(power, (power + offset) // 2)
    return total


def column_weights():
    fine = CELLS * POOL
    main = np.zeros((fine, 9 * LANES), np.float32)
    rim = np.zeros((fine, LANES), np.float32)
    for j in range(PASSES + 1):
        for coarse in range(-2, CELLS + 2):
            for f in range(max(0, POOL * coarse - PASSES), min(fine, POOL * coarse + POOL + PASSES)):
                value = math.comb(PASSES, j) * across(PASSES - j, f, coarse)
                if 0 <= coarse < CELLS:
                    main[f, (PASSES - j) * LANES + coarse] = value
                if coarse in RIM_COLS:
                    rim[f, 6 * j + RIM_COLS.index(coarse)] = value
    assert not rim[64 : fine - 64].any()
    rim[LANES - 64 : LANES] = rim[fine - 64 :]
    rim[LANES : 2 * LANES] = rim[:LANES]
    weights = np.concatenate([main, rim], axis=1)
    out = weights.astype(ml_dtypes.bfloat16)
    assert (out.astype(np.float32) == weights).all()
    return out


def rim_selector():
    row = lax.broadcasted_iota(jnp.int32, (32, 1), 0)
    source = jnp.full((32, 1), -1, jnp.int32)
    for f in range(2):
        for c in range(3):
            source = jnp.where(row == 3 * f + c, 64 * f + c, source)
            source = jnp.where(row == 8 + 3 * f + c, 64 * f + 3 + c, source)
        source = jnp.where(row == 16 + 2 * f, 64 * f + 1, source)
        source = jnp.where(row == 17 + 2 * f, 64 * f + 4, source)
    lane = lax.broadcasted_iota(jnp.int32, (32, 3 * LANES), 1) % LANES
    return jnp.where(lane == source, 1.0, 0.0).astype(BF16)


def place_matrix():
    place = np.zeros((3, 32, 4 * LANES), np.float32)
    for f in range(2):
        add, rim = 2 * f * LANES, (2 * f + 1) * LANES
        place[:, 3 * f + 0, rim + 0] = 1.0
        place[:, 3 * f + 1, add + 0] = 1.0
        place[:, 3 * f + 2, add + 1] = 1.0
        place[:, 8 + 3 * f + 0, add + CELLS - 2] = 1.0
        place[:, 8 + 3 * f + 1, add + CELLS - 1] = 1.0
        place[:, 8 + 3 * f + 2, rim + CELLS - 1] = 1.0
        place[:, 16 + 2 * f, rim + 0] = 1.0
        place[:, 17 + 2 * f, rim + CELLS - 1] = 1.0
    return place.reshape(96, 4 * LANES).astype(ml_dtypes.bfloat16)


def head(x):
    scaled = x * 65537.0
    return scaled - (scaled - x)


def two_parts(x):
    high = head(x)
    return high.astype(BF16), (x - high).astype(BF16)


def three_parts(x):
    high = head(x)
    rest = x - high
    mid = head(rest)
    return high.astype(BF16), mid.astype(BF16), (rest - mid).astype(BF16)


def dot(a, b, dims=(((1,), (0,)), ((), ()))):
    return lax.dot_general(a, b, dims, preferred_element_type=F32)


def three_rows(t):
    rows = t[0].shape[0]
    up = pltpu.roll(t[3], 1, 0)
    down = pltpu.roll(t[0], rows - 1, 0)
    left, middle, right = t[0] + t[1], t[1] + t[2], t[2] + t[3]
    return [left + up, t[0] + middle, middle + t[3], right + down]


def turn(first, second, k):
    cosine = jnp.where(k == 0, 1.0, jnp.where(k == 2, -1.0, 0.0)).astype(F32)
    sine = jnp.where(k == 1, 1.0, jnp.where(k == 3, -1.0, 0.0)).astype(F32)
    return cosine * first - sine * second, sine * first + cosine * second


def send_kernel(here_ref, turns_hbm, u_hbm, v_hbm, up_ref, down_ref, x_ref, turns_ref, sem, turns_sem):
    rows = u_hbm.shape[0]
    copies = [pltpu.make_async_copy(hbm.at[pl.ds(start, 16)], x_ref.at[side, f], sem.at[side, f])
              for side, start in enumerate((0, rows - 16)) for f, hbm in enumerate((u_hbm, v_hbm))]
    table = pltpu.make_async_copy(turns_hbm, turns_ref, turns_sem)
    table.start()
    for copy in copies:
        copy.start()
    table.wait()
    tiles = turns_ref.shape[0]
    here = here_ref[0]
    k_up = lax.rem(4 - turns_ref[here], 4)
    k_down = turns_ref[lax.rem(here + 1, tiles)]
    for copy in copies:
        copy.wait()
    for side, (to_ref, k, start) in enumerate(((up_ref, k_up, 0), (down_ref, k_down, 16 - HALO))):
        for f, x in enumerate(turn(x_ref[side, 0], x_ref[side, 1], k)):
            to_ref[f * HALO : (f + 1) * HALO] = x[start : start + HALO]


EARLY = 4


def prepare_kernel(*refs):
    w_hbm, parts_ref, w_out, rim_ref, early_ref, rim_parts_ref, first_ref, last_ref, sem = refs[8:]
    copy = pltpu.make_async_copy(w_hbm, w_out, sem)
    copy.start()
    lane = lax.broadcasted_iota(jnp.int32, (1, LANES), 1)
    fine = POOL * CELLS
    for f in range(2):
        for p in range(POOL):
            spot = slice((f * POOL + p) * CELLS, (f * POOL + p + 1) * CELLS)
            pieces = [two_parts(refs[4 * f + c][pl.ds(p, CELLS, stride=POOL), :]) for c in range(4)]
            for part in range(2):
                for c in range(4):
                    parts_ref[spot, part * fine + c * LANES : part * fine + (c + 1) * LANES] = pieces[c][part]
                rim_parts_ref[spot, part * LANES : (part + 1) * LANES] = jnp.where(
                    lane < 64, pieces[0][part], pieces[3][part])
    copy.wait()
    z = dot(rim_parts_ref[...], w_out[: 2 * LANES, 9 * LANES :])
    for p in range(POOL):
        u, v = [z[(f * POOL + p) * CELLS : (f * POOL + p + 1) * CELLS] for f in range(2)]
        both = jnp.where(lane < 64, u, pltpu.roll(v, 64, 1))
        for to_ref in (first_ref, last_ref):
            to_ref[p, :PAD] = jnp.zeros((PAD, LANES), F32)
            to_ref[p, PAD:] = both
    for _ in range(PASSES):
        new = three_rows([pltpu.roll(last_ref[p], LANES - 6, 1) for p in range(POOL)])
        for p in range(POOL):
            last_ref[p] = new[p] + first_ref[p]
    pooled = ((last_ref[0] + last_ref[1]) + (last_ref[2] + last_ref[3])) * SCALE
    rim_ref[: PAD + CELLS] = pooled
    rim_ref[PAD + CELLS :] = pooled[:PAD]
    for start in range(0, EARLY, 2):
        cut = slice(start * LANES, (start + 2) * LANES)
        early_ref[:, cut] = dot(parts_ref[:, :fine], w_out[:, cut]) + dot(parts_ref[:, fine:], w_out[:, cut])


def rim_kernel(above_ref, below_ref, w_ref, rim_in, left_ref, right_ref, own_ref, rows_ref, strip_ref, rim_ref):
    lane = lax.broadcasted_iota(jnp.int32, (1, LANES), 1)
    strip_ref[...] = jnp.zeros_like(strip_ref)
    for s, (x_ref, start) in enumerate(((above_ref, 1), (below_ref, 4))):
        ends = jnp.where(lane < 64, x_ref[:, :LANES], x_ref[:, 3 * LANES :])
        rows_ref[s] = ends
        for f in range(2):
            for p in range(POOL):
                spot = ((f * 2 + s) * POOL + p) * 8 + start
                strip_ref[spot : spot + 3] = rows_ref[s, pl.ds(f * HALO + p, 3, stride=POOL), :]
    z = dot(jnp.concatenate(two_parts(strip_ref[...]), axis=1), w_ref[...])
    rim_ref[...] = rim_in[...]
    for s, (spot, start) in enumerate(((7, 3), (PAD + CELLS - 2, 2))):
        first = []
        for p in range(POOL):
            u, v = [z[((f * 2 + s) * POOL + p) * 8 : ((f * 2 + s) * POOL + p + 1) * 8] for f in range(2)]
            first.append(jnp.where(lane < 64, u, pltpu.roll(v, 64, 1)))
        last = first
        for _ in range(PASSES):
            last = [a + b for a, b in zip(three_rows([pltpu.roll(x, LANES - 6, 1) for x in last]), first)]
        pooled = ((last[0] + last[1]) + (last[2] + last[3])) * SCALE
        rim_ref[spot : spot + 3] = rim_ref[spot : spot + 3] + pooled[start : start + 3]
    turned = jnp.transpose(rim_ref[...])
    for to_ref, columns in ((left_ref, (0, 1, 2)), (right_ref, (3, 4, 5)), (own_ref, (1, 4))):
        to_ref[...] = jnp.zeros_like(to_ref)
        for f in range(2):
            for place, c in enumerate(columns):
                spot = len(columns) * f + place
                to_ref[spot : spot + 1] = turned[64 * f + c : 64 * f + c + 1]


def main_kernel(parts_ref, early_ref, w_ref, above_ref, below_ref, _, main_ref, rows_ref, strip_ref, sum_ref):
    strip_ref[...] = jnp.zeros_like(strip_ref)
    for s, (x_ref, start) in enumerate(((above_ref, 5), (below_ref, 8))):
        for c in range(4):
            cut = slice(c * LANES, (c + 1) * LANES)
            rows_ref[s, c] = x_ref[:, cut]
            for f in range(2):
                for p in range(POOL):
                    spot = (f * POOL + p) * 16 + start
                    strip_ref[spot : spot + 3, cut] = rows_ref[s, c, pl.ds(f * HALO + p, 3, stride=POOL), :]
    strips = jnp.concatenate(two_parts(strip_ref[...]), axis=1)
    fine = POOL * CELLS
    for start in range(0, 9, 2):
        wide = min(2, 9 - start)
        w = w_ref[:, start * LANES : (start + wide) * LANES]
        if start < EARLY:
            z = early_ref[:, start * LANES : (start + wide) * LANES]
        else:
            z = dot(parts_ref[:, :fine], w) + dot(parts_ref[:, fine:], w)
        z_strip = dot(strips[:, :fine], w) + dot(strips[:, fine:], w)
        for stage in range(start, start + wide):
            cut = slice((stage - start) * LANES, (stage - start + 1) * LANES)
            for f in range(2):
                own = []
                for p in range(POOL):
                    block = f * POOL + p
                    own.append(jnp.concatenate([
                        z_strip[block * 16 : block * 16 + 8, cut], z[block * CELLS : (block + 1) * CELLS, cut],
                        z_strip[block * 16 + 8 : block * 16 + 16, cut]], axis=0))
                if stage:
                    own = [a + b for a, b in zip(three_rows([sum_ref[f, p] for p in range(POOL)]), own)]
                for p in range(POOL):
                    sum_ref[f, p] = own[p]
    for f in range(2):
        main_ref[f] = ((sum_ref[f, 0] + sum_ref[f, 1]) + (sum_ref[f, 2] + sum_ref[f, 3])) * SCALE


def base_kernel(mask_ref, owner_ref, main_ref, own_ref, from_left_ref, from_right_ref, place_ref, out_ref, field_ref,
                base_ref, term_ref, gram_ref, pack_ref, tile_ref, side_ref):
    lane = lax.broadcasted_iota(jnp.int32, (1, LANES), 1)
    received = jnp.concatenate([from_left_ref[...], from_right_ref[...], own_ref[...]], axis=0)
    placed = dot(jnp.concatenate(three_parts(received), axis=0), place_ref[...], (((0,), (0,)), ((), ())))
    inner = slice(PAD, PAD + CELLS)
    slopes = []
    for f in range(2):
        full = main_ref[f] + placed[:, 2 * f * LANES : (2 * f + 1) * LANES]
        field_ref[f] = full
        rim = placed[inner, (2 * f + 1) * LANES : (2 * f + 2) * LANES]
        centre = full[inner]
        left = jnp.where(lane == 0, rim, pltpu.roll(centre, 1, 1))
        right = jnp.where(lane == LANES - 1, rim, pltpu.roll(centre, LANES - 1, 1))
        side_ref[f, 0] = left
        side_ref[f, 1] = right
        dx = (right - left) * 0.5
        dy = (field_ref[f, PAD + 1 : PAD + 1 + CELLS] - field_ref[f, PAD - 1 : PAD - 1 + CELLS]) * 0.5
        slopes.append((centre, dx, dy))
    (u, u_dx, u_dy), (v, v_dx, v_dy) = slopes
    grid = CELLS // SIDE
    rows = []
    for a in range(grid):
        row = jnp.zeros((1, LANES), F32)
        for e in range(grid):
            row = jnp.where(lane // SIDE == e, (mask_ref[a, e] == 1).astype(F32), row)
        rows.append(jnp.broadcast_to(row, (SIDE, LANES)))
    live = jnp.concatenate(rows, axis=0) > 0.5
    for n, x in enumerate((u, v, v_dx - u_dy, u_dy + v_dx, u_dx - v_dy)):
        base_ref[n] = jnp.where(live, x, 0.0)
    for n, x in enumerate(terms_of([base_ref[n] for n in range(BASES)])):
        term_ref[n] = x
    for n in range(TERMS):
        first = term_ref[n]
        for m in range(n, TERMS):
            product = (first * term_ref[m]).reshape(CELLS // 8, 8, LANES)
            total = jnp.sum(jnp.sum(product, axis=0), axis=0, keepdims=True)
            gram_ref[n * TERMS + m : n * TERMS + m + 1] = total
            if m > n:
                gram_ref[m * TERMS + n : m * TERMS + n + 1] = total
    totals = jnp.sum(gram_ref[...], axis=1, keepdims=True)
    row = lax.broadcasted_iota(jnp.int32, (TERMS * TERMS, 1), 0)
    spread = jnp.where(row % LANES == lane, totals, 0.0)
    halves = [jnp.sum(spread[h * LANES : (h + 1) * LANES], axis=0, keepdims=True) for h in range(2)]
    owners = out_ref.shape[0]
    nothing = grid * grid
    for o in range(owners + 1):
        tile_ref[o] = nothing
    for a in range(grid):
        for e in range(grid):
            tile_ref[jnp.where(mask_ref[a, e] == 1, owner_ref[a, e], owners)] = a * grid + e
    pack_ref[nothing] = jnp.zeros((BLOCK_ROWS, LANES), F32)
    group = lane // SIDE
    rows_of = lax.broadcasted_iota(jnp.int32, (8, LANES), 0)
    for a in range(grid):
        sides = [jnp.zeros((8, LANES), F32)] * grid
        ends = []
        for f in range(2):
            pieces = [field_ref[f, pl.ds(PAD + a * SIDE + q, 8, stride=4), :] for q in range(grid)]
            for e in range(grid):
                block = None
                for q in range(grid):
                    x = pltpu.roll(pieces[q], (q - e) % grid * SIDE, 1) if q != e else pieces[q]
                    block = x if block is None else jnp.where(group == q, x, block)
                pack_ref[a * grid + e, 8 * f : 8 * f + 8] = block
            for side in range(2):
                ends.append(field_ref[f, PAD + a * SIDE - 1 + side * (SIDE + 1) : PAD + a * SIDE + side * (SIDE + 1)])
                for q in range(grid):
                    x = side_ref[f, side, pl.ds(a * SIDE + q, 8, stride=4), :]
                    here = lane == rows_of + (q * SIDE + 8 * side + 16 * f)
                    for e in range(grid):
                        at = e * SIDE + side * (SIDE - 1)
                        sides[e] = jnp.where(here, x[:, at : at + 1], sides[e])
        for e in range(grid):
            pack_ref[a * grid + e, SIDES : SIDES + 1] = jnp.sum(sides[e], axis=0, keepdims=True)
            row = None
            for q in range(4):
                x = pltpu.roll(ends[q], (q - e) % grid * SIDE, 1) if q != e else ends[q]
                row = x if row is None else jnp.where(group == q, x, row)
            pack_ref[a * grid + e, ENDS : ENDS + 1] = row
    for o in range(owners):
        out_ref[o] = pack_ref[tile_ref[o]]
        for h in range(2):
            out_ref[o, GRAM + h : GRAM + h + 1] = halves[h]


def terms_of(base):
    u, v, vort, strain, stretch = base
    return [u, v, vort, strain, stretch, vort * vort, vort * strain, vort * stretch, strain * strain, stretch * stretch,
            strain * stretch, u * vort, v * vort, u * strain, v * stretch, u * v]


def library_kernel(x_ref, out_hbm, gram_ref, out_ref, sem):
    slots = x_ref.shape[0] // BLOCK_ROWS
    rows = lambda at: x_ref[pl.ds(at, slots, stride=BLOCK_ROWS), :]
    turn_by = lambda x, count: pltpu.roll(x, count % LANES, 1) if count % LANES else x
    lane = lax.broadcasted_iota(jnp.int32, (1, LANES), 1)
    sides, ends = rows(SIDES), rows(ENDS)
    fields = [[rows(8 * f + k) for k in range(8)] for f in range(2)]
    lower = [[turn_by(x, SIDE) for x in field] for field in fields]
    higher = [[turn_by(x, -SIDE) for x in field] for field in fields]

    def slopes(f, k):
        x = fields[f][k]
        left = jnp.where(lane % SIDE == 0, turn_by(sides, -(k + 16 * f)), turn_by(x, 1))
        right = jnp.where(lane % SIDE == SIDE - 1, turn_by(sides, SIDE - 1 - (k + 8 + 16 * f)), turn_by(x, -1))
        before = lower[f][k - 1] if k else turn_by(ends, -64 * f)
        after = higher[f][k + 1] if k < 7 else turn_by(ends, 64 - 64 * f)
        up = jnp.where(lane < SIDE, before, lower[f][k])
        down = jnp.where(lane >= LANES - SIDE, after, higher[f][k])
        return (right - left) * 0.5, (down - up) * 0.5

    copies = []
    for k in range(8):
        (u_dx, u_dy), (v_dx, v_dy) = slopes(0, k), slopes(1, k)
        base = [fields[0][k], fields[1][k], v_dx - u_dy, u_dy + v_dx, u_dx - v_dy]
        for n, x in enumerate(terms_of(base)):
            out_ref[k, pl.ds(n, slots, stride=TERMS), :] = x
        copies.append(pltpu.make_async_copy(out_ref.at[k], out_hbm.at[:, pl.ds(k * LANES, LANES)], sem.at[k]))
        copies[k].start()
    totals = [jnp.sum(rows(GRAM + half), axis=0, keepdims=True) for half in range(2)]
    for n in range(TERMS):
        row = totals[n // 8]
        row = pltpu.roll(row, LANES - n % 8 * TERMS, 1) if n % 8 else row
        for c in range(gram_ref.shape[0]):
            gram_ref[c, n : n + 1] = row
    for copy in copies:
        copy.wait()


VMEM = pl.BlockSpec(memory_space=pltpu.VMEM)
HBM = pl.BlockSpec(memory_space=pltpu.HBM)
SMEM = pl.BlockSpec(memory_space=pltpu.SMEM)
PARAMS = pltpu.CompilerParams(vmem_limit_bytes=24 << 20)


def struct(*shape):
    return jax.ShapeDtypeStruct(shape, F32)


def per_device(u_velocity, v_velocity, ocean_mask, tile_owner, lower_edge_quarter_turns):
    tiles, columns = lax.axis_size("tile"), lax.axis_size("col")
    onward = lambda count: [(i, (i + 1) % count) for i in range(count)]
    back = lambda count: [((i + 1) % count, i) for i in range(count)]
    here = lax.axis_index("tile").astype(jnp.int32)[None]
    in_hbm = lambda x: pltpu.with_memory_space_constraint(x, pltpu.HBM)
    up, down = pl.pallas_call(
        send_kernel,
        out_shape=[struct(2 * HALO, POOL * CELLS)] * 2,
        in_specs=[SMEM] + [HBM] * 3,
        out_specs=[VMEM] * 2,
        scratch_shapes=[pltpu.VMEM((2, 2, 16, POOL * CELLS), F32), pltpu.SMEM((tiles,), jnp.int32),
                        pltpu.SemaphoreType.DMA((2, 2)), pltpu.SemaphoreType.DMA],
        compiler_params=PARAMS,
        name="send_rows",
    )(here, *[in_hbm(x) for x in (lower_edge_quarter_turns, u_velocity, v_velocity)])
    up, down, u_velocity, v_velocity = lax.optimization_barrier((up, down, u_velocity, v_velocity))
    above = lax.ppermute(down, "tile", onward(tiles))
    below = lax.ppermute(up, "tile", back(tiles))
    column = lambda c: pl.BlockSpec((POOL * CELLS, LANES), lambda i: (0, c))
    whole = lambda *shape: pl.BlockSpec(shape, lambda i: (0,) * len(shape))
    halo = whole(2 * HALO, POOL * CELLS)
    rows = 2 * POOL * CELLS
    parts, weights, rim, early = pl.pallas_call(
        prepare_kernel,
        out_shape=[jax.ShapeDtypeStruct((rows, 2 * POOL * CELLS), BF16),
                   jax.ShapeDtypeStruct((POOL * CELLS, 10 * LANES), BF16), struct(FULL, LANES),
                   struct(rows, EARLY * LANES)],
        grid=(1,),
        in_specs=[column(c) for c in range(4)] * 2 + [HBM],
        out_specs=[VMEM] * 4,
        scratch_shapes=[pltpu.VMEM((rows, 2 * LANES), BF16)] + [pltpu.VMEM((POOL, PAD + CELLS, LANES), F32)] * 2
        + [pltpu.SemaphoreType.DMA],
        compiler_params=PARAMS,
        name="prepare_rows",
    )(*[u_velocity] * 4, *[v_velocity] * 4, in_hbm(jnp.asarray(column_weights())))
    to_left, to_right, own = pl.pallas_call(
        rim_kernel,
        out_shape=[struct(8, FULL), struct(8, FULL), struct(16, FULL)],
        grid=(1,),
        in_specs=[halo] * 2 + [pl.BlockSpec((2 * LANES, LANES), lambda i: (0, 9)), whole(FULL, LANES)],
        out_specs=[whole(8, FULL), whole(8, FULL), whole(16, FULL)],
        scratch_shapes=[pltpu.VMEM((2, 2 * HALO, LANES), F32), pltpu.VMEM((2 * 2 * POOL * 8, LANES), F32),
                        pltpu.VMEM((FULL, LANES), F32)],
        compiler_params=PARAMS,
        name="rim_columns",
    )(above, below, weights, rim)
    from_right = lax.ppermute(to_left, "col", back(columns))
    from_left = lax.ppermute(to_right, "col", onward(columns))
    main = pl.pallas_call(
        main_kernel,
        out_shape=struct(2, FULL, LANES),
        in_specs=[VMEM] * 6,
        out_specs=VMEM,
        scratch_shapes=[pltpu.VMEM((2, 4, 2 * HALO, LANES), F32), pltpu.VMEM((2 * POOL * 16, POOL * CELLS), F32),
                        pltpu.VMEM((2, POOL, FULL, LANES), F32)],
        compiler_params=PARAMS,
        name="main_columns",
    )(parts, early, weights, above, below, own)
    blocks = pl.pallas_call(
        base_kernel,
        out_shape=struct(tiles, BLOCK_ROWS, LANES),
        in_specs=[SMEM] * 2 + [VMEM] * 5,
        out_specs=VMEM,
        scratch_shapes=[pltpu.VMEM((2, FULL, LANES), F32), pltpu.VMEM((BASES, CELLS, LANES), F32),
                        pltpu.VMEM((TERMS, CELLS, LANES), F32), pltpu.VMEM((TERMS * TERMS, LANES), F32),
                        pltpu.VMEM((17, BLOCK_ROWS, LANES), F32), pltpu.SMEM((tiles + 1,), jnp.int32),
                        pltpu.VMEM((2, 2, CELLS, LANES), F32)],
        compiler_params=PARAMS,
        name="base_fields",
    )(ocean_mask, tile_owner, main, own, from_left, from_right, jnp.asarray(place_matrix()))
    blocks = lax.all_to_all(blocks, "tile", split_axis=0, concat_axis=0, tiled=True)
    library, gram = pl.pallas_call(
        library_kernel,
        out_shape=[struct(tiles * TERMS, SIDE * SIDE), struct(columns, TERMS, LANES)],
        in_specs=[VMEM],
        out_specs=[HBM, VMEM],
        scratch_shapes=[pltpu.VMEM((8, tiles * TERMS, LANES), F32), pltpu.SemaphoreType.DMA((8,))],
        compiler_params=PARAMS,
        name="library_terms",
    )(blocks.reshape(tiles * BLOCK_ROWS, LANES))
    gram = lax.all_to_all(gram, "col", split_axis=0, concat_axis=0, tiled=True)
    gram = jnp.sum(gram, axis=0)[:, :TERMS] / (CELLS * CELLS)
    return library.reshape(1, 1, tiles, TERMS, SIDE * SIDE), gram


def solution(mesh):
    in_specs = (P("tile", "col"), P("tile", "col"), P("tile", "col"), P("tile", "col"), P())
    out_specs = (P("tile", "col", None, None, None), P())
    return jax.shard_map(
        per_device, mesh=mesh, in_specs=in_specs, out_specs=out_specs, check_vma=False
    )
```

```python
import math

import jax
import jax.numpy as jnp
import ml_dtypes
import numpy as np
from jax import lax
from jax.experimental import pallas as pl
from jax.experimental.pallas import tpu as pltpu
from jax.sharding import PartitionSpec as P

PASSES = 8
KAPPA = 0.2
POOL = 4
CELLS = 128
HALO = 12
SIDE = 32
TERMS = 16
PAD = 8
FULL = CELLS + 2 * PAD
LANES = 128
BASES = 5
BLOCK_ROWS = 24
SIDES, ENDS, GRAM = 16, 17, 18
F32 = jnp.float32
BF16 = jnp.bfloat16

SCALE = KAPPA**PASSES / (POOL * POOL)
RIM_COLS = (-2, -1, 0, CELLS - 1, CELLS, CELLS + 1)


def across(power, fine, coarse):
    total = 0
    for inner in range(POOL):
        offset = fine - (POOL * coarse + inner)
        if abs(offset) <= power and (power + offset) % 2 == 0:
            total += math.comb(power, (power + offset) // 2)
    return total


def column_weights():
    fine = CELLS * POOL
    main = np.zeros((fine, 9 * LANES), np.float32)
    rim = np.zeros((fine, LANES), np.float32)
    for j in range(PASSES + 1):
        for coarse in range(-2, CELLS + 2):
            for f in range(max(0, POOL * coarse - PASSES), min(fine, POOL * coarse + POOL + PASSES)):
                value = math.comb(PASSES, j) * across(PASSES - j, f, coarse)
                if 0 <= coarse < CELLS:
                    main[f, (PASSES - j) * LANES + coarse] = value
                if coarse in RIM_COLS:
                    rim[f, 6 * j + RIM_COLS.index(coarse)] = value
    assert not rim[64 : fine - 64].any()
    rim[LANES - 64 : LANES] = rim[fine - 64 :]
    rim[LANES : 2 * LANES] = rim[:LANES]
    weights = np.concatenate([main, rim], axis=1)
    out = weights.astype(ml_dtypes.bfloat16)
    assert (out.astype(np.float32) == weights).all()
    return out


def rim_selector():
    row = lax.broadcasted_iota(jnp.int32, (32, 1), 0)
    source = jnp.full((32, 1), -1, jnp.int32)
    for f in range(2):
        for c in range(3):
            source = jnp.where(row == 3 * f + c, 64 * f + c, source)
            source = jnp.where(row == 8 + 3 * f + c, 64 * f + 3 + c, source)
        source = jnp.where(row == 16 + 2 * f, 64 * f + 1, source)
        source = jnp.where(row == 17 + 2 * f, 64 * f + 4, source)
    lane = lax.broadcasted_iota(jnp.int32, (32, 3 * LANES), 1) % LANES
    return jnp.where(lane == source, 1.0, 0.0).astype(BF16)


def place_matrix():
    place = np.zeros((3, 32, 4 * LANES), np.float32)
    for f in range(2):
        add, rim = 2 * f * LANES, (2 * f + 1) * LANES
        place[:, 3 * f + 0, rim + 0] = 1.0
        place[:, 3 * f + 1, add + 0] = 1.0
        place[:, 3 * f + 2, add + 1] = 1.0
        place[:, 8 + 3 * f + 0, add + CELLS - 2] = 1.0
        place[:, 8 + 3 * f + 1, add + CELLS - 1] = 1.0
        place[:, 8 + 3 * f + 2, rim + CELLS - 1] = 1.0
        place[:, 16 + 2 * f, rim + 0] = 1.0
        place[:, 17 + 2 * f, rim + CELLS - 1] = 1.0
    return place.reshape(96, 4 * LANES).astype(ml_dtypes.bfloat16)


def head(x):
    scaled = x * 65537.0
    return scaled - (scaled - x)


def two_parts(x):
    high = head(x)
    return high.astype(BF16), (x - high).astype(BF16)


def three_parts(x):
    high = head(x)
    rest = x - high
    mid = head(rest)
    return high.astype(BF16), mid.astype(BF16), (rest - mid).astype(BF16)


def dot(a, b, dims=(((1,), (0,)), ((), ()))):
    return lax.dot_general(a, b, dims, preferred_element_type=F32)


def three_rows(t):
    rows = t[0].shape[0]
    up = pltpu.roll(t[3], 1, 0)
    down = pltpu.roll(t[0], rows - 1, 0)
    left, middle, right = t[0] + t[1], t[1] + t[2], t[2] + t[3]
    return [left + up, t[0] + middle, middle + t[3], right + down]


def turn(first, second, k):
    cosine = jnp.where(k == 0, 1.0, jnp.where(k == 2, -1.0, 0.0)).astype(F32)
    sine = jnp.where(k == 1, 1.0, jnp.where(k == 3, -1.0, 0.0)).astype(F32)
    return cosine * first - sine * second, sine * first + cosine * second


def send_kernel(here_ref, turns_hbm, u_hbm, v_hbm, up_ref, down_ref, x_ref, turns_ref, sem, turns_sem):
    rows = u_hbm.shape[0]
    copies = [pltpu.make_async_copy(hbm.at[pl.ds(start, 16)], x_ref.at[side, f], sem.at[side, f])
              for side, start in enumerate((0, rows - 16)) for f, hbm in enumerate((u_hbm, v_hbm))]
    table = pltpu.make_async_copy(turns_hbm, turns_ref, turns_sem)
    table.start()
    for copy in copies:
        copy.start()
    table.wait()
    tiles = turns_ref.shape[0]
    here = here_ref[0]
    k_up = lax.rem(4 - turns_ref[here], 4)
    k_down = turns_ref[lax.rem(here + 1, tiles)]
    for copy in copies:
        copy.wait()
    for side, (to_ref, k, start) in enumerate(((up_ref, k_up, 0), (down_ref, k_down, 16 - HALO))):
        for f, x in enumerate(turn(x_ref[side, 0], x_ref[side, 1], k)):
            to_ref[f * HALO : (f + 1) * HALO] = x[start : start + HALO]


EARLY = 8


def prepare_kernel(*refs):
    w_hbm, parts_ref, w_out, rim_ref, early_ref, rim_parts_ref, first_ref, last_ref, sem = refs[8:]
    copy = pltpu.make_async_copy(w_hbm, w_out, sem)
    copy.start()
    lane = lax.broadcasted_iota(jnp.int32, (1, LANES), 1)
    fine = POOL * CELLS
    for f in range(2):
        for p in range(POOL):
            spot = slice((f * POOL + p) * CELLS, (f * POOL + p + 1) * CELLS)
            pieces = [two_parts(refs[4 * f + c][pl.ds(p, CELLS, stride=POOL), :]) for c in range(4)]
            for part in range(2):
                for c in range(4):
                    parts_ref[spot, part * fine + c * LANES : part * fine + (c + 1) * LANES] = pieces[c][part]
                rim_parts_ref[spot, part * LANES : (part + 1) * LANES] = jnp.where(
                    lane < 64, pieces[0][part], pieces[3][part])
    copy.wait()
    z = dot(rim_parts_ref[...], w_out[: 2 * LANES, 9 * LANES :])
    for p in range(POOL):
        u, v = [z[(f * POOL + p) * CELLS : (f * POOL + p + 1) * CELLS] for f in range(2)]
        both = jnp.where(lane < 64, u, pltpu.roll(v, 64, 1))
        for to_ref in (first_ref, last_ref):
            to_ref[p, :PAD] = jnp.zeros((PAD, LANES), F32)
            to_ref[p, PAD:] = both
    for _ in range(PASSES):
        new = three_rows([pltpu.roll(last_ref[p], LANES - 6, 1) for p in range(POOL)])
        for p in range(POOL):
            last_ref[p] = new[p] + first_ref[p]
    pooled = ((last_ref[0] + last_ref[1]) + (last_ref[2] + last_ref[3])) * SCALE
    rim_ref[: PAD + CELLS] = pooled
    rim_ref[PAD + CELLS :] = pooled[:PAD]
    for start in range(0, EARLY, 2):
        cut = slice(start * LANES, (start + 2) * LANES)
        early_ref[:, cut] = dot(parts_ref[:, :fine], w_out[:, cut]) + dot(parts_ref[:, fine:], w_out[:, cut])


def rim_kernel(above_ref, below_ref, w_ref, rim_in, left_ref, right_ref, own_ref, rows_ref, strip_ref, rim_ref):
    lane = lax.broadcasted_iota(jnp.int32, (1, LANES), 1)
    strip_ref[...] = jnp.zeros_like(strip_ref)
    for s, (x_ref, start) in enumerate(((above_ref, 1), (below_ref, 4))):
        ends = jnp.where(lane < 64, x_ref[:, :LANES], x_ref[:, 3 * LANES :])
        rows_ref[s] = ends
        for f in range(2):
            for p in range(POOL):
                spot = ((f * 2 + s) * POOL + p) * 8 + start
                strip_ref[spot : spot + 3] = rows_ref[s, pl.ds(f * HALO + p, 3, stride=POOL), :]
    z = dot(jnp.concatenate(two_parts(strip_ref[...]), axis=1), w_ref[: 2 * LANES, 9 * LANES :])
    rim_ref[...] = rim_in[...]
    for s, (spot, start) in enumerate(((7, 3), (PAD + CELLS - 2, 2))):
        first = []
        for p in range(POOL):
            u, v = [z[((f * 2 + s) * POOL + p) * 8 : ((f * 2 + s) * POOL + p + 1) * 8] for f in range(2)]
            first.append(jnp.where(lane < 64, u, pltpu.roll(v, 64, 1)))
        last = first
        for _ in range(PASSES):
            last = [a + b for a, b in zip(three_rows([pltpu.roll(x, LANES - 6, 1) for x in last]), first)]
        pooled = ((last[0] + last[1]) + (last[2] + last[3])) * SCALE
        rim_ref[spot : spot + 3] = rim_ref[spot : spot + 3] + pooled[start : start + 3]
    turned = jnp.transpose(rim_ref[...])
    for to_ref, columns in ((left_ref, (0, 1, 2)), (right_ref, (3, 4, 5)), (own_ref, (1, 4))):
        to_ref[...] = jnp.zeros_like(to_ref)
        for f in range(2):
            for place, c in enumerate(columns):
                spot = len(columns) * f + place
                to_ref[spot : spot + 1] = turned[64 * f + c : 64 * f + c + 1]


PAIRS = [(n, m) for n in range(TERMS) for m in range(n, TERMS)]
REACH = 3


def slopes_of(ref, f, left, right):
    up = ref[f, PAD - 1 : PAD - 1 + CELLS]
    down = ref[f, PAD + 1 : PAD + 1 + CELLS]
    return (right - left) * 0.5, (down - up) * 0.5


def main_kernel(mask_ref, parts_ref, early_ref, w_ref, above_ref, below_ref, _, main_ref, live_ref, inner_ref, rows_ref,
                strip_ref, sum_ref, term_ref):
    strip_ref[...] = jnp.zeros_like(strip_ref)
    for s, (x_ref, start) in enumerate(((above_ref, 5), (below_ref, 8))):
        for c in range(4):
            cut = slice(c * LANES, (c + 1) * LANES)
            rows_ref[s, c] = x_ref[:, cut]
            for f in range(2):
                for p in range(POOL):
                    spot = (f * POOL + p) * 16 + start
                    strip_ref[spot : spot + 3, cut] = rows_ref[s, c, pl.ds(f * HALO + p, 3, stride=POOL), :]
    strips = jnp.concatenate(two_parts(strip_ref[...]), axis=1)
    fine = POOL * CELLS
    for start in range(0, 9, 2):
        wide = min(2, 9 - start)
        w = w_ref[:, start * LANES : (start + wide) * LANES]
        if start < EARLY:
            z = early_ref[:, start * LANES : (start + wide) * LANES]
        else:
            z = dot(parts_ref[:, :fine], w) + dot(parts_ref[:, fine:], w)
        z_strip = dot(strips[:, :fine], w) + dot(strips[:, fine:], w)
        for stage in range(start, start + wide):
            cut = slice((stage - start) * LANES, (stage - start + 1) * LANES)
            for f in range(2):
                own = []
                for p in range(POOL):
                    block = f * POOL + p
                    own.append(jnp.concatenate([
                        z_strip[block * 16 : block * 16 + 8, cut], z[block * CELLS : (block + 1) * CELLS, cut],
                        z_strip[block * 16 + 8 : block * 16 + 16, cut]], axis=0))
                if stage:
                    own = [a + b for a, b in zip(three_rows([sum_ref[f, p] for p in range(POOL)]), own)]
                for p in range(POOL):
                    sum_ref[f, p] = own[p]
    for f in range(2):
        main_ref[f] = ((sum_ref[f, 0] + sum_ref[f, 1]) + (sum_ref[f, 2] + sum_ref[f, 3])) * SCALE
    lane = lax.broadcasted_iota(jnp.int32, (1, LANES), 1)
    grid = CELLS // SIDE
    for a in range(grid):
        row = jnp.zeros((1, LANES), F32)
        for e in range(grid):
            row = jnp.where(lane // SIDE == e, (mask_ref[a, e] == 1).astype(F32), row)
        live_ref[a * SIDE : (a + 1) * SIDE] = jnp.broadcast_to(row, (SIDE, LANES))
    keep = (live_ref[...] > 0.5) & (lane >= REACH) & (lane < LANES - REACH)
    u, v = [main_ref[f, PAD : PAD + CELLS] for f in range(2)]
    (u_dx, u_dy), (v_dx, v_dy) = [slopes_of(main_ref, f, pltpu.roll(x, 1, 1), pltpu.roll(x, LANES - 1, 1))
                                  for f, x in enumerate((u, v))]
    for n, x in enumerate((u, v, v_dx - u_dy, u_dy + v_dx, u_dx - v_dy)):
        term_ref[n] = jnp.where(keep, x, 0.0)
    for n, x in enumerate(terms_of([term_ref[n] for n in range(BASES)])):
        if n >= BASES:
            term_ref[n] = x
    for place, (n, m) in enumerate(PAIRS):
        product = (term_ref[n] * term_ref[m]).reshape(CELLS // 8, 8, LANES)
        inner_ref[place] = jnp.sum(product, axis=0)


def base_kernel(mask_vmem, owner_vmem, main_ref, live_ref, inner_ref, own_ref, from_left_ref, from_right_ref, place_ref,
                out_ref, field_ref, gram_ref, pack_ref, tile_ref, side_ref, mask_ref, owner_ref, sem):
    tables = [pltpu.make_async_copy(mask_vmem, mask_ref, sem.at[0]),
              pltpu.make_async_copy(owner_vmem, owner_ref, sem.at[1])]
    for table in tables:
        table.start()
    lane = lax.broadcasted_iota(jnp.int32, (1, LANES), 1)
    received = jnp.concatenate([from_left_ref[...], from_right_ref[...], own_ref[...]], axis=0)
    placed = dot(jnp.concatenate(three_parts(received), axis=0), place_ref[...], (((0,), (0,)), ((), ())))
    inner = slice(PAD, PAD + CELLS)
    slopes = []
    for f in range(2):
        full = main_ref[f] + placed[:, 2 * f * LANES : (2 * f + 1) * LANES]
        field_ref[f] = full
        rim = placed[inner, (2 * f + 1) * LANES : (2 * f + 2) * LANES]
        centre = full[inner]
        left = jnp.where(lane == 0, rim, pltpu.roll(centre, 1, 1))
        right = jnp.where(lane == LANES - 1, rim, pltpu.roll(centre, LANES - 1, 1))
        side_ref[f, 0] = left
        side_ref[f, 1] = right
        slopes.append((centre, *slopes_of(field_ref, f, left, right)))
    (u, u_dx, u_dy), (v, v_dx, v_dy) = slopes
    live = live_ref[...] > 0.5
    outer = []
    for x in (u, v, v_dx - u_dy, u_dy + v_dx, u_dx - v_dy):
        x = jnp.where(live, x, 0.0)
        tile = jnp.zeros((8, LANES), F32)
        for b in range(CELLS // 8):
            tile = jnp.where(lane // 8 == b, pltpu.roll(x[8 * b : 8 * b + 8], (REACH + 8 * b) % LANES, 1), tile)
        outer.append(jnp.where(lane % 8 < 2 * REACH, tile, 0.0))
    outer = terms_of(outer)
    for place, (n, m) in enumerate(PAIRS):
        total = jnp.sum(inner_ref[place] + outer[n] * outer[m], axis=0, keepdims=True)
        gram_ref[n * TERMS + m : n * TERMS + m + 1] = total
        if m > n:
            gram_ref[m * TERMS + n : m * TERMS + n + 1] = total
    totals = jnp.sum(gram_ref[...], axis=1, keepdims=True)
    row = lax.broadcasted_iota(jnp.int32, (TERMS * TERMS, 1), 0)
    spread = jnp.where(row % LANES == lane, totals, 0.0)
    halves = [jnp.sum(spread[h * LANES : (h + 1) * LANES], axis=0, keepdims=True) for h in range(2)]
    owners = out_ref.shape[0]
    grid = CELLS // SIDE
    nothing = grid * grid
    for table in tables:
        table.wait()
    for o in range(owners + 1):
        tile_ref[o] = nothing
    for a in range(grid):
        for e in range(grid):
            tile_ref[jnp.where(mask_ref[a, e] == 1, owner_ref[a, e], owners)] = a * grid + e
    pack_ref[nothing] = jnp.zeros((BLOCK_ROWS, LANES), F32)
    group = lane // SIDE
    rows_of = lax.broadcasted_iota(jnp.int32, (8, LANES), 0)
    for a in range(grid):
        sides = [jnp.zeros((8, LANES), F32)] * grid
        ends = []
        for f in range(2):
            pieces = [field_ref[f, pl.ds(PAD + a * SIDE + q, 8, stride=4), :] for q in range(grid)]
            for e in range(grid):
                block = None
                for q in range(grid):
                    x = pltpu.roll(pieces[q], (q - e) % grid * SIDE, 1) if q != e else pieces[q]
                    block = x if block is None else jnp.where(group == q, x, block)
                pack_ref[a * grid + e, 8 * f : 8 * f + 8] = block
            for side in range(2):
                ends.append(field_ref[f, PAD + a * SIDE - 1 + side * (SIDE + 1) : PAD + a * SIDE + side * (SIDE + 1)])
                for q in range(grid):
                    x = side_ref[f, side, pl.ds(a * SIDE + q, 8, stride=4), :]
                    here = lane == rows_of + (q * SIDE + 8 * side + 16 * f)
                    for e in range(grid):
                        at = e * SIDE + side * (SIDE - 1)
                        sides[e] = jnp.where(here, x[:, at : at + 1], sides[e])
        for e in range(grid):
            pack_ref[a * grid + e, SIDES : SIDES + 1] = jnp.sum(sides[e], axis=0, keepdims=True)
            row = None
            for q in range(4):
                x = pltpu.roll(ends[q], (q - e) % grid * SIDE, 1) if q != e else ends[q]
                row = x if row is None else jnp.where(group == q, x, row)
            pack_ref[a * grid + e, ENDS : ENDS + 1] = row
    for o in range(owners):
        out_ref[o] = pack_ref[tile_ref[o]]
        for h in range(2):
            out_ref[o, GRAM + h : GRAM + h + 1] = halves[h]


def terms_of(base):
    u, v, vort, strain, stretch = base
    return [u, v, vort, strain, stretch, vort * vort, vort * strain, vort * stretch, strain * strain, stretch * stretch,
            strain * stretch, u * vort, v * vort, u * strain, v * stretch, u * v]


def library_kernel(x_ref, out_hbm, gram_ref, out_ref, sem):
    slots = x_ref.shape[0] // BLOCK_ROWS
    rows = lambda at: x_ref[pl.ds(at, slots, stride=BLOCK_ROWS), :]
    turn_by = lambda x, count: pltpu.roll(x, count % LANES, 1) if count % LANES else x
    lane = lax.broadcasted_iota(jnp.int32, (1, LANES), 1)
    sides, ends = rows(SIDES), rows(ENDS)
    fields = [[rows(8 * f + k) for k in range(8)] for f in range(2)]
    lower = [[turn_by(x, SIDE) for x in field] for field in fields]
    higher = [[turn_by(x, -SIDE) for x in field] for field in fields]

    def slopes(f, k):
        x = fields[f][k]
        left = jnp.where(lane % SIDE == 0, turn_by(sides, -(k + 16 * f)), turn_by(x, 1))
        right = jnp.where(lane % SIDE == SIDE - 1, turn_by(sides, SIDE - 1 - (k + 8 + 16 * f)), turn_by(x, -1))
        before = lower[f][k - 1] if k else turn_by(ends, -64 * f)
        after = higher[f][k + 1] if k < 7 else turn_by(ends, 64 - 64 * f)
        up = jnp.where(lane < SIDE, before, lower[f][k])
        down = jnp.where(lane >= LANES - SIDE, after, higher[f][k])
        return (right - left) * 0.5, (down - up) * 0.5

    copies = []
    for k in range(8):
        (u_dx, u_dy), (v_dx, v_dy) = slopes(0, k), slopes(1, k)
        base = [fields[0][k], fields[1][k], v_dx - u_dy, u_dy + v_dx, u_dx - v_dy]
        for n, x in enumerate(terms_of(base)):
            out_ref[k, pl.ds(n, slots, stride=TERMS), :] = x
        copies.append(pltpu.make_async_copy(out_ref.at[k], out_hbm.at[:, pl.ds(k * LANES, LANES)], sem.at[k]))
        copies[k].start()
    totals = [jnp.sum(rows(GRAM + half), axis=0, keepdims=True) for half in range(2)]
    for n in range(TERMS):
        row = totals[n // 8]
        row = pltpu.roll(row, LANES - n % 8 * TERMS, 1) if n % 8 else row
        for c in range(gram_ref.shape[0]):
            gram_ref[c, n : n + 1] = row
    for copy in copies:
        copy.wait()


VMEM = pl.BlockSpec(memory_space=pltpu.VMEM)
HBM = pl.BlockSpec(memory_space=pltpu.HBM)
SMEM = pl.BlockSpec(memory_space=pltpu.SMEM)
PARAMS = pltpu.CompilerParams(vmem_limit_bytes=24 << 20)


def struct(*shape):
    return jax.ShapeDtypeStruct(shape, F32)


def per_device(u_velocity, v_velocity, ocean_mask, tile_owner, lower_edge_quarter_turns):
    tiles, columns = lax.axis_size("tile"), lax.axis_size("col")
    onward = lambda count: [(i, (i + 1) % count) for i in range(count)]
    back = lambda count: [((i + 1) % count, i) for i in range(count)]
    here = lax.axis_index("tile").astype(jnp.int32)[None]
    in_hbm = lambda x: pltpu.with_memory_space_constraint(x, pltpu.HBM)
    up, down = pl.pallas_call(
        send_kernel,
        out_shape=[struct(2 * HALO, POOL * CELLS)] * 2,
        in_specs=[SMEM] + [HBM] * 3,
        out_specs=[VMEM] * 2,
        scratch_shapes=[pltpu.VMEM((2, 2, 16, POOL * CELLS), F32), pltpu.SMEM((tiles,), jnp.int32),
                        pltpu.SemaphoreType.DMA((2, 2)), pltpu.SemaphoreType.DMA],
        compiler_params=PARAMS,
        name="send_rows",
    )(here, *[in_hbm(x) for x in (lower_edge_quarter_turns, u_velocity, v_velocity)])
    up, down, u_velocity, v_velocity = lax.optimization_barrier((up, down, u_velocity, v_velocity))
    above = lax.ppermute(down, "tile", onward(tiles))
    below = lax.ppermute(up, "tile", back(tiles))
    column = lambda c: pl.BlockSpec((POOL * CELLS, LANES), lambda i: (0, c))
    rows = 2 * POOL * CELLS
    parts, weights, rim, early = pl.pallas_call(
        prepare_kernel,
        out_shape=[jax.ShapeDtypeStruct((rows, 2 * POOL * CELLS), BF16),
                   jax.ShapeDtypeStruct((POOL * CELLS, 10 * LANES), BF16), struct(FULL, LANES),
                   struct(rows, EARLY * LANES)],
        grid=(1,),
        in_specs=[column(c) for c in range(4)] * 2 + [HBM],
        out_specs=[VMEM] * 4,
        scratch_shapes=[pltpu.VMEM((rows, 2 * LANES), BF16)] + [pltpu.VMEM((POOL, PAD + CELLS, LANES), F32)] * 2
        + [pltpu.SemaphoreType.DMA],
        compiler_params=PARAMS,
        name="prepare_rows",
    )(*[u_velocity] * 4, *[v_velocity] * 4, in_hbm(jnp.asarray(column_weights())))
    to_left, to_right, own = pl.pallas_call(
        rim_kernel,
        out_shape=[struct(8, FULL), struct(8, FULL), struct(16, FULL)],
        in_specs=[VMEM] * 4,
        out_specs=[VMEM] * 3,
        scratch_shapes=[pltpu.VMEM((2, 2 * HALO, LANES), F32), pltpu.VMEM((2 * 2 * POOL * 8, LANES), F32),
                        pltpu.VMEM((FULL, LANES), F32)],
        compiler_params=PARAMS,
        name="rim_columns",
    )(above, below, weights, rim)
    from_right = lax.ppermute(to_left, "col", back(columns))
    from_left = lax.ppermute(to_right, "col", onward(columns))
    main, live, inner = pl.pallas_call(
        main_kernel,
        out_shape=[struct(2, FULL, LANES), struct(CELLS, LANES), struct(len(PAIRS), 8, LANES)],
        in_specs=[SMEM] + [VMEM] * 6,
        out_specs=[VMEM] * 3,
        scratch_shapes=[pltpu.VMEM((2, 4, 2 * HALO, LANES), F32), pltpu.VMEM((2 * POOL * 16, POOL * CELLS), F32),
                        pltpu.VMEM((2, POOL, FULL, LANES), F32), pltpu.VMEM((TERMS, CELLS, LANES), F32)],
        compiler_params=PARAMS,
        name="main_columns",
    )(ocean_mask, parts, early, weights, above, below, own)
    blocks = pl.pallas_call(
        base_kernel,
        out_shape=struct(tiles, BLOCK_ROWS, LANES),
        in_specs=[VMEM] * 9,
        out_specs=VMEM,
        scratch_shapes=[pltpu.VMEM((2, FULL, LANES), F32), pltpu.VMEM((TERMS * TERMS, LANES), F32),
                        pltpu.VMEM((17, BLOCK_ROWS, LANES), F32), pltpu.SMEM((tiles + 1,), jnp.int32),
                        pltpu.VMEM((2, 2, CELLS, LANES), F32), pltpu.SMEM(ocean_mask.shape, jnp.int32),
                        pltpu.SMEM(tile_owner.shape, jnp.int32), pltpu.SemaphoreType.DMA((2,))],
        compiler_params=PARAMS,
        name="base_fields",
    )(ocean_mask, tile_owner, main, live, inner, own, from_left, from_right, jnp.asarray(place_matrix()))
    blocks = lax.all_to_all(blocks, "tile", split_axis=0, concat_axis=0, tiled=True)
    library, gram = pl.pallas_call(
        library_kernel,
        out_shape=[struct(tiles * TERMS, SIDE * SIDE), struct(columns, TERMS, LANES)],
        in_specs=[VMEM],
        out_specs=[HBM, VMEM],
        scratch_shapes=[pltpu.VMEM((8, tiles * TERMS, LANES), F32), pltpu.SemaphoreType.DMA((8,))],
        compiler_params=PARAMS,
        name="library_terms",
    )(blocks.reshape(tiles * BLOCK_ROWS, LANES))
    gram = lax.all_to_all(gram, "col", split_axis=0, concat_axis=0, tiled=True)
    gram = jnp.sum(gram, axis=0)[:, :TERMS] / (CELLS * CELLS)
    return library.reshape(1, 1, tiles, TERMS, SIDE * SIDE), gram


def solution(mesh):
    in_specs = (P("tile", "col"), P("tile", "col"), P("tile", "col"), P("tile", "col"), P())
    out_specs = (P("tile", "col", None, None, None), P())
    return jax.shard_map(
        per_device, mesh=mesh, in_specs=in_specs, out_specs=out_specs, check_vma=False
    )
```

```python
import math

import jax
import jax.numpy as jnp
import ml_dtypes
import numpy as np
from jax import lax
from jax.experimental import pallas as pl
from jax.experimental.pallas import tpu as pltpu
from jax.sharding import PartitionSpec as P

PASSES = 8
KAPPA = 0.2
POOL = 4
CELLS = 128
HALO = 12
SIDE = 32
TERMS = 16
PAD = 8
FULL = CELLS + 2 * PAD
LANES = 128
BASES = 5
BLOCK_ROWS = 24
SIDES, ENDS, GRAM = 16, 17, 18
F32 = jnp.float32
BF16 = jnp.bfloat16

SCALE = KAPPA**PASSES / (POOL * POOL)
RIM_COLS = (-2, -1, 0, CELLS - 1, CELLS, CELLS + 1)


def across(power, fine, coarse):
    total = 0
    for inner in range(POOL):
        offset = fine - (POOL * coarse + inner)
        if abs(offset) <= power and (power + offset) % 2 == 0:
            total += math.comb(power, (power + offset) // 2)
    return total


def column_weights():
    fine = CELLS * POOL
    main = np.zeros((fine, 9 * LANES), np.float32)
    rim = np.zeros((fine, LANES), np.float32)
    for j in range(PASSES + 1):
        for coarse in range(-2, CELLS + 2):
            for f in range(max(0, POOL * coarse - PASSES), min(fine, POOL * coarse + POOL + PASSES)):
                value = math.comb(PASSES, j) * across(PASSES - j, f, coarse)
                if 0 <= coarse < CELLS:
                    main[f, (PASSES - j) * LANES + coarse] = value
                if coarse in RIM_COLS:
                    rim[f, 6 * j + RIM_COLS.index(coarse)] = value
    assert not rim[64 : fine - 64].any()
    rim[LANES - 64 : LANES] = rim[fine - 64 :]
    rim[LANES : 2 * LANES] = rim[:LANES]
    weights = np.concatenate([main, rim], axis=1)
    out = weights.astype(ml_dtypes.bfloat16)
    assert (out.astype(np.float32) == weights).all()
    return out


def rim_selector():
    row = lax.broadcasted_iota(jnp.int32, (32, 1), 0)
    source = jnp.full((32, 1), -1, jnp.int32)
    for f in range(2):
        for c in range(3):
            source = jnp.where(row == 3 * f + c, 64 * f + c, source)
            source = jnp.where(row == 8 + 3 * f + c, 64 * f + 3 + c, source)
        source = jnp.where(row == 16 + 2 * f, 64 * f + 1, source)
        source = jnp.where(row == 17 + 2 * f, 64 * f + 4, source)
    lane = lax.broadcasted_iota(jnp.int32, (32, 3 * LANES), 1) % LANES
    return jnp.where(lane == source, 1.0, 0.0).astype(BF16)


def place_matrix():
    place = np.zeros((3, 32, 4 * LANES), np.float32)
    for f in range(2):
        add, rim = 2 * f * LANES, (2 * f + 1) * LANES
        place[:, 3 * f + 0, rim + 0] = 1.0
        place[:, 3 * f + 1, add + 0] = 1.0
        place[:, 3 * f + 2, add + 1] = 1.0
        place[:, 8 + 3 * f + 0, add + CELLS - 2] = 1.0
        place[:, 8 + 3 * f + 1, add + CELLS - 1] = 1.0
        place[:, 8 + 3 * f + 2, rim + CELLS - 1] = 1.0
        place[:, 16 + 2 * f, rim + 0] = 1.0
        place[:, 17 + 2 * f, rim + CELLS - 1] = 1.0
    return place.reshape(96, 4 * LANES).astype(ml_dtypes.bfloat16)


def head(x):
    scaled = x * 65537.0
    return scaled - (scaled - x)


def two_parts(x):
    high = head(x)
    return high.astype(BF16), (x - high).astype(BF16)


def three_parts(x):
    high = head(x)
    rest = x - high
    mid = head(rest)
    return high.astype(BF16), mid.astype(BF16), (rest - mid).astype(BF16)


def dot(a, b, dims=(((1,), (0,)), ((), ()))):
    return lax.dot_general(a, b, dims, preferred_element_type=F32)


def three_rows(t):
    rows = t[0].shape[0]
    up = pltpu.roll(t[3], 1, 0)
    down = pltpu.roll(t[0], rows - 1, 0)
    left, middle, right = t[0] + t[1], t[1] + t[2], t[2] + t[3]
    return [left + up, t[0] + middle, middle + t[3], right + down]


def turn(first, second, k):
    cosine = jnp.where(k == 0, 1.0, jnp.where(k == 2, -1.0, 0.0)).astype(F32)
    sine = jnp.where(k == 1, 1.0, jnp.where(k == 3, -1.0, 0.0)).astype(F32)
    return cosine * first - sine * second, sine * first + cosine * second


def send_kernel(here_ref, turns_hbm, u_hbm, v_hbm, up_ref, down_ref, x_ref, turns_ref, sem, turns_sem):
    rows = u_hbm.shape[0]
    copies = [pltpu.make_async_copy(hbm.at[pl.ds(start, 16)], x_ref.at[side, f], sem.at[side, f])
              for side, start in enumerate((0, rows - 16)) for f, hbm in enumerate((u_hbm, v_hbm))]
    table = pltpu.make_async_copy(turns_hbm, turns_ref, turns_sem)
    table.start()
    for copy in copies:
        copy.start()
    table.wait()
    tiles = turns_ref.shape[0]
    here = here_ref[0]
    k_up = lax.rem(4 - turns_ref[here], 4)
    k_down = turns_ref[lax.rem(here + 1, tiles)]
    for copy in copies:
        copy.wait()
    for side, (to_ref, k, start) in enumerate(((up_ref, k_up, 0), (down_ref, k_down, 16 - HALO))):
        for f, x in enumerate(turn(x_ref[side, 0], x_ref[side, 1], k)):
            to_ref[f * HALO : (f + 1) * HALO] = x[start : start + HALO]


EARLY = 6


def prepare_kernel(*refs):
    w_hbm, parts_ref, w_out, rim_ref, early_ref, rim_parts_ref, first_ref, last_ref, sem = refs[8:]
    copy = pltpu.make_async_copy(w_hbm, w_out, sem)
    copy.start()
    lane = lax.broadcasted_iota(jnp.int32, (1, LANES), 1)
    fine = POOL * CELLS
    for f in range(2):
        for p in range(POOL):
            spot = slice((f * POOL + p) * CELLS, (f * POOL + p + 1) * CELLS)
            pieces = [two_parts(refs[4 * f + c][pl.ds(p, CELLS, stride=POOL), :]) for c in range(4)]
            for part in range(2):
                for c in range(4):
                    parts_ref[spot, part * fine + c * LANES : part * fine + (c + 1) * LANES] = pieces[c][part]
                rim_parts_ref[spot, part * LANES : (part + 1) * LANES] = jnp.where(
                    lane < 64, pieces[0][part], pieces[3][part])
    copy.wait()
    z = dot(rim_parts_ref[...], w_out[: 2 * LANES, 9 * LANES :])
    for p in range(POOL):
        u, v = [z[(f * POOL + p) * CELLS : (f * POOL + p + 1) * CELLS] for f in range(2)]
        both = jnp.where(lane < 64, u, pltpu.roll(v, 64, 1))
        for to_ref in (first_ref, last_ref):
            to_ref[p, :PAD] = jnp.zeros((PAD, LANES), F32)
            to_ref[p, PAD:] = both
    for _ in range(PASSES):
        new = three_rows([pltpu.roll(last_ref[p], LANES - 6, 1) for p in range(POOL)])
        for p in range(POOL):
            last_ref[p] = new[p] + first_ref[p]
    pooled = ((last_ref[0] + last_ref[1]) + (last_ref[2] + last_ref[3])) * SCALE
    rim_ref[: PAD + CELLS] = pooled
    rim_ref[PAD + CELLS :] = pooled[:PAD]
    for start in range(0, EARLY, 2):
        cut = slice(start * LANES, (start + 2) * LANES)
        early_ref[:, cut] = dot(parts_ref[:, :fine], w_out[:, cut]) + dot(parts_ref[:, fine:], w_out[:, cut])


def rim_kernel(above_ref, below_ref, w_ref, rim_in, left_ref, right_ref, own_ref, rows_ref, strip_ref, rim_ref):
    lane = lax.broadcasted_iota(jnp.int32, (1, LANES), 1)
    strip_ref[...] = jnp.zeros_like(strip_ref)
    for s, (x_ref, start) in enumerate(((above_ref, 1), (below_ref, 4))):
        ends = jnp.where(lane < 64, x_ref[:, :LANES], x_ref[:, 3 * LANES :])
        rows_ref[s] = ends
        for f in range(2):
            for p in range(POOL):
                spot = ((f * 2 + s) * POOL + p) * 8 + start
                strip_ref[spot : spot + 3] = rows_ref[s, pl.ds(f * HALO + p, 3, stride=POOL), :]
    z = dot(jnp.concatenate(two_parts(strip_ref[...]), axis=1), w_ref[: 2 * LANES, 9 * LANES :])
    rim_ref[...] = rim_in[...]
    for s, (spot, start) in enumerate(((7, 3), (PAD + CELLS - 2, 2))):
        first = []
        for p in range(POOL):
            u, v = [z[((f * 2 + s) * POOL + p) * 8 : ((f * 2 + s) * POOL + p + 1) * 8] for f in range(2)]
            first.append(jnp.where(lane < 64, u, pltpu.roll(v, 64, 1)))
        last = first
        for _ in range(PASSES):
            last = [a + b for a, b in zip(three_rows([pltpu.roll(x, LANES - 6, 1) for x in last]), first)]
        pooled = ((last[0] + last[1]) + (last[2] + last[3])) * SCALE
        rim_ref[spot : spot + 3] = rim_ref[spot : spot + 3] + pooled[start : start + 3]
    turned = jnp.transpose(rim_ref[...])
    for to_ref, columns in ((left_ref, (0, 1, 2)), (right_ref, (3, 4, 5)), (own_ref, (1, 4))):
        to_ref[...] = jnp.zeros_like(to_ref)
        for f in range(2):
            for place, c in enumerate(columns):
                spot = len(columns) * f + place
                to_ref[spot : spot + 1] = turned[64 * f + c : 64 * f + c + 1]


PAIRS = [(n, m) for n in range(TERMS) for m in range(n, TERMS)]
REACH = 3


def slopes_of(ref, f, left, right):
    up = ref[f, PAD - 1 : PAD - 1 + CELLS]
    down = ref[f, PAD + 1 : PAD + 1 + CELLS]
    return (right - left) * 0.5, (down - up) * 0.5


def main_kernel(mask_ref, parts_ref, early_ref, w_ref, above_ref, below_ref, _, main_ref, live_ref, inner_ref, rows_ref,
                strip_ref, sum_ref, term_ref):
    strip_ref[...] = jnp.zeros_like(strip_ref)
    for s, (x_ref, start) in enumerate(((above_ref, 5), (below_ref, 8))):
        for c in range(4):
            cut = slice(c * LANES, (c + 1) * LANES)
            rows_ref[s, c] = x_ref[:, cut]
            for f in range(2):
                for p in range(POOL):
                    spot = (f * POOL + p) * 16 + start
                    strip_ref[spot : spot + 3, cut] = rows_ref[s, c, pl.ds(f * HALO + p, 3, stride=POOL), :]
    strips = jnp.concatenate(two_parts(strip_ref[...]), axis=1)
    fine = POOL * CELLS
    for start in range(0, 9, 2):
        wide = min(2, 9 - start)
        w = w_ref[:, start * LANES : (start + wide) * LANES]
        if start < EARLY:
            z = early_ref[:, start * LANES : (start + wide) * LANES]
        else:
            z = dot(parts_ref[:, :fine], w) + dot(parts_ref[:, fine:], w)
        z_strip = dot(strips[:, :fine], w) + dot(strips[:, fine:], w)
        for stage in range(start, start + wide):
            cut = slice((stage - start) * LANES, (stage - start + 1) * LANES)
            for f in range(2):
                own = []
                for p in range(POOL):
                    block = f * POOL + p
                    own.append(jnp.concatenate([
                        z_strip[block * 16 : block * 16 + 8, cut], z[block * CELLS : (block + 1) * CELLS, cut],
                        z_strip[block * 16 + 8 : block * 16 + 16, cut]], axis=0))
                if stage:
                    own = [a + b for a, b in zip(three_rows([sum_ref[f, p] for p in range(POOL)]), own)]
                for p in range(POOL):
                    sum_ref[f, p] = own[p]
    for f in range(2):
        main_ref[f] = ((sum_ref[f, 0] + sum_ref[f, 1]) + (sum_ref[f, 2] + sum_ref[f, 3])) * SCALE
    lane = lax.broadcasted_iota(jnp.int32, (1, LANES), 1)
    grid = CELLS // SIDE
    for a in range(grid):
        row = jnp.zeros((1, LANES), F32)
        for e in range(grid):
            row = jnp.where(lane // SIDE == e, (mask_ref[a, e] == 1).astype(F32), row)
        live_ref[a * SIDE : (a + 1) * SIDE] = jnp.broadcast_to(row, (SIDE, LANES))
    keep = (live_ref[...] > 0.5) & (lane >= REACH) & (lane < LANES - REACH)
    u, v = [main_ref[f, PAD : PAD + CELLS] for f in range(2)]
    (u_dx, u_dy), (v_dx, v_dy) = [slopes_of(main_ref, f, pltpu.roll(x, 1, 1), pltpu.roll(x, LANES - 1, 1))
                                  for f, x in enumerate((u, v))]
    for n, x in enumerate((u, v, v_dx - u_dy, u_dy + v_dx, u_dx - v_dy)):
        term_ref[n] = jnp.where(keep, x, 0.0)
    for n, x in enumerate(terms_of([term_ref[n] for n in range(BASES)])):
        if n >= BASES:
            term_ref[n] = x
    for place, (n, m) in enumerate(PAIRS):
        product = (term_ref[n] * term_ref[m]).reshape(CELLS // 8, 8, LANES)
        inner_ref[place] = jnp.sum(product, axis=0)


def base_kernel(mask_vmem, owner_vmem, main_ref, live_ref, inner_ref, own_ref, from_left_ref, from_right_ref, place_ref,
                out_ref, field_ref, gram_ref, pack_ref, tile_ref, side_ref, mask_ref, owner_ref, sem):
    tables = [pltpu.make_async_copy(mask_vmem, mask_ref, sem.at[0]),
              pltpu.make_async_copy(owner_vmem, owner_ref, sem.at[1])]
    for table in tables:
        table.start()
    lane = lax.broadcasted_iota(jnp.int32, (1, LANES), 1)
    received = jnp.concatenate([from_left_ref[...], from_right_ref[...], own_ref[...]], axis=0)
    placed = dot(jnp.concatenate(three_parts(received), axis=0), place_ref[...], (((0,), (0,)), ((), ())))
    inner = slice(PAD, PAD + CELLS)
    slopes = []
    for f in range(2):
        full = main_ref[f] + placed[:, 2 * f * LANES : (2 * f + 1) * LANES]
        field_ref[f] = full
        rim = placed[inner, (2 * f + 1) * LANES : (2 * f + 2) * LANES]
        centre = full[inner]
        left = jnp.where(lane == 0, rim, pltpu.roll(centre, 1, 1))
        right = jnp.where(lane == LANES - 1, rim, pltpu.roll(centre, LANES - 1, 1))
        side_ref[f, 0] = left
        side_ref[f, 1] = right
        slopes.append((centre, *slopes_of(field_ref, f, left, right)))
    (u, u_dx, u_dy), (v, v_dx, v_dy) = slopes
    live = live_ref[...] > 0.5
    outer = []
    for x in (u, v, v_dx - u_dy, u_dy + v_dx, u_dx - v_dy):
        x = jnp.where(live, x, 0.0)
        tile = jnp.zeros((8, LANES), F32)
        for b in range(CELLS // 8):
            tile = jnp.where(lane // 8 == b, pltpu.roll(x[8 * b : 8 * b + 8], (REACH + 8 * b) % LANES, 1), tile)
        outer.append(jnp.where(lane % 8 < 2 * REACH, tile, 0.0))
    outer = terms_of(outer)
    for place, (n, m) in enumerate(PAIRS):
        total = jnp.sum(inner_ref[place] + outer[n] * outer[m], axis=0, keepdims=True)
        gram_ref[n * TERMS + m : n * TERMS + m + 1] = total
        if m > n:
            gram_ref[m * TERMS + n : m * TERMS + n + 1] = total
    totals = jnp.sum(gram_ref[...], axis=1, keepdims=True)
    row = lax.broadcasted_iota(jnp.int32, (TERMS * TERMS, 1), 0)
    spread = jnp.where(row % LANES == lane, totals, 0.0)
    halves = [jnp.sum(spread[h * LANES : (h + 1) * LANES], axis=0, keepdims=True) for h in range(2)]
    owners = out_ref.shape[0]
    grid = CELLS // SIDE
    nothing = grid * grid
    for table in tables:
        table.wait()
    for o in range(owners + 1):
        tile_ref[o] = nothing
    for a in range(grid):
        for e in range(grid):
            tile_ref[jnp.where(mask_ref[a, e] == 1, owner_ref[a, e], owners)] = a * grid + e
    pack_ref[nothing] = jnp.zeros((BLOCK_ROWS, LANES), F32)
    group = lane // SIDE
    rows_of = lax.broadcasted_iota(jnp.int32, (8, LANES), 0)
    for a in range(grid):
        sides = [jnp.zeros((8, LANES), F32)] * grid
        ends = []
        for f in range(2):
            pieces = [field_ref[f, pl.ds(PAD + a * SIDE + q, 8, stride=4), :] for q in range(grid)]
            for e in range(grid):
                block = None
                for q in range(grid):
                    x = pltpu.roll(pieces[q], (q - e) % grid * SIDE, 1) if q != e else pieces[q]
                    block = x if block is None else jnp.where(group == q, x, block)
                pack_ref[a * grid + e, 8 * f : 8 * f + 8] = block
            for side in range(2):
                ends.append(field_ref[f, PAD + a * SIDE - 1 + side * (SIDE + 1) : PAD + a * SIDE + side * (SIDE + 1)])
                for q in range(grid):
                    x = side_ref[f, side, pl.ds(a * SIDE + q, 8, stride=4), :]
                    here = lane == rows_of + (q * SIDE + 8 * side + 16 * f)
                    for e in range(grid):
                        at = e * SIDE + side * (SIDE - 1)
                        sides[e] = jnp.where(here, x[:, at : at + 1], sides[e])
        for e in range(grid):
            pack_ref[a * grid + e, SIDES : SIDES + 1] = jnp.sum(sides[e], axis=0, keepdims=True)
            row = None
            for q in range(4):
                x = pltpu.roll(ends[q], (q - e) % grid * SIDE, 1) if q != e else ends[q]
                row = x if row is None else jnp.where(group == q, x, row)
            pack_ref[a * grid + e, ENDS : ENDS + 1] = row
    for o in range(owners):
        out_ref[o] = pack_ref[tile_ref[o]]
        for h in range(2):
            out_ref[o, GRAM + h : GRAM + h + 1] = halves[h]


def terms_of(base):
    u, v, vort, strain, stretch = base
    return [u, v, vort, strain, stretch, vort * vort, vort * strain, vort * stretch, strain * strain, stretch * stretch,
            strain * stretch, u * vort, v * vort, u * strain, v * stretch, u * v]


def library_kernel(x_ref, out_hbm, out_ref, sem):
    slots = x_ref.shape[0] // BLOCK_ROWS
    rows = lambda at: x_ref[pl.ds(at, slots, stride=BLOCK_ROWS), :]
    turn_by = lambda x, count: pltpu.roll(x, count % LANES, 1) if count % LANES else x
    lane = lax.broadcasted_iota(jnp.int32, (1, LANES), 1)
    sides, ends = rows(SIDES), rows(ENDS)
    fields = [[rows(8 * f + k) for k in range(8)] for f in range(2)]
    lower = [[turn_by(x, SIDE) for x in field] for field in fields]
    higher = [[turn_by(x, -SIDE) for x in field] for field in fields]

    def slopes(f, k):
        x = fields[f][k]
        left = jnp.where(lane % SIDE == 0, turn_by(sides, -(k + 16 * f)), turn_by(x, 1))
        right = jnp.where(lane % SIDE == SIDE - 1, turn_by(sides, SIDE - 1 - (k + 8 + 16 * f)), turn_by(x, -1))
        before = lower[f][k - 1] if k else turn_by(ends, -64 * f)
        after = higher[f][k + 1] if k < 7 else turn_by(ends, 64 - 64 * f)
        up = jnp.where(lane < SIDE, before, lower[f][k])
        down = jnp.where(lane >= LANES - SIDE, after, higher[f][k])
        return (right - left) * 0.5, (down - up) * 0.5

    copies = []
    for k in range(8):
        (u_dx, u_dy), (v_dx, v_dy) = slopes(0, k), slopes(1, k)
        base = [fields[0][k], fields[1][k], v_dx - u_dy, u_dy + v_dx, u_dx - v_dy]
        for n, x in enumerate(terms_of(base)):
            out_ref[k, pl.ds(n, slots, stride=TERMS), :] = x
        copies.append(pltpu.make_async_copy(out_ref.at[k], out_hbm.at[:, pl.ds(k * LANES, LANES)], sem.at[k]))
        copies[k].start()
    for copy in copies:
        copy.wait()


VMEM = pl.BlockSpec(memory_space=pltpu.VMEM)
HBM = pl.BlockSpec(memory_space=pltpu.HBM)
SMEM = pl.BlockSpec(memory_space=pltpu.SMEM)
PARAMS = pltpu.CompilerParams(vmem_limit_bytes=24 << 20)


def struct(*shape):
    return jax.ShapeDtypeStruct(shape, F32)


def per_device(u_velocity, v_velocity, ocean_mask, tile_owner, lower_edge_quarter_turns):
    tiles, columns = lax.axis_size("tile"), lax.axis_size("col")
    onward = lambda count: [(i, (i + 1) % count) for i in range(count)]
    back = lambda count: [((i + 1) % count, i) for i in range(count)]
    here = lax.axis_index("tile").astype(jnp.int32)[None]
    in_hbm = lambda x: pltpu.with_memory_space_constraint(x, pltpu.HBM)
    up, down = pl.pallas_call(
        send_kernel,
        out_shape=[struct(2 * HALO, POOL * CELLS)] * 2,
        in_specs=[SMEM] + [HBM] * 3,
        out_specs=[VMEM] * 2,
        scratch_shapes=[pltpu.VMEM((2, 2, 16, POOL * CELLS), F32), pltpu.SMEM((tiles,), jnp.int32),
                        pltpu.SemaphoreType.DMA((2, 2)), pltpu.SemaphoreType.DMA],
        compiler_params=PARAMS,
        name="send_rows",
    )(here, *[in_hbm(x) for x in (lower_edge_quarter_turns, u_velocity, v_velocity)])
    up, down, u_velocity, v_velocity = lax.optimization_barrier((up, down, u_velocity, v_velocity))
    above = lax.ppermute(down, "tile", onward(tiles))
    below = lax.ppermute(up, "tile", back(tiles))
    column = lambda c: pl.BlockSpec((POOL * CELLS, LANES), lambda i: (0, c))
    rows = 2 * POOL * CELLS
    parts, weights, rim, early = pl.pallas_call(
        prepare_kernel,
        out_shape=[jax.ShapeDtypeStruct((rows, 2 * POOL * CELLS), BF16),
                   jax.ShapeDtypeStruct((POOL * CELLS, 10 * LANES), BF16), struct(FULL, LANES),
                   struct(rows, EARLY * LANES)],
        grid=(1,),
        in_specs=[column(c) for c in range(4)] * 2 + [HBM],
        out_specs=[VMEM] * 4,
        scratch_shapes=[pltpu.VMEM((rows, 2 * LANES), BF16)] + [pltpu.VMEM((POOL, PAD + CELLS, LANES), F32)] * 2
        + [pltpu.SemaphoreType.DMA],
        compiler_params=PARAMS,
        name="prepare_rows",
    )(*[u_velocity] * 4, *[v_velocity] * 4, in_hbm(jnp.asarray(column_weights())))
    to_left, to_right, own = pl.pallas_call(
        rim_kernel,
        out_shape=[struct(8, FULL), struct(8, FULL), struct(16, FULL)],
        in_specs=[VMEM] * 4,
        out_specs=[VMEM] * 3,
        scratch_shapes=[pltpu.VMEM((2, 2 * HALO, LANES), F32), pltpu.VMEM((2 * 2 * POOL * 8, LANES), F32),
                        pltpu.VMEM((FULL, LANES), F32)],
        compiler_params=PARAMS,
        name="rim_columns",
    )(above, below, weights, rim)
    from_right = lax.ppermute(to_left, "col", back(columns))
    from_left = lax.ppermute(to_right, "col", onward(columns))
    main, live, inner = pl.pallas_call(
        main_kernel,
        out_shape=[struct(2, FULL, LANES), struct(CELLS, LANES), struct(len(PAIRS), 8, LANES)],
        in_specs=[SMEM] + [VMEM] * 6,
        out_specs=[VMEM] * 3,
        scratch_shapes=[pltpu.VMEM((2, 4, 2 * HALO, LANES), F32), pltpu.VMEM((2 * POOL * 16, POOL * CELLS), F32),
                        pltpu.VMEM((2, POOL, FULL, LANES), F32), pltpu.VMEM((TERMS, CELLS, LANES), F32)],
        compiler_params=PARAMS,
        name="main_columns",
    )(ocean_mask, parts, early, weights, above, below, own)
    blocks = pl.pallas_call(
        base_kernel,
        out_shape=struct(tiles, BLOCK_ROWS, LANES),
        in_specs=[VMEM] * 9,
        out_specs=VMEM,
        scratch_shapes=[pltpu.VMEM((2, FULL, LANES), F32), pltpu.VMEM((TERMS * TERMS, LANES), F32),
                        pltpu.VMEM((17, BLOCK_ROWS, LANES), F32), pltpu.SMEM((tiles + 1,), jnp.int32),
                        pltpu.VMEM((2, 2, CELLS, LANES), F32), pltpu.SMEM(ocean_mask.shape, jnp.int32),
                        pltpu.SMEM(tile_owner.shape, jnp.int32), pltpu.SemaphoreType.DMA((2,))],
        compiler_params=PARAMS,
        name="base_fields",
    )(ocean_mask, tile_owner, main, live, inner, own, from_left, from_right, jnp.asarray(place_matrix()))
    blocks = lax.all_to_all(blocks, "tile", split_axis=0, concat_axis=0, tiled=True)
    gram = jnp.sum(blocks[:, GRAM : GRAM + 2], axis=0)
    gram = lax.all_to_all(jnp.broadcast_to(gram, (columns, 2, LANES)), "col", split_axis=0, concat_axis=0, tiled=True)
    library = pl.pallas_call(
        library_kernel,
        out_shape=struct(tiles * TERMS, SIDE * SIDE),
        in_specs=[VMEM],
        out_specs=HBM,
        scratch_shapes=[pltpu.VMEM((8, tiles * TERMS, LANES), F32), pltpu.SemaphoreType.DMA((8,))],
        compiler_params=PARAMS,
        cost_estimate=pl.CostEstimate(flops=2 * tiles * TERMS * SIDE * SIDE, transcendentals=0,
                                      bytes_accessed=5 * tiles * TERMS * SIDE * SIDE),
        name="library_terms",
    )(blocks.reshape(tiles * BLOCK_ROWS, LANES))
    gram = jnp.sum(gram, axis=0).reshape(TERMS, TERMS) / (CELLS * CELLS)
    return library.reshape(1, 1, tiles, TERMS, SIDE * SIDE), gram


def solution(mesh):
    in_specs = (P("tile", "col"), P("tile", "col"), P("tile", "col"), P("tile", "col"), P())
    out_specs = (P("tile", "col", None, None, None), P())
    return jax.shard_map(
        per_device, mesh=mesh, in_specs=in_specs, out_specs=out_specs, check_vma=False
    )
```

```python
import math

import jax
import jax.numpy as jnp
import ml_dtypes
import numpy as np
from jax import lax
from jax.experimental import pallas as pl
from jax.experimental.pallas import tpu as pltpu
from jax.sharding import PartitionSpec as P

PASSES = 8
KAPPA = 0.2
POOL = 4
CELLS = 128
HALO = 12
SIDE = 32
TERMS = 16
PAD = 8
FULL = CELLS + 2 * PAD
LANES = 128
BASES = 5
BLOCK_ROWS = 24
SIDES, ENDS, GRAM = 16, 17, 18
F32 = jnp.float32
BF16 = jnp.bfloat16

SCALE = KAPPA**PASSES / (POOL * POOL)
RIM_COLS = (-2, -1, 0, CELLS - 1, CELLS, CELLS + 1)


def across(power, fine, coarse):
    total = 0
    for inner in range(POOL):
        offset = fine - (POOL * coarse + inner)
        if abs(offset) <= power and (power + offset) % 2 == 0:
            total += math.comb(power, (power + offset) // 2)
    return total


def column_weights():
    fine = CELLS * POOL
    main = np.zeros((fine, 9 * LANES), np.float32)
    rim = np.zeros((fine, LANES), np.float32)
    for j in range(PASSES + 1):
        for coarse in range(-2, CELLS + 2):
            for f in range(max(0, POOL * coarse - PASSES), min(fine, POOL * coarse + POOL + PASSES)):
                value = math.comb(PASSES, j) * across(PASSES - j, f, coarse)
                if 0 <= coarse < CELLS:
                    main[f, (PASSES - j) * LANES + coarse] = value
                if coarse in RIM_COLS:
                    rim[f, 6 * j + RIM_COLS.index(coarse)] = value
    assert not rim[64 : fine - 64].any()
    rim[LANES - 64 : LANES] = rim[fine - 64 :]
    rim[LANES : 2 * LANES] = rim[:LANES]
    weights = np.concatenate([main, rim], axis=1)
    out = weights.astype(ml_dtypes.bfloat16)
    assert (out.astype(np.float32) == weights).all()
    return out


def rim_selector():
    row = lax.broadcasted_iota(jnp.int32, (32, 1), 0)
    source = jnp.full((32, 1), -1, jnp.int32)
    for f in range(2):
        for c in range(3):
            source = jnp.where(row == 3 * f + c, 64 * f + c, source)
            source = jnp.where(row == 8 + 3 * f + c, 64 * f + 3 + c, source)
        source = jnp.where(row == 16 + 2 * f, 64 * f + 1, source)
        source = jnp.where(row == 17 + 2 * f, 64 * f + 4, source)
    lane = lax.broadcasted_iota(jnp.int32, (32, 3 * LANES), 1) % LANES
    return jnp.where(lane == source, 1.0, 0.0).astype(BF16)


def place_matrix():
    place = np.zeros((3, 32, 4 * LANES), np.float32)
    for f in range(2):
        add, rim = 2 * f * LANES, (2 * f + 1) * LANES
        place[:, 3 * f + 0, rim + 0] = 1.0
        place[:, 3 * f + 1, add + 0] = 1.0
        place[:, 3 * f + 2, add + 1] = 1.0
        place[:, 8 + 3 * f + 0, add + CELLS - 2] = 1.0
        place[:, 8 + 3 * f + 1, add + CELLS - 1] = 1.0
        place[:, 8 + 3 * f + 2, rim + CELLS - 1] = 1.0
        place[:, 16 + 2 * f, rim + 0] = 1.0
        place[:, 17 + 2 * f, rim + CELLS - 1] = 1.0
    return place.reshape(96, 4 * LANES).astype(ml_dtypes.bfloat16)


def head(x):
    scaled = x * 65537.0
    return scaled - (scaled - x)


def two_parts(x):
    high = head(x)
    return high.astype(BF16), (x - high).astype(BF16)


def three_parts(x):
    high = head(x)
    rest = x - high
    mid = head(rest)
    return high.astype(BF16), mid.astype(BF16), (rest - mid).astype(BF16)


def dot(a, b, dims=(((1,), (0,)), ((), ()))):
    return lax.dot_general(a, b, dims, preferred_element_type=F32)


def three_rows(t):
    rows = t[0].shape[0]
    up = pltpu.roll(t[3], 1, 0)
    down = pltpu.roll(t[0], rows - 1, 0)
    left, middle, right = t[0] + t[1], t[1] + t[2], t[2] + t[3]
    return [left + up, t[0] + middle, middle + t[3], right + down]


def turn(first, second, k):
    cosine = jnp.where(k == 0, 1.0, jnp.where(k == 2, -1.0, 0.0)).astype(F32)
    sine = jnp.where(k == 1, 1.0, jnp.where(k == 3, -1.0, 0.0)).astype(F32)
    return cosine * first - sine * second, sine * first + cosine * second


def send_kernel(here_ref, turns_hbm, u_hbm, v_hbm, up_ref, down_ref, x_ref, turns_ref, sem, turns_sem):
    rows = u_hbm.shape[0]
    copies = [pltpu.make_async_copy(hbm.at[pl.ds(start, 16)], x_ref.at[side, f], sem.at[side, f])
              for side, start in enumerate((0, rows - 16)) for f, hbm in enumerate((u_hbm, v_hbm))]
    table = pltpu.make_async_copy(turns_hbm, turns_ref, turns_sem)
    table.start()
    for copy in copies:
        copy.start()
    table.wait()
    tiles = turns_ref.shape[0]
    here = here_ref[0]
    k_up = lax.rem(4 - turns_ref[here], 4)
    k_down = turns_ref[lax.rem(here + 1, tiles)]
    for copy in copies:
        copy.wait()
    for side, (to_ref, k, start) in enumerate(((up_ref, k_up, 0), (down_ref, k_down, 16 - HALO))):
        for f, x in enumerate(turn(x_ref[side, 0], x_ref[side, 1], k)):
            to_ref[f * HALO : (f + 1) * HALO] = x[start : start + HALO]


EARLY = 6


def prepare_kernel(*refs):
    w_hbm, parts_ref, w_out, rim_ref, early_ref, rim_parts_ref, first_ref, last_ref, sem = refs[8:]
    copy = pltpu.make_async_copy(w_hbm, w_out, sem)
    copy.start()
    lane = lax.broadcasted_iota(jnp.int32, (1, LANES), 1)
    fine = POOL * CELLS
    for f in range(2):
        for p in range(POOL):
            spot = slice((f * POOL + p) * CELLS, (f * POOL + p + 1) * CELLS)
            pieces = [two_parts(refs[4 * f + c][pl.ds(p, CELLS, stride=POOL), :]) for c in range(4)]
            for part in range(2):
                for c in range(4):
                    parts_ref[spot, part * fine + c * LANES : part * fine + (c + 1) * LANES] = pieces[c][part]
                rim_parts_ref[spot, part * LANES : (part + 1) * LANES] = jnp.where(
                    lane < 64, pieces[0][part], pieces[3][part])
    copy.wait()
    z = dot(rim_parts_ref[...], w_out[: 2 * LANES, 9 * LANES :])
    for p in range(POOL):
        u, v = [z[(f * POOL + p) * CELLS : (f * POOL + p + 1) * CELLS] for f in range(2)]
        both = jnp.where(lane < 64, u, pltpu.roll(v, 64, 1))
        for to_ref in (first_ref, last_ref):
            to_ref[p, :PAD] = jnp.zeros((PAD, LANES), F32)
            to_ref[p, PAD:] = both
    for _ in range(PASSES):
        new = three_rows([pltpu.roll(last_ref[p], LANES - 6, 1) for p in range(POOL)])
        for p in range(POOL):
            last_ref[p] = new[p] + first_ref[p]
    pooled = ((last_ref[0] + last_ref[1]) + (last_ref[2] + last_ref[3])) * SCALE
    rim_ref[: PAD + CELLS] = pooled
    rim_ref[PAD + CELLS :] = pooled[:PAD]
    for start in range(0, EARLY, 2):
        cut = slice(start * LANES, (start + 2) * LANES)
        early_ref[:, cut] = dot(parts_ref[:, :fine], w_out[:, cut]) + dot(parts_ref[:, fine:], w_out[:, cut])


def rim_kernel(above_ref, below_ref, w_ref, rim_in, left_ref, right_ref, own_ref, rows_ref, strip_ref, rim_ref):
    lane = lax.broadcasted_iota(jnp.int32, (1, LANES), 1)
    strip_ref[...] = jnp.zeros_like(strip_ref)
    for s, (x_ref, start) in enumerate(((above_ref, 1), (below_ref, 4))):
        ends = jnp.where(lane < 64, x_ref[:, :LANES], x_ref[:, 3 * LANES :])
        rows_ref[s] = ends
        for f in range(2):
            for p in range(POOL):
                spot = ((f * 2 + s) * POOL + p) * 8 + start
                strip_ref[spot : spot + 3] = rows_ref[s, pl.ds(f * HALO + p, 3, stride=POOL), :]
    z = dot(jnp.concatenate(two_parts(strip_ref[...]), axis=1), w_ref[: 2 * LANES, 9 * LANES :])
    rim_ref[...] = rim_in[...]
    for s, (spot, start) in enumerate(((7, 3), (PAD + CELLS - 2, 2))):
        first = []
        for p in range(POOL):
            u, v = [z[((f * 2 + s) * POOL + p) * 8 : ((f * 2 + s) * POOL + p + 1) * 8] for f in range(2)]
            first.append(jnp.where(lane < 64, u, pltpu.roll(v, 64, 1)))
        powers = [first] + [[pltpu.roll(x, LANES - 6 * j, 1) for x in first] for j in range(1, PASSES + 1)]
        last = powers[PASSES]
        for j in range(PASSES - 1, -1, -1):
            last = [a + b for a, b in zip(three_rows(last), powers[j])]
        pooled = ((last[0] + last[1]) + (last[2] + last[3])) * SCALE
        rim_ref[spot : spot + 3] = rim_ref[spot : spot + 3] + pooled[start : start + 3]
    turned = jnp.transpose(rim_ref[...])
    for to_ref, columns in ((left_ref, (0, 1, 2)), (right_ref, (3, 4, 5)), (own_ref, (1, 4))):
        to_ref[...] = jnp.zeros_like(to_ref)
        for f in range(2):
            for place, c in enumerate(columns):
                spot = len(columns) * f + place
                to_ref[spot : spot + 1] = turned[64 * f + c : 64 * f + c + 1]


PAIRS = [(n, m) for n in range(TERMS) for m in range(n, TERMS)]
REACH = 3


def slopes_of(ref, f, left, right):
    up = ref[f, PAD - 1 : PAD - 1 + CELLS]
    down = ref[f, PAD + 1 : PAD + 1 + CELLS]
    return (right - left) * 0.5, (down - up) * 0.5


def main_kernel(mask_ref, parts_ref, early_ref, w_ref, above_ref, below_ref, _, main_ref, live_ref, inner_ref, rows_ref,
                strip_ref, sum_ref, term_ref):
    strip_ref[...] = jnp.zeros_like(strip_ref)
    for s, (x_ref, start) in enumerate(((above_ref, 5), (below_ref, 8))):
        for c in range(4):
            cut = slice(c * LANES, (c + 1) * LANES)
            rows_ref[s, c] = x_ref[:, cut]
            for f in range(2):
                for p in range(POOL):
                    spot = (f * POOL + p) * 16 + start
                    strip_ref[spot : spot + 3, cut] = rows_ref[s, c, pl.ds(f * HALO + p, 3, stride=POOL), :]
    strips = jnp.concatenate(two_parts(strip_ref[...]), axis=1)
    fine = POOL * CELLS
    for start in range(0, 9, 2):
        wide = min(2, 9 - start)
        w = w_ref[:, start * LANES : (start + wide) * LANES]
        if start < EARLY:
            z = early_ref[:, start * LANES : (start + wide) * LANES]
        else:
            z = dot(parts_ref[:, :fine], w) + dot(parts_ref[:, fine:], w)
        z_strip = dot(strips[:, :fine], w) + dot(strips[:, fine:], w)
        for stage in range(start, start + wide):
            cut = slice((stage - start) * LANES, (stage - start + 1) * LANES)
            for f in range(2):
                own = []
                for p in range(POOL):
                    block = f * POOL + p
                    own.append(jnp.concatenate([
                        z_strip[block * 16 : block * 16 + 8, cut], z[block * CELLS : (block + 1) * CELLS, cut],
                        z_strip[block * 16 + 8 : block * 16 + 16, cut]], axis=0))
                if stage:
                    own = [a + b for a, b in zip(three_rows([sum_ref[f, p] for p in range(POOL)]), own)]
                for p in range(POOL):
                    sum_ref[f, p] = own[p]
    for f in range(2):
        main_ref[f] = ((sum_ref[f, 0] + sum_ref[f, 1]) + (sum_ref[f, 2] + sum_ref[f, 3])) * SCALE
    lane = lax.broadcasted_iota(jnp.int32, (1, LANES), 1)
    grid = CELLS // SIDE
    for a in range(grid):
        row = jnp.zeros((1, LANES), F32)
        for e in range(grid):
            row = jnp.where(lane // SIDE == e, (mask_ref[a, e] == 1).astype(F32), row)
        live_ref[a * SIDE : (a + 1) * SIDE] = jnp.broadcast_to(row, (SIDE, LANES))
    keep = (live_ref[...] > 0.5) & (lane >= REACH) & (lane < LANES - REACH)
    u, v = [main_ref[f, PAD : PAD + CELLS] for f in range(2)]
    (u_dx, u_dy), (v_dx, v_dy) = [slopes_of(main_ref, f, pltpu.roll(x, 1, 1), pltpu.roll(x, LANES - 1, 1))
                                  for f, x in enumerate((u, v))]
    for n, x in enumerate((u, v, v_dx - u_dy, u_dy + v_dx, u_dx - v_dy)):
        term_ref[n] = jnp.where(keep, x, 0.0)
    for n, x in enumerate(terms_of([term_ref[n] for n in range(BASES)])):
        if n >= BASES:
            term_ref[n] = x
    for place, (n, m) in enumerate(PAIRS):
        product = (term_ref[n] * term_ref[m]).reshape(CELLS // 8, 8, LANES)
        inner_ref[place] = jnp.sum(product, axis=0)


def base_kernel(mask_vmem, owner_vmem, main_ref, live_ref, inner_ref, own_ref, from_left_ref, from_right_ref, place_ref,
                out_ref, field_ref, gram_ref, pack_ref, tile_ref, side_ref, mask_ref, owner_ref, sem):
    tables = [pltpu.make_async_copy(mask_vmem, mask_ref, sem.at[0]),
              pltpu.make_async_copy(owner_vmem, owner_ref, sem.at[1])]
    for table in tables:
        table.start()
    lane = lax.broadcasted_iota(jnp.int32, (1, LANES), 1)
    received = jnp.concatenate([from_left_ref[...], from_right_ref[...], own_ref[...]], axis=0)
    placed = dot(jnp.concatenate(three_parts(received), axis=0), place_ref[...], (((0,), (0,)), ((), ())))
    inner = slice(PAD, PAD + CELLS)
    slopes, beside = [], []
    for f in range(2):
        full = main_ref[f] + placed[:, 2 * f * LANES : (2 * f + 1) * LANES]
        field_ref[f] = full
        rim = placed[inner, (2 * f + 1) * LANES : (2 * f + 2) * LANES]
        centre = full[inner]
        left = jnp.where(lane == 0, rim, pltpu.roll(centre, 1, 1))
        right = jnp.where(lane == LANES - 1, rim, pltpu.roll(centre, LANES - 1, 1))
        beside.append((left, right))
        slopes.append((centre, *slopes_of(field_ref, f, left, right)))
    (u, u_dx, u_dy), (v, v_dx, v_dy) = slopes
    live = live_ref[...] > 0.5
    outer = []
    for x in (u, v, v_dx - u_dy, u_dy + v_dx, u_dx - v_dy):
        x = jnp.where(live, x, 0.0)
        tile = jnp.zeros((8, LANES), F32)
        for b in range(CELLS // 8):
            tile = jnp.where(lane // 8 == b, pltpu.roll(x[8 * b : 8 * b + 8], (REACH + 8 * b) % LANES, 1), tile)
        outer.append(jnp.where(lane % 8 < 2 * REACH, tile, 0.0))
    outer = terms_of(outer)
    for place, (n, m) in enumerate(PAIRS):
        total = jnp.sum(inner_ref[place] + outer[n] * outer[m], axis=0, keepdims=True)
        gram_ref[n * TERMS + m : n * TERMS + m + 1] = total
        if m > n:
            gram_ref[m * TERMS + n : m * TERMS + n + 1] = total
    totals = jnp.sum(gram_ref[...], axis=1, keepdims=True)
    row = lax.broadcasted_iota(jnp.int32, (TERMS * TERMS, 1), 0)
    spread = jnp.where(row % LANES == lane, totals, 0.0)
    halves = [jnp.sum(spread[h * LANES : (h + 1) * LANES], axis=0, keepdims=True) for h in range(2)]
    owners = out_ref.shape[0]
    grid = CELLS // SIDE
    nothing = grid * grid
    for table in tables:
        table.wait()
    for o in range(owners + 1):
        tile_ref[o] = nothing
    for a in range(grid):
        for e in range(grid):
            tile_ref[jnp.where(mask_ref[a, e] == 1, owner_ref[a, e], owners)] = a * grid + e
    pack_ref[nothing] = jnp.zeros((BLOCK_ROWS, LANES), F32)
    group = lane // SIDE
    rims = jnp.where(lane % SIDE == 0, beside[0][0], pltpu.roll(beside[1][0], 1, 1))
    rims = jnp.where(lane % SIDE == SIDE - 1, beside[0][1], rims)
    side_ref[...] = jnp.transpose(jnp.where(lane % SIDE == SIDE - 2, pltpu.roll(beside[1][1], LANES - 1, 1), rims))
    for a in range(grid):
        ends = []
        for f in range(2):
            pieces = [field_ref[f, pl.ds(PAD + a * SIDE + q, 8, stride=4), :] for q in range(grid)]
            for e in range(grid):
                block = None
                for q in range(grid):
                    x = pltpu.roll(pieces[q], (q - e) % grid * SIDE, 1) if q != e else pieces[q]
                    block = x if block is None else jnp.where(group == q, x, block)
                pack_ref[a * grid + e, 8 * f : 8 * f + 8] = block
            for side in range(2):
                ends.append(field_ref[f, PAD + a * SIDE - 1 + side * (SIDE + 1) : PAD + a * SIDE + side * (SIDE + 1)])
        for e in range(grid):
            sides = [side_ref[e * SIDE + at : e * SIDE + at + 1] for at in (0, SIDE - 1, 1, SIDE - 2)]
            for spot, parts, own in ((SIDES, sides, a), (ENDS, ends, e)):
                row = None
                for q in range(4):
                    x = pltpu.roll(parts[q], (q - own) % 4 * SIDE, 1) if q != own else parts[q]
                    row = x if row is None else jnp.where(group == q, x, row)
                pack_ref[a * grid + e, spot : spot + 1] = row
    for o in range(owners):
        out_ref[o] = pack_ref[tile_ref[o]]
        for h in range(2):
            out_ref[o, GRAM + h : GRAM + h + 1] = halves[h]


def terms_of(base):
    u, v, vort, strain, stretch = base
    return [u, v, vort, strain, stretch, vort * vort, vort * strain, vort * stretch, strain * strain, stretch * stretch,
            strain * stretch, u * vort, v * vort, u * strain, v * stretch, u * v]


def library_kernel(x_ref, out_hbm, out_ref, sem):
    slots = x_ref.shape[0] // BLOCK_ROWS
    rows = lambda at: x_ref[pl.ds(at, slots, stride=BLOCK_ROWS), :]
    turn_by = lambda x, count: pltpu.roll(x, count % LANES, 1) if count % LANES else x
    lane = lax.broadcasted_iota(jnp.int32, (1, LANES), 1)
    sides, ends = rows(SIDES), rows(ENDS)
    fields = [[rows(8 * f + k) for k in range(8)] for f in range(2)]
    lower = [[turn_by(x, SIDE) for x in field] for field in fields]
    higher = [[turn_by(x, -SIDE) for x in field] for field in fields]

    def slopes(f, k):
        x = fields[f][k]
        left, right = turn_by(x, 1), turn_by(x, -1)
        for q in range(4):
            start = 64 * f + 4 * k + q
            left = jnp.where(lane == SIDE * q, turn_by(sides, SIDE * q - start), left)
            right = jnp.where(lane == SIDE * (q + 1) - 1, turn_by(sides, SIDE * q - 1 - start), right)
        before = lower[f][k - 1] if k else turn_by(ends, -64 * f)
        after = higher[f][k + 1] if k < 7 else turn_by(ends, 64 - 64 * f)
        up = jnp.where(lane < SIDE, before, lower[f][k])
        down = jnp.where(lane >= LANES - SIDE, after, higher[f][k])
        return (right - left) * 0.5, (down - up) * 0.5

    copies = []
    for k in range(8):
        (u_dx, u_dy), (v_dx, v_dy) = slopes(0, k), slopes(1, k)
        base = [fields[0][k], fields[1][k], v_dx - u_dy, u_dy + v_dx, u_dx - v_dy]
        for n, x in enumerate(terms_of(base)):
            out_ref[k, pl.ds(n, slots, stride=TERMS), :] = x
        copies.append(pltpu.make_async_copy(out_ref.at[k], out_hbm.at[:, pl.ds(k * LANES, LANES)], sem.at[k]))
        copies[k].start()
    for copy in copies:
        copy.wait()


VMEM = pl.BlockSpec(memory_space=pltpu.VMEM)
HBM = pl.BlockSpec(memory_space=pltpu.HBM)
SMEM = pl.BlockSpec(memory_space=pltpu.SMEM)
PARAMS = pltpu.CompilerParams(vmem_limit_bytes=24 << 20)


def struct(*shape):
    return jax.ShapeDtypeStruct(shape, F32)


def per_device(u_velocity, v_velocity, ocean_mask, tile_owner, lower_edge_quarter_turns):
    tiles, columns = lax.axis_size("tile"), lax.axis_size("col")
    onward = lambda count: [(i, (i + 1) % count) for i in range(count)]
    back = lambda count: [((i + 1) % count, i) for i in range(count)]
    here = lax.axis_index("tile").astype(jnp.int32)[None]
    in_hbm = lambda x: pltpu.with_memory_space_constraint(x, pltpu.HBM)
    up, down = pl.pallas_call(
        send_kernel,
        out_shape=[struct(2 * HALO, POOL * CELLS)] * 2,
        in_specs=[SMEM] + [HBM] * 3,
        out_specs=[VMEM] * 2,
        scratch_shapes=[pltpu.VMEM((2, 2, 16, POOL * CELLS), F32), pltpu.SMEM((tiles,), jnp.int32),
                        pltpu.SemaphoreType.DMA((2, 2)), pltpu.SemaphoreType.DMA],
        compiler_params=PARAMS,
        name="send_rows",
    )(here, *[in_hbm(x) for x in (lower_edge_quarter_turns, u_velocity, v_velocity)])
    up, down, u_velocity, v_velocity = lax.optimization_barrier((up, down, u_velocity, v_velocity))
    above = lax.ppermute(down, "tile", onward(tiles))
    below = lax.ppermute(up, "tile", back(tiles))
    column = lambda c: pl.BlockSpec((POOL * CELLS, LANES), lambda i: (0, c))
    rows = 2 * POOL * CELLS
    parts, weights, rim, early = pl.pallas_call(
        prepare_kernel,
        out_shape=[jax.ShapeDtypeStruct((rows, 2 * POOL * CELLS), BF16),
                   jax.ShapeDtypeStruct((POOL * CELLS, 10 * LANES), BF16), struct(FULL, LANES),
                   struct(rows, EARLY * LANES)],
        grid=(1,),
        in_specs=[column(c) for c in range(4)] * 2 + [HBM],
        out_specs=[VMEM] * 4,
        scratch_shapes=[pltpu.VMEM((rows, 2 * LANES), BF16)] + [pltpu.VMEM((POOL, PAD + CELLS, LANES), F32)] * 2
        + [pltpu.SemaphoreType.DMA],
        compiler_params=PARAMS,
        name="prepare_rows",
    )(*[u_velocity] * 4, *[v_velocity] * 4, in_hbm(jnp.asarray(column_weights())))
    to_left, to_right, own = pl.pallas_call(
        rim_kernel,
        out_shape=[struct(8, FULL), struct(8, FULL), struct(16, FULL)],
        in_specs=[VMEM] * 4,
        out_specs=[VMEM] * 3,
        scratch_shapes=[pltpu.VMEM((2, 2 * HALO, LANES), F32), pltpu.VMEM((2 * 2 * POOL * 8, LANES), F32),
                        pltpu.VMEM((FULL, LANES), F32)],
        compiler_params=PARAMS,
        name="rim_columns",
    )(above, below, weights, rim)
    from_right = lax.ppermute(to_left, "col", back(columns))
    from_left = lax.ppermute(to_right, "col", onward(columns))
    main, live, inner = pl.pallas_call(
        main_kernel,
        out_shape=[struct(2, FULL, LANES), struct(CELLS, LANES), struct(len(PAIRS), 8, LANES)],
        in_specs=[SMEM] + [VMEM] * 6,
        out_specs=[VMEM] * 3,
        scratch_shapes=[pltpu.VMEM((2, 4, 2 * HALO, LANES), F32), pltpu.VMEM((2 * POOL * 16, POOL * CELLS), F32),
                        pltpu.VMEM((2, POOL, FULL, LANES), F32), pltpu.VMEM((TERMS, CELLS, LANES), F32)],
        compiler_params=PARAMS,
        name="main_columns",
    )(ocean_mask, parts, early, weights, above, below, own)
    blocks = pl.pallas_call(
        base_kernel,
        out_shape=struct(tiles, BLOCK_ROWS, LANES),
        in_specs=[VMEM] * 9,
        out_specs=VMEM,
        scratch_shapes=[pltpu.VMEM((2, FULL, LANES), F32), pltpu.VMEM((TERMS * TERMS, LANES), F32),
                        pltpu.VMEM((17, BLOCK_ROWS, LANES), F32), pltpu.SMEM((tiles + 1,), jnp.int32),
                        pltpu.VMEM((LANES, CELLS), F32), pltpu.SMEM(ocean_mask.shape, jnp.int32),
                        pltpu.SMEM(tile_owner.shape, jnp.int32), pltpu.SemaphoreType.DMA((2,))],
        compiler_params=PARAMS,
        name="base_fields",
    )(ocean_mask, tile_owner, main, live, inner, own, from_left, from_right, jnp.asarray(place_matrix()))
    blocks = lax.all_to_all(blocks, "tile", split_axis=0, concat_axis=0, tiled=True)
    gram = jnp.sum(blocks[:, GRAM : GRAM + 2], axis=0)
    gram = lax.all_to_all(jnp.broadcast_to(gram, (columns, 2, LANES)), "col", split_axis=0, concat_axis=0, tiled=True)
    library = pl.pallas_call(
        library_kernel,
        out_shape=struct(tiles * TERMS, SIDE * SIDE),
        in_specs=[VMEM],
        out_specs=HBM,
        scratch_shapes=[pltpu.VMEM((8, tiles * TERMS, LANES), F32), pltpu.SemaphoreType.DMA((8,))],
        compiler_params=PARAMS,
        cost_estimate=pl.CostEstimate(flops=2 * tiles * TERMS * SIDE * SIDE, transcendentals=0,
                                      bytes_accessed=5 * tiles * TERMS * SIDE * SIDE),
        name="library_terms",
    )(blocks.reshape(tiles * BLOCK_ROWS, LANES))
    gram = jnp.sum(gram, axis=0).reshape(TERMS, TERMS) / (CELLS * CELLS)
    return library.reshape(1, 1, tiles, TERMS, SIDE * SIDE), gram


def solution(mesh):
    in_specs = (P("tile", "col"), P("tile", "col"), P("tile", "col"), P("tile", "col"), P())
    out_specs = (P("tile", "col", None, None, None), P())
    return jax.shard_map(
        per_device, mesh=mesh, in_specs=in_specs, out_specs=out_specs, check_vma=False
    )
```

```python
import math

import jax
import jax.numpy as jnp
import ml_dtypes
import numpy as np
from jax import lax
from jax.experimental import pallas as pl
from jax.experimental.pallas import tpu as pltpu
from jax.sharding import PartitionSpec as P

PASSES = 8
KAPPA = 0.2
POOL = 4
CELLS = 128
HALO = 12
SIDE = 32
TERMS = 16
PAD = 8
FULL = CELLS + 2 * PAD
LANES = 128
BASES = 5
BLOCK_ROWS = 24
SIDES, ENDS, GRAM = 16, 17, 18
F32 = jnp.float32
BF16 = jnp.bfloat16

SCALE = KAPPA**PASSES / (POOL * POOL)
RIM_COLS = (-2, -1, 0, CELLS - 1, CELLS, CELLS + 1)


def across(power, fine, coarse):
    total = 0
    for inner in range(POOL):
        offset = fine - (POOL * coarse + inner)
        if abs(offset) <= power and (power + offset) % 2 == 0:
            total += math.comb(power, (power + offset) // 2)
    return total


def column_weights():
    fine = CELLS * POOL
    main = np.zeros((fine, 9 * LANES), np.float32)
    rim = np.zeros((fine, LANES), np.float32)
    for j in range(PASSES + 1):
        for coarse in range(-2, CELLS + 2):
            for f in range(max(0, POOL * coarse - PASSES), min(fine, POOL * coarse + POOL + PASSES)):
                value = math.comb(PASSES, j) * across(PASSES - j, f, coarse)
                if 0 <= coarse < CELLS:
                    main[f, (PASSES - j) * LANES + coarse] = value
                if coarse in RIM_COLS:
                    rim[f, 6 * j + RIM_COLS.index(coarse)] = value
    assert not rim[64 : fine - 64].any()
    rim[LANES - 64 : LANES] = rim[fine - 64 :]
    rim[LANES : 2 * LANES] = rim[:LANES]
    weights = np.concatenate([main, rim], axis=1)
    out = weights.astype(ml_dtypes.bfloat16)
    assert (out.astype(np.float32) == weights).all()
    return out


def rim_selector():
    row = lax.broadcasted_iota(jnp.int32, (32, 1), 0)
    source = jnp.full((32, 1), -1, jnp.int32)
    for f in range(2):
        for c in range(3):
            source = jnp.where(row == 3 * f + c, 64 * f + c, source)
            source = jnp.where(row == 8 + 3 * f + c, 64 * f + 3 + c, source)
        source = jnp.where(row == 16 + 2 * f, 64 * f + 1, source)
        source = jnp.where(row == 17 + 2 * f, 64 * f + 4, source)
    lane = lax.broadcasted_iota(jnp.int32, (32, 3 * LANES), 1) % LANES
    return jnp.where(lane == source, 1.0, 0.0).astype(BF16)


def place_matrix():
    place = np.zeros((3, 32, 4 * LANES), np.float32)
    for f in range(2):
        add, rim = 2 * f * LANES, (2 * f + 1) * LANES
        place[:, 3 * f + 0, rim + 0] = 1.0
        place[:, 3 * f + 1, add + 0] = 1.0
        place[:, 3 * f + 2, add + 1] = 1.0
        place[:, 8 + 3 * f + 0, add + CELLS - 2] = 1.0
        place[:, 8 + 3 * f + 1, add + CELLS - 1] = 1.0
        place[:, 8 + 3 * f + 2, rim + CELLS - 1] = 1.0
        place[:, 16 + 2 * f, rim + 0] = 1.0
        place[:, 17 + 2 * f, rim + CELLS - 1] = 1.0
    return place.reshape(96, 4 * LANES).astype(ml_dtypes.bfloat16)


def head(x):
    scaled = x * 65537.0
    return scaled - (scaled - x)


def two_parts(x):
    high = head(x)
    return high.astype(BF16), (x - high).astype(BF16)


def three_parts(x):
    high = head(x)
    rest = x - high
    mid = head(rest)
    return high.astype(BF16), mid.astype(BF16), (rest - mid).astype(BF16)


def dot(a, b, dims=(((1,), (0,)), ((), ()))):
    return lax.dot_general(a, b, dims, preferred_element_type=F32)


def three_rows(t):
    rows = t[0].shape[0]
    up = pltpu.roll(t[3], 1, 0)
    down = pltpu.roll(t[0], rows - 1, 0)
    left, middle, right = t[0] + t[1], t[1] + t[2], t[2] + t[3]
    return [left + up, t[0] + middle, middle + t[3], right + down]


def turn(first, second, k):
    cosine = jnp.where(k == 0, 1.0, jnp.where(k == 2, -1.0, 0.0)).astype(F32)
    sine = jnp.where(k == 1, 1.0, jnp.where(k == 3, -1.0, 0.0)).astype(F32)
    return cosine * first - sine * second, sine * first + cosine * second


def send_kernel(here_ref, turns_hbm, u_hbm, v_hbm, up_ref, down_ref, x_ref, turns_ref, sem, turns_sem):
    rows = u_hbm.shape[0]
    copies = [pltpu.make_async_copy(hbm.at[pl.ds(start, 16)], x_ref.at[side, f], sem.at[side, f])
              for side, start in enumerate((0, rows - 16)) for f, hbm in enumerate((u_hbm, v_hbm))]
    table = pltpu.make_async_copy(turns_hbm, turns_ref, turns_sem)
    table.start()
    for copy in copies:
        copy.start()
    table.wait()
    tiles = turns_ref.shape[0]
    here = here_ref[0]
    k_up = lax.rem(4 - turns_ref[here], 4)
    k_down = turns_ref[lax.rem(here + 1, tiles)]
    for copy in copies:
        copy.wait()
    for side, (to_ref, k, start) in enumerate(((up_ref, k_up, 0), (down_ref, k_down, 16 - HALO))):
        for f, x in enumerate(turn(x_ref[side, 0], x_ref[side, 1], k)):
            to_ref[f * HALO : (f + 1) * HALO] = x[start : start + HALO]


EARLY = 6


def prepare_kernel(*refs):
    w_hbm, parts_ref, w_out, rim_ref, early_ref, rim_parts_ref, first_ref, last_ref, sem = refs[8:]
    copy = pltpu.make_async_copy(w_hbm, w_out, sem)
    copy.start()
    lane = lax.broadcasted_iota(jnp.int32, (1, LANES), 1)
    fine = POOL * CELLS
    for f in range(2):
        for p in range(POOL):
            spot = slice((f * POOL + p) * CELLS, (f * POOL + p + 1) * CELLS)
            pieces = [two_parts(refs[4 * f + c][pl.ds(p, CELLS, stride=POOL), :]) for c in range(4)]
            for part in range(2):
                for c in range(4):
                    parts_ref[spot, part * fine + c * LANES : part * fine + (c + 1) * LANES] = pieces[c][part]
                rim_parts_ref[spot, part * LANES : (part + 1) * LANES] = jnp.where(
                    lane < 64, pieces[0][part], pieces[3][part])
    copy.wait()
    z = dot(rim_parts_ref[...], w_out[: 2 * LANES, 9 * LANES :])
    for p in range(POOL):
        u, v = [z[(f * POOL + p) * CELLS : (f * POOL + p + 1) * CELLS] for f in range(2)]
        both = jnp.where(lane < 64, u, pltpu.roll(v, 64, 1))
        for to_ref in (first_ref, last_ref):
            to_ref[p, :PAD] = jnp.zeros((PAD, LANES), F32)
            to_ref[p, PAD:] = both
    for _ in range(PASSES):
        new = three_rows([pltpu.roll(last_ref[p], LANES - 6, 1) for p in range(POOL)])
        for p in range(POOL):
            last_ref[p] = new[p] + first_ref[p]
    pooled = ((last_ref[0] + last_ref[1]) + (last_ref[2] + last_ref[3])) * SCALE
    rim_ref[: PAD + CELLS] = pooled
    rim_ref[PAD + CELLS :] = pooled[:PAD]
    for start in range(0, EARLY, 2):
        cut = slice(start * LANES, (start + 2) * LANES)
        early_ref[:, cut] = dot(parts_ref[:, :fine], w_out[:, cut]) + dot(parts_ref[:, fine:], w_out[:, cut])


def rim_kernel(above_ref, below_ref, w_ref, rim_in, left_ref, right_ref, own_ref, rows_ref, strip_ref, rim_ref):
    lane = lax.broadcasted_iota(jnp.int32, (1, LANES), 1)
    strip_ref[...] = jnp.zeros_like(strip_ref)
    for s, (x_ref, start) in enumerate(((above_ref, 1), (below_ref, 4))):
        ends = jnp.where(lane < 64, x_ref[:, :LANES], x_ref[:, 3 * LANES :])
        rows_ref[s] = ends
        for f in range(2):
            for p in range(POOL):
                spot = ((f * 2 + s) * POOL + p) * 8 + start
                strip_ref[spot : spot + 3] = rows_ref[s, pl.ds(f * HALO + p, 3, stride=POOL), :]
    z = dot(jnp.concatenate(two_parts(strip_ref[...]), axis=1), w_ref[: 2 * LANES, 9 * LANES :])
    rim_ref[...] = rim_in[...]
    for s, (spot, start) in enumerate(((7, 3), (PAD + CELLS - 2, 2))):
        first = []
        for p in range(POOL):
            u, v = [z[((f * 2 + s) * POOL + p) * 8 : ((f * 2 + s) * POOL + p + 1) * 8] for f in range(2)]
            first.append(jnp.where(lane < 64, u, pltpu.roll(v, 64, 1)))
        powers = [first] + [[pltpu.roll(x, LANES - 6 * j, 1) for x in first] for j in range(1, PASSES + 1)]
        last = powers[PASSES]
        for j in range(PASSES - 1, -1, -1):
            last = [a + b for a, b in zip(three_rows(last), powers[j])]
        pooled = ((last[0] + last[1]) + (last[2] + last[3])) * SCALE
        rim_ref[spot : spot + 3] = rim_ref[spot : spot + 3] + pooled[start : start + 3]
    turned = jnp.transpose(rim_ref[...])
    for to_ref, columns in ((left_ref, (0, 1, 2)), (right_ref, (3, 4, 5)), (own_ref, (1, 4))):
        to_ref[...] = jnp.zeros_like(to_ref)
        for f in range(2):
            for place, c in enumerate(columns):
                spot = len(columns) * f + place
                to_ref[spot : spot + 1] = turned[64 * f + c : 64 * f + c + 1]


PAIRS = [(n, m) for n in range(TERMS) for m in range(n, TERMS)]
REACH = 3


def slopes_of(ref, f, left, right):
    up = ref[f, PAD - 1 : PAD - 1 + CELLS]
    down = ref[f, PAD + 1 : PAD + 1 + CELLS]
    return (right - left) * 0.5, (down - up) * 0.5


def main_kernel(mask_ref, parts_ref, early_ref, w_ref, above_ref, below_ref, _, main_ref, live_ref, inner_ref, rows_ref,
                strip_ref, sum_ref, term_ref):
    strip_ref[...] = jnp.zeros_like(strip_ref)
    for s, (x_ref, start) in enumerate(((above_ref, 5), (below_ref, 8))):
        for c in range(4):
            cut = slice(c * LANES, (c + 1) * LANES)
            rows_ref[s, c] = x_ref[:, cut]
            for f in range(2):
                for p in range(POOL):
                    spot = (f * POOL + p) * 16 + start
                    strip_ref[spot : spot + 3, cut] = rows_ref[s, c, pl.ds(f * HALO + p, 3, stride=POOL), :]
    strips = jnp.concatenate(two_parts(strip_ref[...]), axis=0)
    fine = POOL * CELLS
    for start in range(0, 9, 2):
        wide = min(2, 9 - start)
        w = w_ref[:, start * LANES : (start + wide) * LANES]
        if start < EARLY:
            z = early_ref[:, start * LANES : (start + wide) * LANES]
        else:
            z = dot(parts_ref[:, :fine], w) + dot(parts_ref[:, fine:], w)
        both = dot(strips, w)
        z_strip = both[: both.shape[0] // 2] + both[both.shape[0] // 2 :]
        for stage in range(start, start + wide):
            cut = slice((stage - start) * LANES, (stage - start + 1) * LANES)
            for f in range(2):
                own = []
                for p in range(POOL):
                    block = f * POOL + p
                    own.append(jnp.concatenate([
                        z_strip[block * 16 : block * 16 + 8, cut], z[block * CELLS : (block + 1) * CELLS, cut],
                        z_strip[block * 16 + 8 : block * 16 + 16, cut]], axis=0))
                if stage:
                    own = [a + b for a, b in zip(three_rows([sum_ref[f, p] for p in range(POOL)]), own)]
                for p in range(POOL):
                    sum_ref[f, p] = own[p]
    for f in range(2):
        main_ref[f] = ((sum_ref[f, 0] + sum_ref[f, 1]) + (sum_ref[f, 2] + sum_ref[f, 3])) * SCALE
    lane = lax.broadcasted_iota(jnp.int32, (1, LANES), 1)
    grid = CELLS // SIDE
    for a in range(grid):
        row = jnp.zeros((1, LANES), F32)
        for e in range(grid):
            row = jnp.where(lane // SIDE == e, (mask_ref[a, e] == 1).astype(F32), row)
        live_ref[a * SIDE : (a + 1) * SIDE] = jnp.broadcast_to(row, (SIDE, LANES))
    keep = (live_ref[...] > 0.5) & (lane >= REACH) & (lane < LANES - REACH)
    u, v = [main_ref[f, PAD : PAD + CELLS] for f in range(2)]
    (u_dx, u_dy), (v_dx, v_dy) = [slopes_of(main_ref, f, pltpu.roll(x, 1, 1), pltpu.roll(x, LANES - 1, 1))
                                  for f, x in enumerate((u, v))]
    for n, x in enumerate((u, v, v_dx - u_dy, u_dy + v_dx, u_dx - v_dy)):
        term_ref[n] = jnp.where(keep, x, 0.0)
    for n, x in enumerate(terms_of([term_ref[n] for n in range(BASES)])):
        if n >= BASES:
            term_ref[n] = x
    for place, (n, m) in enumerate(PAIRS):
        product = (term_ref[n] * term_ref[m]).reshape(CELLS // 8, 8, LANES)
        inner_ref[place] = jnp.sum(product, axis=0)


def base_kernel(mask_vmem, owner_vmem, main_ref, live_ref, inner_ref, own_ref, from_left_ref, from_right_ref, place_ref,
                out_ref, field_ref, gram_ref, pack_ref, tile_ref, side_ref, mask_ref, owner_ref, sem):
    tables = [pltpu.make_async_copy(mask_vmem, mask_ref, sem.at[0]),
              pltpu.make_async_copy(owner_vmem, owner_ref, sem.at[1])]
    for table in tables:
        table.start()
    lane = lax.broadcasted_iota(jnp.int32, (1, LANES), 1)
    received = jnp.concatenate([from_left_ref[...], from_right_ref[...], own_ref[...]], axis=0)
    placed = dot(jnp.concatenate(three_parts(received), axis=0), place_ref[...], (((0,), (0,)), ((), ())))
    inner = slice(PAD, PAD + CELLS)
    slopes, beside = [], []
    for f in range(2):
        full = main_ref[f] + placed[:, 2 * f * LANES : (2 * f + 1) * LANES]
        field_ref[f] = full
        rim = placed[inner, (2 * f + 1) * LANES : (2 * f + 2) * LANES]
        centre = full[inner]
        left = jnp.where(lane == 0, rim, pltpu.roll(centre, 1, 1))
        right = jnp.where(lane == LANES - 1, rim, pltpu.roll(centre, LANES - 1, 1))
        beside.append((left, right))
        slopes.append((centre, *slopes_of(field_ref, f, left, right)))
    (u, u_dx, u_dy), (v, v_dx, v_dy) = slopes
    live = live_ref[...] > 0.5
    outer = []
    for x in (u, v, v_dx - u_dy, u_dy + v_dx, u_dx - v_dy):
        x = jnp.where(live, x, 0.0)
        tile = jnp.zeros((8, LANES), F32)
        for b in range(CELLS // 8):
            tile = jnp.where(lane // 8 == b, pltpu.roll(x[8 * b : 8 * b + 8], (REACH + 8 * b) % LANES, 1), tile)
        outer.append(jnp.where(lane % 8 < 2 * REACH, tile, 0.0))
    outer = terms_of(outer)
    for place, (n, m) in enumerate(PAIRS):
        total = jnp.sum(inner_ref[place] + outer[n] * outer[m], axis=0, keepdims=True)
        gram_ref[n * TERMS + m : n * TERMS + m + 1] = total
        if m > n:
            gram_ref[m * TERMS + n : m * TERMS + n + 1] = total
    totals = jnp.sum(gram_ref[...], axis=1, keepdims=True)
    row = lax.broadcasted_iota(jnp.int32, (TERMS * TERMS, 1), 0)
    spread = jnp.where(row % LANES == lane, totals, 0.0)
    halves = [jnp.sum(spread[h * LANES : (h + 1) * LANES], axis=0, keepdims=True) for h in range(2)]
    owners = out_ref.shape[0]
    grid = CELLS // SIDE
    nothing = grid * grid
    for table in tables:
        table.wait()
    for o in range(owners + 1):
        tile_ref[o] = nothing
    for a in range(grid):
        for e in range(grid):
            tile_ref[jnp.where(mask_ref[a, e] == 1, owner_ref[a, e], owners)] = a * grid + e
    pack_ref[nothing] = jnp.zeros((BLOCK_ROWS, LANES), F32)
    group = lane // SIDE
    rims = jnp.where(lane % SIDE == 0, beside[0][0], pltpu.roll(beside[1][0], 1, 1))
    rims = jnp.where(lane % SIDE == SIDE - 1, beside[0][1], rims)
    side_ref[...] = jnp.transpose(jnp.where(lane % SIDE == SIDE - 2, pltpu.roll(beside[1][1], LANES - 1, 1), rims))
    for a in range(grid):
        ends = []
        for f in range(2):
            pieces = [field_ref[f, pl.ds(PAD + a * SIDE + q, 8, stride=4), :] for q in range(grid)]
            for e in range(grid):
                block = None
                for q in range(grid):
                    x = pltpu.roll(pieces[q], (q - e) % grid * SIDE, 1) if q != e else pieces[q]
                    block = x if block is None else jnp.where(group == q, x, block)
                pack_ref[a * grid + e, 8 * f : 8 * f + 8] = block
            for side in range(2):
                ends.append(field_ref[f, PAD + a * SIDE - 1 + side * (SIDE + 1) : PAD + a * SIDE + side * (SIDE + 1)])
        for e in range(grid):
            sides = [side_ref[e * SIDE + at : e * SIDE + at + 1] for at in (0, SIDE - 1, 1, SIDE - 2)]
            for spot, parts, own in ((SIDES, sides, a), (ENDS, ends, e)):
                row = None
                for q in range(4):
                    x = pltpu.roll(parts[q], (q - own) % 4 * SIDE, 1) if q != own else parts[q]
                    row = x if row is None else jnp.where(group == q, x, row)
                pack_ref[a * grid + e, spot : spot + 1] = row
    for o in range(owners):
        out_ref[o] = pack_ref[tile_ref[o]]
        for h in range(2):
            out_ref[o, GRAM + h : GRAM + h + 1] = halves[h]


def terms_of(base):
    u, v, vort, strain, stretch = base
    return [u, v, vort, strain, stretch, vort * vort, vort * strain, vort * stretch, strain * strain, stretch * stretch,
            strain * stretch, u * vort, v * vort, u * strain, v * stretch, u * v]


def library_kernel(x_ref, out_hbm, out_ref, sem):
    slots = x_ref.shape[0] // BLOCK_ROWS
    rows = lambda at: x_ref[pl.ds(at, slots, stride=BLOCK_ROWS), :]
    turn_by = lambda x, count: pltpu.roll(x, count % LANES, 1) if count % LANES else x
    lane = lax.broadcasted_iota(jnp.int32, (1, LANES), 1)
    sides, ends = rows(SIDES), rows(ENDS)
    fields = [[rows(8 * f + k) for k in range(8)] for f in range(2)]
    lower = [[turn_by(x, SIDE) for x in field] for field in fields]
    higher = [[turn_by(x, -SIDE) for x in field] for field in fields]

    def slopes(f, k):
        x = fields[f][k]
        left, right = turn_by(x, 1), turn_by(x, -1)
        for q in range(4):
            start = 64 * f + 4 * k + q
            left = jnp.where(lane == SIDE * q, turn_by(sides, SIDE * q - start), left)
            right = jnp.where(lane == SIDE * (q + 1) - 1, turn_by(sides, SIDE * q - 1 - start), right)
        before = lower[f][k - 1] if k else turn_by(ends, -64 * f)
        after = higher[f][k + 1] if k < 7 else turn_by(ends, 64 - 64 * f)
        up = jnp.where(lane < SIDE, before, lower[f][k])
        down = jnp.where(lane >= LANES - SIDE, after, higher[f][k])
        return (right - left) * 0.5, (down - up) * 0.5

    copies = []
    for k in range(8):
        (u_dx, u_dy), (v_dx, v_dy) = slopes(0, k), slopes(1, k)
        base = [fields[0][k], fields[1][k], v_dx - u_dy, u_dy + v_dx, u_dx - v_dy]
        for n, x in enumerate(terms_of(base)):
            out_ref[k, pl.ds(n, slots, stride=TERMS), :] = x
        copies.append(pltpu.make_async_copy(out_ref.at[k], out_hbm.at[:, pl.ds(k * LANES, LANES)], sem.at[k]))
        copies[k].start()
    for copy in copies:
        copy.wait()


VMEM = pl.BlockSpec(memory_space=pltpu.VMEM)
HBM = pl.BlockSpec(memory_space=pltpu.HBM)
SMEM = pl.BlockSpec(memory_space=pltpu.SMEM)
PARAMS = pltpu.CompilerParams(vmem_limit_bytes=24 << 20)


def struct(*shape):
    return jax.ShapeDtypeStruct(shape, F32)


def per_device(u_velocity, v_velocity, ocean_mask, tile_owner, lower_edge_quarter_turns):
    tiles, columns = lax.axis_size("tile"), lax.axis_size("col")
    onward = lambda count: [(i, (i + 1) % count) for i in range(count)]
    back = lambda count: [((i + 1) % count, i) for i in range(count)]
    here = lax.axis_index("tile").astype(jnp.int32)[None]
    in_hbm = lambda x: pltpu.with_memory_space_constraint(x, pltpu.HBM)
    up, down = pl.pallas_call(
        send_kernel,
        out_shape=[struct(2 * HALO, POOL * CELLS)] * 2,
        in_specs=[SMEM] + [HBM] * 3,
        out_specs=[VMEM] * 2,
        scratch_shapes=[pltpu.VMEM((2, 2, 16, POOL * CELLS), F32), pltpu.SMEM((tiles,), jnp.int32),
                        pltpu.SemaphoreType.DMA((2, 2)), pltpu.SemaphoreType.DMA],
        compiler_params=PARAMS,
        name="send_rows",
    )(here, *[in_hbm(x) for x in (lower_edge_quarter_turns, u_velocity, v_velocity)])
    up, down, u_velocity, v_velocity = lax.optimization_barrier((up, down, u_velocity, v_velocity))
    above = lax.ppermute(down, "tile", onward(tiles))
    below = lax.ppermute(up, "tile", back(tiles))
    column = lambda c: pl.BlockSpec((POOL * CELLS, LANES), lambda i: (0, c))
    rows = 2 * POOL * CELLS
    parts, weights, rim, early = pl.pallas_call(
        prepare_kernel,
        out_shape=[jax.ShapeDtypeStruct((rows, 2 * POOL * CELLS), BF16),
                   jax.ShapeDtypeStruct((POOL * CELLS, 10 * LANES), BF16), struct(FULL, LANES),
                   struct(rows, EARLY * LANES)],
        grid=(1,),
        in_specs=[column(c) for c in range(4)] * 2 + [HBM],
        out_specs=[VMEM] * 4,
        scratch_shapes=[pltpu.VMEM((rows, 2 * LANES), BF16)] + [pltpu.VMEM((POOL, PAD + CELLS, LANES), F32)] * 2
        + [pltpu.SemaphoreType.DMA],
        compiler_params=PARAMS,
        name="prepare_rows",
    )(*[u_velocity] * 4, *[v_velocity] * 4, in_hbm(jnp.asarray(column_weights())))
    to_left, to_right, own = pl.pallas_call(
        rim_kernel,
        out_shape=[struct(8, FULL), struct(8, FULL), struct(16, FULL)],
        in_specs=[VMEM] * 4,
        out_specs=[VMEM] * 3,
        scratch_shapes=[pltpu.VMEM((2, 2 * HALO, LANES), F32), pltpu.VMEM((2 * 2 * POOL * 8, LANES), F32),
                        pltpu.VMEM((FULL, LANES), F32)],
        compiler_params=PARAMS,
        name="rim_columns",
    )(above, below, weights, rim)
    from_right = lax.ppermute(to_left, "col", back(columns))
    from_left = lax.ppermute(to_right, "col", onward(columns))
    main, live, inner = pl.pallas_call(
        main_kernel,
        out_shape=[struct(2, FULL, LANES), struct(CELLS, LANES), struct(len(PAIRS), 8, LANES)],
        in_specs=[SMEM] + [VMEM] * 6,
        out_specs=[VMEM] * 3,
        scratch_shapes=[pltpu.VMEM((2, 4, 2 * HALO, LANES), F32), pltpu.VMEM((2 * POOL * 16, POOL * CELLS), F32),
                        pltpu.VMEM((2, POOL, FULL, LANES), F32), pltpu.VMEM((TERMS, CELLS, LANES), F32)],
        compiler_params=PARAMS,
        name="main_columns",
    )(ocean_mask, parts, early, weights, above, below, own)
    blocks = pl.pallas_call(
        base_kernel,
        out_shape=struct(tiles, BLOCK_ROWS, LANES),
        in_specs=[VMEM] * 9,
        out_specs=VMEM,
        scratch_shapes=[pltpu.VMEM((2, FULL, LANES), F32), pltpu.VMEM((TERMS * TERMS, LANES), F32),
                        pltpu.VMEM((17, BLOCK_ROWS, LANES), F32), pltpu.SMEM((tiles + 1,), jnp.int32),
                        pltpu.VMEM((LANES, CELLS), F32), pltpu.SMEM(ocean_mask.shape, jnp.int32),
                        pltpu.SMEM(tile_owner.shape, jnp.int32), pltpu.SemaphoreType.DMA((2,))],
        compiler_params=PARAMS,
        name="base_fields",
    )(ocean_mask, tile_owner, main, live, inner, own, from_left, from_right, jnp.asarray(place_matrix()))
    blocks = lax.all_to_all(blocks, "tile", split_axis=0, concat_axis=0, tiled=True)
    gram = jnp.sum(blocks[:, GRAM : GRAM + 2], axis=0)
    gram = lax.all_to_all(jnp.broadcast_to(gram, (columns, 2, LANES)), "col", split_axis=0, concat_axis=0, tiled=True)
    library = pl.pallas_call(
        library_kernel,
        out_shape=struct(tiles * TERMS, SIDE * SIDE),
        in_specs=[VMEM],
        out_specs=HBM,
        scratch_shapes=[pltpu.VMEM((8, tiles * TERMS, LANES), F32), pltpu.SemaphoreType.DMA((8,))],
        compiler_params=PARAMS,
        cost_estimate=pl.CostEstimate(flops=2 * tiles * TERMS * SIDE * SIDE, transcendentals=0,
                                      bytes_accessed=5 * tiles * TERMS * SIDE * SIDE),
        name="library_terms",
    )(blocks.reshape(tiles * BLOCK_ROWS, LANES))
    gram = jnp.sum(gram, axis=0).reshape(TERMS, TERMS) / (CELLS * CELLS)
    return library.reshape(1, 1, tiles, TERMS, SIDE * SIDE), gram


def solution(mesh):
    in_specs = (P("tile", "col"), P("tile", "col"), P("tile", "col"), P("tile", "col"), P())
    out_specs = (P("tile", "col", None, None, None), P())
    return jax.shard_map(
        per_device, mesh=mesh, in_specs=in_specs, out_specs=out_specs, check_vma=False
    )
```

```python
import math

import jax
import jax.numpy as jnp
import ml_dtypes
import numpy as np
from jax import lax
from jax.experimental import pallas as pl
from jax.experimental.pallas import tpu as pltpu
from jax.sharding import PartitionSpec as P

PASSES = 8
KAPPA = 0.2
POOL = 4
CELLS = 128
HALO = 12
SIDE = 32
TERMS = 16
PAD = 8
FULL = CELLS + 2 * PAD
LANES = 128
BASES = 5
BLOCK_ROWS = 24
SIDES, ENDS, GRAM = 16, 17, 18
F32 = jnp.float32
BF16 = jnp.bfloat16

SCALE = KAPPA**PASSES / (POOL * POOL)
RIM_COLS = (-2, -1, 0, CELLS - 1, CELLS, CELLS + 1)


def across(power, fine, coarse):
    total = 0
    for inner in range(POOL):
        offset = fine - (POOL * coarse + inner)
        if abs(offset) <= power and (power + offset) % 2 == 0:
            total += math.comb(power, (power + offset) // 2)
    return total


def column_weights():
    fine = CELLS * POOL
    main = np.zeros((fine, 9 * LANES), np.float32)
    rim = np.zeros((fine, LANES), np.float32)
    for j in range(PASSES + 1):
        for coarse in range(-2, CELLS + 2):
            for f in range(max(0, POOL * coarse - PASSES), min(fine, POOL * coarse + POOL + PASSES)):
                value = math.comb(PASSES, j) * across(PASSES - j, f, coarse)
                if 0 <= coarse < CELLS:
                    main[f, (PASSES - j) * LANES + coarse] = value
                if coarse in RIM_COLS:
                    rim[f, 6 * j + RIM_COLS.index(coarse)] = value
    assert not rim[64 : fine - 64].any()
    rim[LANES - 64 : LANES] = rim[fine - 64 :]
    rim[LANES : 2 * LANES] = rim[:LANES]
    weights = np.concatenate([main, rim], axis=1)
    out = weights.astype(ml_dtypes.bfloat16)
    assert (out.astype(np.float32) == weights).all()
    return out


def rim_selector():
    row = lax.broadcasted_iota(jnp.int32, (32, 1), 0)
    source = jnp.full((32, 1), -1, jnp.int32)
    for f in range(2):
        for c in range(3):
            source = jnp.where(row == 3 * f + c, 64 * f + c, source)
            source = jnp.where(row == 8 + 3 * f + c, 64 * f + 3 + c, source)
        source = jnp.where(row == 16 + 2 * f, 64 * f + 1, source)
        source = jnp.where(row == 17 + 2 * f, 64 * f + 4, source)
    lane = lax.broadcasted_iota(jnp.int32, (32, 3 * LANES), 1) % LANES
    return jnp.where(lane == source, 1.0, 0.0).astype(BF16)


def place_matrix():
    place = np.zeros((3, 32, 4 * LANES), np.float32)
    for f in range(2):
        add, rim = 2 * f * LANES, (2 * f + 1) * LANES
        place[:, 3 * f + 0, rim + 0] = 1.0
        place[:, 3 * f + 1, add + 0] = 1.0
        place[:, 3 * f + 2, add + 1] = 1.0
        place[:, 8 + 3 * f + 0, add + CELLS - 2] = 1.0
        place[:, 8 + 3 * f + 1, add + CELLS - 1] = 1.0
        place[:, 8 + 3 * f + 2, rim + CELLS - 1] = 1.0
        place[:, 16 + 2 * f, rim + 0] = 1.0
        place[:, 17 + 2 * f, rim + CELLS - 1] = 1.0
    return place.reshape(96, 4 * LANES).astype(ml_dtypes.bfloat16)


def head(x):
    scaled = x * 65537.0
    return scaled - (scaled - x)


def two_parts(x):
    high = head(x)
    return high.astype(BF16), (x - high).astype(BF16)


def three_parts(x):
    high = head(x)
    rest = x - high
    mid = head(rest)
    return high.astype(BF16), mid.astype(BF16), (rest - mid).astype(BF16)


def dot(a, b, dims=(((1,), (0,)), ((), ()))):
    return lax.dot_general(a, b, dims, preferred_element_type=F32)


def three_rows(t):
    rows = t[0].shape[0]
    up = pltpu.roll(t[3], 1, 0)
    down = pltpu.roll(t[0], rows - 1, 0)
    left, middle, right = t[0] + t[1], t[1] + t[2], t[2] + t[3]
    return [left + up, t[0] + middle, middle + t[3], right + down]


def turn(first, second, k):
    cosine = jnp.where(k == 0, 1.0, jnp.where(k == 2, -1.0, 0.0)).astype(F32)
    sine = jnp.where(k == 1, 1.0, jnp.where(k == 3, -1.0, 0.0)).astype(F32)
    return cosine * first - sine * second, sine * first + cosine * second


def send_kernel(here_ref, turns_hbm, u_hbm, v_hbm, up_ref, down_ref, x_ref, turns_ref, sem, turns_sem):
    rows = u_hbm.shape[0]
    copies = [pltpu.make_async_copy(hbm.at[pl.ds(start, 16)], x_ref.at[side, f], sem.at[side, f])
              for side, start in enumerate((0, rows - 16)) for f, hbm in enumerate((u_hbm, v_hbm))]
    table = pltpu.make_async_copy(turns_hbm, turns_ref, turns_sem)
    table.start()
    for copy in copies:
        copy.start()
    table.wait()
    tiles = turns_ref.shape[0]
    here = here_ref[0]
    k_up = lax.rem(4 - turns_ref[here], 4)
    k_down = turns_ref[lax.rem(here + 1, tiles)]
    for copy in copies:
        copy.wait()
    for side, (to_ref, k, start) in enumerate(((up_ref, k_up, 0), (down_ref, k_down, 16 - HALO))):
        for f, x in enumerate(turn(x_ref[side, 0], x_ref[side, 1], k)):
            to_ref[f * HALO : (f + 1) * HALO] = x[start : start + HALO]


EARLY = 8


def prepare_kernel(*refs):
    w_hbm, parts_ref, w_out, rim_ref, early_ref, rim_parts_ref, first_ref, last_ref, sem = refs[8:]
    copy = pltpu.make_async_copy(w_hbm, w_out, sem)
    copy.start()
    lane = lax.broadcasted_iota(jnp.int32, (1, LANES), 1)
    fine = POOL * CELLS
    for f in range(2):
        for p in range(POOL):
            spot = slice((f * POOL + p) * CELLS, (f * POOL + p + 1) * CELLS)
            pieces = [two_parts(refs[4 * f + c][pl.ds(p, CELLS, stride=POOL), :]) for c in range(4)]
            for part in range(2):
                for c in range(4):
                    parts_ref[spot, part * fine + c * LANES : part * fine + (c + 1) * LANES] = pieces[c][part]
                rim_parts_ref[spot, part * LANES : (part + 1) * LANES] = jnp.where(
                    lane < 64, pieces[0][part], pieces[3][part])
    copy.wait()
    z = dot(rim_parts_ref[...], w_out[: 2 * LANES, 9 * LANES :])
    for p in range(POOL):
        u, v = [z[(f * POOL + p) * CELLS : (f * POOL + p + 1) * CELLS] for f in range(2)]
        both = jnp.where(lane < 64, u, pltpu.roll(v, 64, 1))
        for to_ref in (first_ref, last_ref):
            to_ref[p, :PAD] = jnp.zeros((PAD, LANES), F32)
            to_ref[p, PAD:] = both
    for _ in range(PASSES):
        new = three_rows([pltpu.roll(last_ref[p], LANES - 6, 1) for p in range(POOL)])
        for p in range(POOL):
            last_ref[p] = new[p] + first_ref[p]
    pooled = ((last_ref[0] + last_ref[1]) + (last_ref[2] + last_ref[3])) * SCALE
    rim_ref[: PAD + CELLS] = pooled
    rim_ref[PAD + CELLS :] = pooled[:PAD]
    for start in range(0, EARLY, 2):
        cut = slice(start * LANES, (start + 2) * LANES)
        early_ref[:, cut] = dot(parts_ref[:, :fine], w_out[:, cut]) + dot(parts_ref[:, fine:], w_out[:, cut])


def rim_kernel(above_ref, below_ref, w_ref, rim_in, left_ref, right_ref, own_ref, rows_ref, strip_ref, rim_ref):
    lane = lax.broadcasted_iota(jnp.int32, (1, LANES), 1)
    strip_ref[...] = jnp.zeros_like(strip_ref)
    for s, (x_ref, start) in enumerate(((above_ref, 1), (below_ref, 4))):
        ends = jnp.where(lane < 64, x_ref[:, :LANES], x_ref[:, 3 * LANES :])
        rows_ref[s] = ends
        for f in range(2):
            for p in range(POOL):
                spot = ((f * 2 + s) * POOL + p) * 8 + start
                strip_ref[spot : spot + 3] = rows_ref[s, pl.ds(f * HALO + p, 3, stride=POOL), :]
    z = dot(jnp.concatenate(two_parts(strip_ref[...]), axis=1), w_ref[: 2 * LANES, 9 * LANES :])
    rim_ref[...] = rim_in[...]
    for s, (spot, start) in enumerate(((7, 3), (PAD + CELLS - 2, 2))):
        first = []
        for p in range(POOL):
            u, v = [z[((f * 2 + s) * POOL + p) * 8 : ((f * 2 + s) * POOL + p + 1) * 8] for f in range(2)]
            first.append(jnp.where(lane < 64, u, pltpu.roll(v, 64, 1)))
        powers = [first] + [[pltpu.roll(x, LANES - 6 * j, 1) for x in first] for j in range(1, PASSES + 1)]
        last = powers[PASSES]
        for j in range(PASSES - 1, -1, -1):
            last = [a + b for a, b in zip(three_rows(last), powers[j])]
        pooled = ((last[0] + last[1]) + (last[2] + last[3])) * SCALE
        rim_ref[spot : spot + 3] = rim_ref[spot : spot + 3] + pooled[start : start + 3]
    turned = jnp.transpose(rim_ref[...])
    for to_ref, columns in ((left_ref, (0, 1, 2)), (right_ref, (3, 4, 5)), (own_ref, (1, 4))):
        to_ref[...] = jnp.zeros_like(to_ref)
        for f in range(2):
            for place, c in enumerate(columns):
                spot = len(columns) * f + place
                to_ref[spot : spot + 1] = turned[64 * f + c : 64 * f + c + 1]


PAIRS = [(n, m) for n in range(TERMS) for m in range(n, TERMS)]
REACH = 3


def slopes_of(ref, f, left, right):
    up = ref[f, PAD - 1 : PAD - 1 + CELLS]
    down = ref[f, PAD + 1 : PAD + 1 + CELLS]
    return (right - left) * 0.5, (down - up) * 0.5


def main_kernel(mask_ref, parts_ref, early_ref, w_ref, above_ref, below_ref, _, main_ref, live_ref, inner_ref, rows_ref,
                strip_ref, sum_ref, term_ref):
    strip_ref[...] = jnp.zeros_like(strip_ref)
    for s, (x_ref, start) in enumerate(((above_ref, 5), (below_ref, 8))):
        for c in range(4):
            cut = slice(c * LANES, (c + 1) * LANES)
            rows_ref[s, c] = x_ref[:, cut]
            for f in range(2):
                for p in range(POOL):
                    spot = (f * POOL + p) * 16 + start
                    strip_ref[spot : spot + 3, cut] = rows_ref[s, c, pl.ds(f * HALO + p, 3, stride=POOL), :]
    strips = jnp.concatenate(two_parts(strip_ref[...]), axis=0)
    fine = POOL * CELLS
    for start in range(0, 9, 2):
        wide = min(2, 9 - start)
        w = w_ref[:, start * LANES : (start + wide) * LANES]
        if start < EARLY:
            z = early_ref[:, start * LANES : (start + wide) * LANES]
        else:
            z = dot(parts_ref[:, :fine], w) + dot(parts_ref[:, fine:], w)
        both = dot(strips, w)
        z_strip = both[: both.shape[0] // 2] + both[both.shape[0] // 2 :]
        for stage in range(start, start + wide):
            cut = slice((stage - start) * LANES, (stage - start + 1) * LANES)
            for f in range(2):
                own = []
                for p in range(POOL):
                    block = f * POOL + p
                    own.append(jnp.concatenate([
                        z_strip[block * 16 : block * 16 + 8, cut], z[block * CELLS : (block + 1) * CELLS, cut],
                        z_strip[block * 16 + 8 : block * 16 + 16, cut]], axis=0))
                if stage:
                    own = [a + b for a, b in zip(three_rows([sum_ref[f, p] for p in range(POOL)]), own)]
                for p in range(POOL):
                    sum_ref[f, p] = own[p]
    for f in range(2):
        main_ref[f] = ((sum_ref[f, 0] + sum_ref[f, 1]) + (sum_ref[f, 2] + sum_ref[f, 3])) * SCALE
    lane = lax.broadcasted_iota(jnp.int32, (1, LANES), 1)
    grid = CELLS // SIDE
    for a in range(grid):
        row = jnp.zeros((1, LANES), F32)
        for e in range(grid):
            row = jnp.where(lane // SIDE == e, (mask_ref[a, e] == 1).astype(F32), row)
        live_ref[a * SIDE : (a + 1) * SIDE] = jnp.broadcast_to(row, (SIDE, LANES))
    keep = (live_ref[...] > 0.5) & (lane >= REACH) & (lane < LANES - REACH)
    u, v = [main_ref[f, PAD : PAD + CELLS] for f in range(2)]
    (u_dx, u_dy), (v_dx, v_dy) = [slopes_of(main_ref, f, pltpu.roll(x, 1, 1), pltpu.roll(x, LANES - 1, 1))
                                  for f, x in enumerate((u, v))]
    for n, x in enumerate((u, v, v_dx - u_dy, u_dy + v_dx, u_dx - v_dy)):
        term_ref[n] = jnp.where(keep, x, 0.0)
    for n, x in enumerate(terms_of([term_ref[n] for n in range(BASES)])):
        if n >= BASES:
            term_ref[n] = x
    for place, (n, m) in enumerate(PAIRS):
        product = (term_ref[n] * term_ref[m]).reshape(CELLS // 8, 8, LANES)
        inner_ref[place] = jnp.sum(product, axis=0)


def base_kernel(mask_vmem, owner_vmem, main_ref, live_ref, inner_ref, own_ref, from_left_ref, from_right_ref, place_ref,
                out_ref, field_ref, gram_ref, pack_ref, tile_ref, side_ref, mask_ref, owner_ref, sem):
    tables = [pltpu.make_async_copy(mask_vmem, mask_ref, sem.at[0]),
              pltpu.make_async_copy(owner_vmem, owner_ref, sem.at[1])]
    for table in tables:
        table.start()
    lane = lax.broadcasted_iota(jnp.int32, (1, LANES), 1)
    received = jnp.concatenate([from_left_ref[...], from_right_ref[...], own_ref[...]], axis=0)
    placed = dot(jnp.concatenate(three_parts(received), axis=0), place_ref[...], (((0,), (0,)), ((), ())))
    inner = slice(PAD, PAD + CELLS)
    slopes, beside = [], []
    for f in range(2):
        full = main_ref[f] + placed[:, 2 * f * LANES : (2 * f + 1) * LANES]
        field_ref[f] = full
        rim = placed[inner, (2 * f + 1) * LANES : (2 * f + 2) * LANES]
        centre = full[inner]
        left = jnp.where(lane == 0, rim, pltpu.roll(centre, 1, 1))
        right = jnp.where(lane == LANES - 1, rim, pltpu.roll(centre, LANES - 1, 1))
        beside.append((left, right))
        slopes.append((centre, *slopes_of(field_ref, f, left, right)))
    (u, u_dx, u_dy), (v, v_dx, v_dy) = slopes
    live = live_ref[...] > 0.5
    outer = []
    for x in (u, v, v_dx - u_dy, u_dy + v_dx, u_dx - v_dy):
        x = jnp.where(live, x, 0.0)
        tile = jnp.zeros((8, LANES), F32)
        for b in range(CELLS // 8):
            tile = jnp.where(lane // 8 == b, pltpu.roll(x[8 * b : 8 * b + 8], (REACH + 8 * b) % LANES, 1), tile)
        outer.append(jnp.where(lane % 8 < 2 * REACH, tile, 0.0))
    outer = terms_of(outer)
    for place, (n, m) in enumerate(PAIRS):
        total = jnp.sum(inner_ref[place] + outer[n] * outer[m], axis=0, keepdims=True)
        gram_ref[n * TERMS + m : n * TERMS + m + 1] = total
        if m > n:
            gram_ref[m * TERMS + n : m * TERMS + n + 1] = total
    totals = jnp.sum(gram_ref[...], axis=1, keepdims=True)
    row = lax.broadcasted_iota(jnp.int32, (TERMS * TERMS, 1), 0)
    spread = jnp.where(row % LANES == lane, totals, 0.0)
    halves = [jnp.sum(spread[h * LANES : (h + 1) * LANES], axis=0, keepdims=True) for h in range(2)]
    owners = out_ref.shape[0]
    grid = CELLS // SIDE
    nothing = grid * grid
    for table in tables:
        table.wait()
    for o in range(owners + 1):
        tile_ref[o] = nothing
    for a in range(grid):
        for e in range(grid):
            tile_ref[jnp.where(mask_ref[a, e] == 1, owner_ref[a, e], owners)] = a * grid + e
    pack_ref[nothing] = jnp.zeros((BLOCK_ROWS, LANES), F32)
    group = lane // SIDE
    rims = jnp.where(lane % SIDE == 0, beside[0][0], pltpu.roll(beside[1][0], 1, 1))
    rims = jnp.where(lane % SIDE == SIDE - 1, beside[0][1], rims)
    side_ref[...] = jnp.transpose(jnp.where(lane % SIDE == SIDE - 2, pltpu.roll(beside[1][1], LANES - 1, 1), rims))
    for a in range(grid):
        ends = []
        for f in range(2):
            pieces = [field_ref[f, pl.ds(PAD + a * SIDE + q, 8, stride=4), :] for q in range(grid)]
            for e in range(grid):
                block = None
                for q in range(grid):
                    x = pltpu.roll(pieces[q], (q - e) % grid * SIDE, 1) if q != e else pieces[q]
                    block = x if block is None else jnp.where(group == q, x, block)
                pack_ref[a * grid + e, 8 * f : 8 * f + 8] = block
            for side in range(2):
                ends.append(field_ref[f, PAD + a * SIDE - 1 + side * (SIDE + 1) : PAD + a * SIDE + side * (SIDE + 1)])
        for e in range(grid):
            sides = [side_ref[e * SIDE + at : e * SIDE + at + 1] for at in (0, SIDE - 1, 1, SIDE - 2)]
            for spot, parts, own in ((SIDES, sides, a), (ENDS, ends, e)):
                row = None
                for q in range(4):
                    x = pltpu.roll(parts[q], (q - own) % 4 * SIDE, 1) if q != own else parts[q]
                    row = x if row is None else jnp.where(group == q, x, row)
                pack_ref[a * grid + e, spot : spot + 1] = row
    for o in range(owners):
        out_ref[o] = pack_ref[tile_ref[o]]
        for h in range(2):
            out_ref[o, GRAM + h : GRAM + h + 1] = halves[h]


def terms_of(base):
    u, v, vort, strain, stretch = base
    return [u, v, vort, strain, stretch, vort * vort, vort * strain, vort * stretch, strain * strain, stretch * stretch,
            strain * stretch, u * vort, v * vort, u * strain, v * stretch, u * v]


def library_kernel(x_ref, out_hbm, out_ref, sem):
    slots = x_ref.shape[0] // BLOCK_ROWS
    rows = lambda at: x_ref[pl.ds(at, slots, stride=BLOCK_ROWS), :]
    turn_by = lambda x, count: pltpu.roll(x, count % LANES, 1) if count % LANES else x
    lane = lax.broadcasted_iota(jnp.int32, (1, LANES), 1)
    sides, ends = rows(SIDES), rows(ENDS)
    fields = [[rows(8 * f + k) for k in range(8)] for f in range(2)]
    lower = [[turn_by(x, SIDE) for x in field] for field in fields]
    higher = [[turn_by(x, -SIDE) for x in field] for field in fields]

    def slopes(f, k):
        x = fields[f][k]
        left, right = turn_by(x, 1), turn_by(x, -1)
        for q in range(4):
            start = 64 * f + 4 * k + q
            left = jnp.where(lane == SIDE * q, turn_by(sides, SIDE * q - start), left)
            right = jnp.where(lane == SIDE * (q + 1) - 1, turn_by(sides, SIDE * q - 1 - start), right)
        before = lower[f][k - 1] if k else turn_by(ends, -64 * f)
        after = higher[f][k + 1] if k < 7 else turn_by(ends, 64 - 64 * f)
        up = jnp.where(lane < SIDE, before, lower[f][k])
        down = jnp.where(lane >= LANES - SIDE, after, higher[f][k])
        return (right - left) * 0.5, (down - up) * 0.5

    copies = []
    for k in range(8):
        (u_dx, u_dy), (v_dx, v_dy) = slopes(0, k), slopes(1, k)
        base = [fields[0][k], fields[1][k], v_dx - u_dy, u_dy + v_dx, u_dx - v_dy]
        for n, x in enumerate(terms_of(base)):
            out_ref[k, pl.ds(n, slots, stride=TERMS), :] = x
        copies.append(pltpu.make_async_copy(out_ref.at[k], out_hbm.at[:, pl.ds(k * LANES, LANES)], sem.at[k]))
        copies[k].start()
    for copy in copies:
        copy.wait()


VMEM = pl.BlockSpec(memory_space=pltpu.VMEM)
HBM = pl.BlockSpec(memory_space=pltpu.HBM)
SMEM = pl.BlockSpec(memory_space=pltpu.SMEM)
PARAMS = pltpu.CompilerParams(vmem_limit_bytes=24 << 20)


def struct(*shape):
    return jax.ShapeDtypeStruct(shape, F32)


def per_device(u_velocity, v_velocity, ocean_mask, tile_owner, lower_edge_quarter_turns):
    tiles, columns = lax.axis_size("tile"), lax.axis_size("col")
    onward = lambda count: [(i, (i + 1) % count) for i in range(count)]
    back = lambda count: [((i + 1) % count, i) for i in range(count)]
    here = lax.axis_index("tile").astype(jnp.int32)[None]
    in_hbm = lambda x: pltpu.with_memory_space_constraint(x, pltpu.HBM)
    up, down = pl.pallas_call(
        send_kernel,
        out_shape=[struct(2 * HALO, POOL * CELLS)] * 2,
        in_specs=[SMEM] + [HBM] * 3,
        out_specs=[VMEM] * 2,
        scratch_shapes=[pltpu.VMEM((2, 2, 16, POOL * CELLS), F32), pltpu.SMEM((tiles,), jnp.int32),
                        pltpu.SemaphoreType.DMA((2, 2)), pltpu.SemaphoreType.DMA],
        compiler_params=PARAMS,
        name="send_rows",
    )(here, *[in_hbm(x) for x in (lower_edge_quarter_turns, u_velocity, v_velocity)])
    up, down, u_velocity, v_velocity = lax.optimization_barrier((up, down, u_velocity, v_velocity))
    above = lax.ppermute(down, "tile", onward(tiles))
    below = lax.ppermute(up, "tile", back(tiles))
    column = lambda c: pl.BlockSpec((POOL * CELLS, LANES), lambda i: (0, c))
    rows = 2 * POOL * CELLS
    parts, weights, rim, early = pl.pallas_call(
        prepare_kernel,
        out_shape=[jax.ShapeDtypeStruct((rows, 2 * POOL * CELLS), BF16),
                   jax.ShapeDtypeStruct((POOL * CELLS, 10 * LANES), BF16), struct(FULL, LANES),
                   struct(rows, EARLY * LANES)],
        grid=(1,),
        in_specs=[column(c) for c in range(4)] * 2 + [HBM],
        out_specs=[VMEM] * 4,
        scratch_shapes=[pltpu.VMEM((rows, 2 * LANES), BF16)] + [pltpu.VMEM((POOL, PAD + CELLS, LANES), F32)] * 2
        + [pltpu.SemaphoreType.DMA],
        compiler_params=PARAMS,
        name="prepare_rows",
    )(*[u_velocity] * 4, *[v_velocity] * 4, in_hbm(jnp.asarray(column_weights())))
    to_left, to_right, own = pl.pallas_call(
        rim_kernel,
        out_shape=[struct(8, FULL), struct(8, FULL), struct(16, FULL)],
        in_specs=[VMEM] * 4,
        out_specs=[VMEM] * 3,
        scratch_shapes=[pltpu.VMEM((2, 2 * HALO, LANES), F32), pltpu.VMEM((2 * 2 * POOL * 8, LANES), F32),
                        pltpu.VMEM((FULL, LANES), F32)],
        compiler_params=PARAMS,
        name="rim_columns",
    )(above, below, weights, rim)
    from_right = lax.ppermute(to_left, "col", back(columns))
    from_left = lax.ppermute(to_right, "col", onward(columns))
    main, live, inner = pl.pallas_call(
        main_kernel,
        out_shape=[struct(2, FULL, LANES), struct(CELLS, LANES), struct(len(PAIRS), 8, LANES)],
        in_specs=[SMEM] + [VMEM] * 6,
        out_specs=[VMEM] * 3,
        scratch_shapes=[pltpu.VMEM((2, 4, 2 * HALO, LANES), F32), pltpu.VMEM((2 * POOL * 16, POOL * CELLS), F32),
                        pltpu.VMEM((2, POOL, FULL, LANES), F32), pltpu.VMEM((TERMS, CELLS, LANES), F32)],
        compiler_params=PARAMS,
        name="main_columns",
    )(ocean_mask, parts, early, weights, above, below, own)
    blocks = pl.pallas_call(
        base_kernel,
        out_shape=struct(tiles, BLOCK_ROWS, LANES),
        in_specs=[VMEM] * 9,
        out_specs=VMEM,
        scratch_shapes=[pltpu.VMEM((2, FULL, LANES), F32), pltpu.VMEM((TERMS * TERMS, LANES), F32),
                        pltpu.VMEM((17, BLOCK_ROWS, LANES), F32), pltpu.SMEM((tiles + 1,), jnp.int32),
                        pltpu.VMEM((LANES, CELLS), F32), pltpu.SMEM(ocean_mask.shape, jnp.int32),
                        pltpu.SMEM(tile_owner.shape, jnp.int32), pltpu.SemaphoreType.DMA((2,))],
        compiler_params=PARAMS,
        name="base_fields",
    )(ocean_mask, tile_owner, main, live, inner, own, from_left, from_right, jnp.asarray(place_matrix()))
    blocks = lax.all_to_all(blocks, "tile", split_axis=0, concat_axis=0, tiled=True)
    gram = jnp.sum(blocks[:, GRAM : GRAM + 2], axis=0)
    gram = lax.all_to_all(jnp.broadcast_to(gram, (columns, 2, LANES)), "col", split_axis=0, concat_axis=0, tiled=True)
    library = pl.pallas_call(
        library_kernel,
        out_shape=struct(tiles * TERMS, SIDE * SIDE),
        in_specs=[VMEM],
        out_specs=HBM,
        scratch_shapes=[pltpu.VMEM((8, tiles * TERMS, LANES), F32), pltpu.SemaphoreType.DMA((8,))],
        compiler_params=PARAMS,
        cost_estimate=pl.CostEstimate(flops=2 * tiles * TERMS * SIDE * SIDE, transcendentals=0,
                                      bytes_accessed=5 * tiles * TERMS * SIDE * SIDE),
        name="library_terms",
    )(blocks.reshape(tiles * BLOCK_ROWS, LANES))
    gram = jnp.sum(gram, axis=0).reshape(TERMS, TERMS) / (CELLS * CELLS)
    return library.reshape(1, 1, tiles, TERMS, SIDE * SIDE), gram


def solution(mesh):
    in_specs = (P("tile", "col"), P("tile", "col"), P("tile", "col"), P("tile", "col"), P())
    out_specs = (P("tile", "col", None, None, None), P())
    return jax.shard_map(
        per_device, mesh=mesh, in_specs=in_specs, out_specs=out_specs, check_vma=False
    )
```

```python
import math

import jax
import jax.numpy as jnp
import ml_dtypes
import numpy as np
from jax import lax
from jax.experimental import pallas as pl
from jax.experimental.pallas import tpu as pltpu
from jax.sharding import PartitionSpec as P

PASSES = 8
KAPPA = 0.2
POOL = 4
CELLS = 128
HALO = 12
SIDE = 32
TERMS = 16
PAD = 8
FULL = CELLS + 2 * PAD
LANES = 128
BASES = 5
BLOCK_ROWS = 24
SIDES, ENDS, GRAM = 16, 17, 18
F32 = jnp.float32
BF16 = jnp.bfloat16

SCALE = KAPPA**PASSES / (POOL * POOL)
RIM_COLS = (-2, -1, 0, CELLS - 1, CELLS, CELLS + 1)


def across(power, fine, coarse):
    total = 0
    for inner in range(POOL):
        offset = fine - (POOL * coarse + inner)
        if abs(offset) <= power and (power + offset) % 2 == 0:
            total += math.comb(power, (power + offset) // 2)
    return total


def column_weights():
    fine = CELLS * POOL
    main = np.zeros((fine, 9 * LANES), np.float32)
    rim = np.zeros((fine, LANES), np.float32)
    for j in range(PASSES + 1):
        for coarse in range(-2, CELLS + 2):
            for f in range(max(0, POOL * coarse - PASSES), min(fine, POOL * coarse + POOL + PASSES)):
                value = math.comb(PASSES, j) * across(PASSES - j, f, coarse)
                if 0 <= coarse < CELLS:
                    main[f, (PASSES - j) * LANES + coarse] = value
                if coarse in RIM_COLS:
                    rim[f, 6 * j + RIM_COLS.index(coarse)] = value
    assert not rim[64 : fine - 64].any()
    rim[LANES - 64 : LANES] = rim[fine - 64 :]
    rim[LANES : 2 * LANES] = rim[:LANES]
    weights = np.concatenate([main, rim], axis=1)
    out = weights.astype(ml_dtypes.bfloat16)
    assert (out.astype(np.float32) == weights).all()
    return out


def rim_selector():
    row = lax.broadcasted_iota(jnp.int32, (32, 1), 0)
    source = jnp.full((32, 1), -1, jnp.int32)
    for f in range(2):
        for c in range(3):
            source = jnp.where(row == 3 * f + c, 64 * f + c, source)
            source = jnp.where(row == 8 + 3 * f + c, 64 * f + 3 + c, source)
        source = jnp.where(row == 16 + 2 * f, 64 * f + 1, source)
        source = jnp.where(row == 17 + 2 * f, 64 * f + 4, source)
    lane = lax.broadcasted_iota(jnp.int32, (32, 3 * LANES), 1) % LANES
    return jnp.where(lane == source, 1.0, 0.0).astype(BF16)


def place_matrix():
    place = np.zeros((3, 32, 4 * LANES), np.float32)
    for f in range(2):
        add, rim = 2 * f * LANES, (2 * f + 1) * LANES
        place[:, 3 * f + 0, rim + 0] = 1.0
        place[:, 3 * f + 1, add + 0] = 1.0
        place[:, 3 * f + 2, add + 1] = 1.0
        place[:, 8 + 3 * f + 0, add + CELLS - 2] = 1.0
        place[:, 8 + 3 * f + 1, add + CELLS - 1] = 1.0
        place[:, 8 + 3 * f + 2, rim + CELLS - 1] = 1.0
        place[:, 16 + 2 * f, rim + 0] = 1.0
        place[:, 17 + 2 * f, rim + CELLS - 1] = 1.0
    return place.reshape(96, 4 * LANES).astype(ml_dtypes.bfloat16)


def head(x):
    scaled = x * 65537.0
    return scaled - (scaled - x)


def two_parts(x):
    high = head(x)
    return high.astype(BF16), (x - high).astype(BF16)


def three_parts(x):
    high = head(x)
    rest = x - high
    mid = head(rest)
    return high.astype(BF16), mid.astype(BF16), (rest - mid).astype(BF16)


def dot(a, b, dims=(((1,), (0,)), ((), ()))):
    return lax.dot_general(a, b, dims, preferred_element_type=F32)


def three_rows(t):
    rows = t[0].shape[0]
    up = pltpu.roll(t[3], 1, 0)
    down = pltpu.roll(t[0], rows - 1, 0)
    left, middle, right = t[0] + t[1], t[1] + t[2], t[2] + t[3]
    return [left + up, t[0] + middle, middle + t[3], right + down]


def turn(first, second, k):
    cosine = jnp.where(k == 0, 1.0, jnp.where(k == 2, -1.0, 0.0)).astype(F32)
    sine = jnp.where(k == 1, 1.0, jnp.where(k == 3, -1.0, 0.0)).astype(F32)
    return cosine * first - sine * second, sine * first + cosine * second


def send_kernel(here_ref, turns_hbm, u_hbm, v_hbm, up_ref, down_ref, x_ref, turns_ref, sem, turns_sem):
    rows = u_hbm.shape[0]
    copies = [pltpu.make_async_copy(hbm.at[pl.ds(start, 16)], x_ref.at[side, f], sem.at[side, f])
              for side, start in enumerate((0, rows - 16)) for f, hbm in enumerate((u_hbm, v_hbm))]
    table = pltpu.make_async_copy(turns_hbm, turns_ref, turns_sem)
    table.start()
    for copy in copies:
        copy.start()
    table.wait()
    tiles = turns_ref.shape[0]
    here = here_ref[0]
    k_up = lax.rem(4 - turns_ref[here], 4)
    k_down = turns_ref[lax.rem(here + 1, tiles)]
    for copy in copies:
        copy.wait()
    for side, (to_ref, k, start) in enumerate(((up_ref, k_up, 0), (down_ref, k_down, 16 - HALO))):
        for f, x in enumerate(turn(x_ref[side, 0], x_ref[side, 1], k)):
            to_ref[f * HALO : (f + 1) * HALO] = x[start : start + HALO]


EARLY = 6


def prepare_kernel(*refs):
    w_hbm, parts_ref, w_out, rim_ref, early_ref, rim_parts_ref, first_ref, last_ref, sem = refs[8:]
    copy = pltpu.make_async_copy(w_hbm, w_out, sem)
    copy.start()
    lane = lax.broadcasted_iota(jnp.int32, (1, LANES), 1)
    fine = POOL * CELLS
    for f in range(2):
        for p in range(POOL):
            spot = slice((f * POOL + p) * CELLS, (f * POOL + p + 1) * CELLS)
            pieces = [two_parts(refs[4 * f + c][pl.ds(p, CELLS, stride=POOL), :]) for c in range(4)]
            for part in range(2):
                for c in range(4):
                    parts_ref[spot, part * fine + c * LANES : part * fine + (c + 1) * LANES] = pieces[c][part]
                rim_parts_ref[spot, part * LANES : (part + 1) * LANES] = jnp.where(
                    lane < 64, pieces[0][part], pieces[3][part])
    copy.wait()
    z = dot(rim_parts_ref[...], w_out[: 2 * LANES, 9 * LANES :])
    for p in range(POOL):
        u, v = [z[(f * POOL + p) * CELLS : (f * POOL + p + 1) * CELLS] for f in range(2)]
        both = jnp.where(lane < 64, u, pltpu.roll(v, 64, 1))
        for to_ref in (first_ref, last_ref):
            to_ref[p, :PAD] = jnp.zeros((PAD, LANES), F32)
            to_ref[p, PAD:] = both
    for _ in range(PASSES):
        new = three_rows([pltpu.roll(last_ref[p], LANES - 6, 1) for p in range(POOL)])
        for p in range(POOL):
            last_ref[p] = new[p] + first_ref[p]
    pooled = ((last_ref[0] + last_ref[1]) + (last_ref[2] + last_ref[3])) * SCALE
    rim_ref[: PAD + CELLS] = pooled
    rim_ref[PAD + CELLS :] = pooled[:PAD]
    for start in range(0, EARLY, 2):
        cut = slice(start * LANES, (start + 2) * LANES)
        early_ref[:, cut] = dot(parts_ref[:, :fine], w_out[:, cut]) + dot(parts_ref[:, fine:], w_out[:, cut])


def rim_kernel(above_ref, below_ref, w_ref, rim_in, left_ref, right_ref, own_ref, rows_ref, strip_ref, rim_ref):
    lane = lax.broadcasted_iota(jnp.int32, (1, LANES), 1)
    strip_ref[...] = jnp.zeros_like(strip_ref)
    for s, (x_ref, start) in enumerate(((above_ref, 1), (below_ref, 4))):
        ends = jnp.where(lane < 64, x_ref[:, :LANES], x_ref[:, 3 * LANES :])
        rows_ref[s] = ends
        for f in range(2):
            for p in range(POOL):
                spot = ((f * 2 + s) * POOL + p) * 8 + start
                strip_ref[spot : spot + 3] = rows_ref[s, pl.ds(f * HALO + p, 3, stride=POOL), :]
    z = dot(jnp.concatenate(two_parts(strip_ref[...]), axis=1), w_ref[: 2 * LANES, 9 * LANES :])
    rim_ref[...] = rim_in[...]
    for s, (spot, start) in enumerate(((7, 3), (PAD + CELLS - 2, 2))):
        first = []
        for p in range(POOL):
            u, v = [z[((f * 2 + s) * POOL + p) * 8 : ((f * 2 + s) * POOL + p + 1) * 8] for f in range(2)]
            first.append(jnp.where(lane < 64, u, pltpu.roll(v, 64, 1)))
        powers = [first] + [[pltpu.roll(x, LANES - 6 * j, 1) for x in first] for j in range(1, PASSES + 1)]
        last = powers[PASSES]
        for j in range(PASSES - 1, -1, -1):
            last = [a + b for a, b in zip(three_rows(last), powers[j])]
        pooled = ((last[0] + last[1]) + (last[2] + last[3])) * SCALE
        rim_ref[spot : spot + 3] = rim_ref[spot : spot + 3] + pooled[start : start + 3]
    turned = jnp.transpose(rim_ref[...])
    for to_ref, columns in ((left_ref, (0, 1, 2)), (right_ref, (3, 4, 5)), (own_ref, (1, 4))):
        to_ref[...] = jnp.zeros_like(to_ref)
        for f in range(2):
            for place, c in enumerate(columns):
                spot = len(columns) * f + place
                to_ref[spot : spot + 1] = turned[64 * f + c : 64 * f + c + 1]


PAIRS = [(n, m) for n in range(TERMS) for m in range(n, TERMS)]
REACH = 3


def slopes_of(ref, f, left, right):
    up = ref[f, PAD - 1 : PAD - 1 + CELLS]
    down = ref[f, PAD + 1 : PAD + 1 + CELLS]
    return (right - left) * 0.5, (down - up) * 0.5


def main_kernel(mask_ref, parts_ref, early_ref, w_ref, above_ref, below_ref, _, main_ref, live_ref, inner_ref, rows_ref,
                strip_ref, sum_ref, term_ref):
    strip_ref[...] = jnp.zeros_like(strip_ref)
    for s, (x_ref, start) in enumerate(((above_ref, 5), (below_ref, 8))):
        for c in range(4):
            cut = slice(c * LANES, (c + 1) * LANES)
            rows_ref[s, c] = x_ref[:, cut]
            for f in range(2):
                for p in range(POOL):
                    spot = (f * POOL + p) * 16 + start
                    strip_ref[spot : spot + 3, cut] = rows_ref[s, c, pl.ds(f * HALO + p, 3, stride=POOL), :]
    strips = jnp.concatenate(two_parts(strip_ref[...]), axis=1)
    fine = POOL * CELLS
    for start in range(0, 9, 2):
        wide = min(2, 9 - start)
        w = w_ref[:, start * LANES : (start + wide) * LANES]
        if start < EARLY:
            z = early_ref[:, start * LANES : (start + wide) * LANES]
        else:
            z = dot(parts_ref[:, :fine], w) + dot(parts_ref[:, fine:], w)
        z_strip = dot(strips[:, :fine], w) + dot(strips[:, fine:], w)
        for stage in range(start, start + wide):
            cut = slice((stage - start) * LANES, (stage - start + 1) * LANES)
            for f in range(2):
                own = []
                for p in range(POOL):
                    block = f * POOL + p
                    own.append(jnp.concatenate([
                        z_strip[block * 16 : block * 16 + 8, cut], z[block * CELLS : (block + 1) * CELLS, cut],
                        z_strip[block * 16 + 8 : block * 16 + 16, cut]], axis=0))
                if stage:
                    own = [a + b for a, b in zip(three_rows([sum_ref[f, p] for p in range(POOL)]), own)]
                for p in range(POOL):
                    sum_ref[f, p] = own[p]
    for f in range(2):
        main_ref[f] = ((sum_ref[f, 0] + sum_ref[f, 1]) + (sum_ref[f, 2] + sum_ref[f, 3])) * SCALE
    lane = lax.broadcasted_iota(jnp.int32, (1, LANES), 1)
    grid = CELLS // SIDE
    for a in range(grid):
        row = jnp.zeros((1, LANES), F32)
        for e in range(grid):
            row = jnp.where(lane // SIDE == e, (mask_ref[a, e] == 1).astype(F32), row)
        live_ref[a * SIDE : (a + 1) * SIDE] = jnp.broadcast_to(row, (SIDE, LANES))
    keep = (live_ref[...] > 0.5) & (lane >= REACH) & (lane < LANES - REACH)
    u, v = [main_ref[f, PAD : PAD + CELLS] for f in range(2)]
    (u_dx, u_dy), (v_dx, v_dy) = [slopes_of(main_ref, f, pltpu.roll(x, 1, 1), pltpu.roll(x, LANES - 1, 1))
                                  for f, x in enumerate((u, v))]
    for n, x in enumerate((u, v, v_dx - u_dy, u_dy + v_dx, u_dx - v_dy)):
        term_ref[n] = jnp.where(keep, x, 0.0)
    for n, x in enumerate(terms_of([term_ref[n] for n in range(BASES)])):
        if n >= BASES:
            term_ref[n] = x
    for place, (n, m) in enumerate(PAIRS):
        product = (term_ref[n] * term_ref[m]).reshape(CELLS // 8, 8, LANES)
        inner_ref[place] = jnp.sum(product, axis=0)


def base_kernel(mask_vmem, owner_vmem, main_ref, live_ref, inner_ref, own_ref, from_left_ref, from_right_ref, place_ref,
                out_ref, field_ref, gram_ref, pack_ref, tile_ref, side_ref, mask_ref, owner_ref, sem):
    tables = [pltpu.make_async_copy(mask_vmem, mask_ref, sem.at[0]),
              pltpu.make_async_copy(owner_vmem, owner_ref, sem.at[1])]
    for table in tables:
        table.start()
    lane = lax.broadcasted_iota(jnp.int32, (1, LANES), 1)
    received = jnp.concatenate([from_left_ref[...], from_right_ref[...], own_ref[...]], axis=0)
    placed = dot(jnp.concatenate(three_parts(received), axis=0), place_ref[...], (((0,), (0,)), ((), ())))
    inner = slice(PAD, PAD + CELLS)
    slopes, beside = [], []
    for f in range(2):
        full = main_ref[f] + placed[:, 2 * f * LANES : (2 * f + 1) * LANES]
        field_ref[f] = full
        rim = placed[inner, (2 * f + 1) * LANES : (2 * f + 2) * LANES]
        centre = full[inner]
        left = jnp.where(lane == 0, rim, pltpu.roll(centre, 1, 1))
        right = jnp.where(lane == LANES - 1, rim, pltpu.roll(centre, LANES - 1, 1))
        beside.append((left, right))
        slopes.append((centre, *slopes_of(field_ref, f, left, right)))
    (u, u_dx, u_dy), (v, v_dx, v_dy) = slopes
    live = live_ref[...] > 0.5
    outer = []
    for x in (u, v, v_dx - u_dy, u_dy + v_dx, u_dx - v_dy):
        x = jnp.where(live, x, 0.0)
        tile = jnp.zeros((8, LANES), F32)
        for b in range(CELLS // 8):
            tile = jnp.where(lane // 8 == b, pltpu.roll(x[8 * b : 8 * b + 8], (REACH + 8 * b) % LANES, 1), tile)
        outer.append(jnp.where(lane % 8 < 2 * REACH, tile, 0.0))
    outer = terms_of(outer)
    for place, (n, m) in enumerate(PAIRS):
        total = jnp.sum(inner_ref[place] + outer[n] * outer[m], axis=0, keepdims=True)
        gram_ref[n * TERMS + m : n * TERMS + m + 1] = total
        if m > n:
            gram_ref[m * TERMS + n : m * TERMS + n + 1] = total
    totals = jnp.sum(gram_ref[...], axis=1, keepdims=True) * (1.0 / (CELLS * CELLS))
    row = lax.broadcasted_iota(jnp.int32, (TERMS * TERMS, 1), 0)
    spread = jnp.where(row % LANES == lane, totals, 0.0)
    halves = [jnp.sum(spread[h * LANES : (h + 1) * LANES], axis=0, keepdims=True) for h in range(2)]
    owners = out_ref.shape[0]
    grid = CELLS // SIDE
    nothing = grid * grid
    for table in tables:
        table.wait()
    for o in range(owners + 1):
        tile_ref[o] = nothing
    for a in range(grid):
        for e in range(grid):
            tile_ref[jnp.where(mask_ref[a, e] == 1, owner_ref[a, e], owners)] = a * grid + e
    pack_ref[nothing] = jnp.zeros((BLOCK_ROWS, LANES), F32)
    group = lane // SIDE
    rims = jnp.where(lane % SIDE == 0, beside[0][0], pltpu.roll(beside[1][0], 1, 1))
    rims = jnp.where(lane % SIDE == SIDE - 1, beside[0][1], rims)
    side_ref[...] = jnp.transpose(jnp.where(lane % SIDE == SIDE - 2, pltpu.roll(beside[1][1], LANES - 1, 1), rims))
    for a in range(grid):
        ends = []
        for f in range(2):
            pieces = [field_ref[f, pl.ds(PAD + a * SIDE + q, 8, stride=4), :] for q in range(grid)]
            for e in range(grid):
                block = None
                for q in range(grid):
                    x = pltpu.roll(pieces[q], (q - e) % grid * SIDE, 1) if q != e else pieces[q]
                    block = x if block is None else jnp.where(group == q, x, block)
                pack_ref[a * grid + e, 8 * f : 8 * f + 8] = block
            for side in range(2):
                ends.append(field_ref[f, PAD + a * SIDE - 1 + side * (SIDE + 1) : PAD + a * SIDE + side * (SIDE + 1)])
        for e in range(grid):
            sides = [side_ref[e * SIDE + at : e * SIDE + at + 1] for at in (0, SIDE - 1, 1, SIDE - 2)]
            for spot, parts, own in ((SIDES, sides, a), (ENDS, ends, e)):
                row = None
                for q in range(4):
                    x = pltpu.roll(parts[q], (q - own) % 4 * SIDE, 1) if q != own else parts[q]
                    row = x if row is None else jnp.where(group == q, x, row)
                pack_ref[a * grid + e, spot : spot + 1] = row
    for o in range(owners):
        out_ref[o] = pack_ref[tile_ref[o]]
        for h in range(2):
            out_ref[o, GRAM + h : GRAM + h + 1] = halves[h]


def terms_of(base):
    u, v, vort, strain, stretch = base
    return [u, v, vort, strain, stretch, vort * vort, vort * strain, vort * stretch, strain * strain, stretch * stretch,
            strain * stretch, u * vort, v * vort, u * strain, v * stretch, u * v]


def library_kernel(x_ref, out_hbm, out_ref, sem):
    slots = x_ref.shape[0] // BLOCK_ROWS
    rows = lambda at: x_ref[pl.ds(at, slots, stride=BLOCK_ROWS), :]
    turn_by = lambda x, count: pltpu.roll(x, count % LANES, 1) if count % LANES else x
    lane = lax.broadcasted_iota(jnp.int32, (1, LANES), 1)
    sides, ends = rows(SIDES), rows(ENDS)
    fields = [[rows(8 * f + k) for k in range(8)] for f in range(2)]
    lower = [[turn_by(x, SIDE) for x in field] for field in fields]
    higher = [[turn_by(x, -SIDE) for x in field] for field in fields]

    def slopes(f, k):
        x = fields[f][k]
        left, right = turn_by(x, 1), turn_by(x, -1)
        for q in range(4):
            start = 64 * f + 4 * k + q
            left = jnp.where(lane == SIDE * q, turn_by(sides, SIDE * q - start), left)
            right = jnp.where(lane == SIDE * (q + 1) - 1, turn_by(sides, SIDE * q - 1 - start), right)
        before = lower[f][k - 1] if k else turn_by(ends, -64 * f)
        after = higher[f][k + 1] if k < 7 else turn_by(ends, 64 - 64 * f)
        up = jnp.where(lane < SIDE, before, lower[f][k])
        down = jnp.where(lane >= LANES - SIDE, after, higher[f][k])
        return (right - left) * 0.5, (down - up) * 0.5

    copies = []
    for k in range(8):
        (u_dx, u_dy), (v_dx, v_dy) = slopes(0, k), slopes(1, k)
        base = [fields[0][k], fields[1][k], v_dx - u_dy, u_dy + v_dx, u_dx - v_dy]
        for n, x in enumerate(terms_of(base)):
            out_ref[k, pl.ds(n, slots, stride=TERMS), :] = x
        copies.append(pltpu.make_async_copy(out_ref.at[k], out_hbm.at[:, pl.ds(k * LANES, LANES)], sem.at[k]))
        copies[k].start()
    for copy in copies:
        copy.wait()


VMEM = pl.BlockSpec(memory_space=pltpu.VMEM)
HBM = pl.BlockSpec(memory_space=pltpu.HBM)
SMEM = pl.BlockSpec(memory_space=pltpu.SMEM)
PARAMS = pltpu.CompilerParams(vmem_limit_bytes=24 << 20)


def struct(*shape):
    return jax.ShapeDtypeStruct(shape, F32)


def per_device(u_velocity, v_velocity, ocean_mask, tile_owner, lower_edge_quarter_turns):
    tiles, columns = lax.axis_size("tile"), lax.axis_size("col")
    onward = lambda count: [(i, (i + 1) % count) for i in range(count)]
    back = lambda count: [((i + 1) % count, i) for i in range(count)]
    here = lax.axis_index("tile").astype(jnp.int32)[None]
    in_hbm = lambda x: pltpu.with_memory_space_constraint(x, pltpu.HBM)
    up, down = pl.pallas_call(
        send_kernel,
        out_shape=[struct(2 * HALO, POOL * CELLS)] * 2,
        in_specs=[SMEM] + [HBM] * 3,
        out_specs=[VMEM] * 2,
        scratch_shapes=[pltpu.VMEM((2, 2, 16, POOL * CELLS), F32), pltpu.SMEM((tiles,), jnp.int32),
                        pltpu.SemaphoreType.DMA((2, 2)), pltpu.SemaphoreType.DMA],
        compiler_params=PARAMS,
        name="send_rows",
    )(here, *[in_hbm(x) for x in (lower_edge_quarter_turns, u_velocity, v_velocity)])
    up, down, u_velocity, v_velocity = lax.optimization_barrier((up, down, u_velocity, v_velocity))
    above = lax.ppermute(down, "tile", onward(tiles))
    below = lax.ppermute(up, "tile", back(tiles))
    column = lambda c: pl.BlockSpec((POOL * CELLS, LANES), lambda i: (0, c))
    rows = 2 * POOL * CELLS
    parts, weights, rim, early = pl.pallas_call(
        prepare_kernel,
        out_shape=[jax.ShapeDtypeStruct((rows, 2 * POOL * CELLS), BF16),
                   jax.ShapeDtypeStruct((POOL * CELLS, 10 * LANES), BF16), struct(FULL, LANES),
                   struct(rows, EARLY * LANES)],
        grid=(1,),
        in_specs=[column(c) for c in range(4)] * 2 + [HBM],
        out_specs=[VMEM] * 4,
        scratch_shapes=[pltpu.VMEM((rows, 2 * LANES), BF16)] + [pltpu.VMEM((POOL, PAD + CELLS, LANES), F32)] * 2
        + [pltpu.SemaphoreType.DMA],
        compiler_params=PARAMS,
        name="prepare_rows",
    )(*[u_velocity] * 4, *[v_velocity] * 4, in_hbm(jnp.asarray(column_weights())))
    to_left, to_right, own = pl.pallas_call(
        rim_kernel,
        out_shape=[struct(8, FULL), struct(8, FULL), struct(16, FULL)],
        in_specs=[VMEM] * 4,
        out_specs=[VMEM] * 3,
        scratch_shapes=[pltpu.VMEM((2, 2 * HALO, LANES), F32), pltpu.VMEM((2 * 2 * POOL * 8, LANES), F32),
                        pltpu.VMEM((FULL, LANES), F32)],
        compiler_params=PARAMS,
        name="rim_columns",
    )(above, below, weights, rim)
    from_right = lax.ppermute(to_left, "col", back(columns))
    from_left = lax.ppermute(to_right, "col", onward(columns))
    main, live, inner = pl.pallas_call(
        main_kernel,
        out_shape=[struct(2, FULL, LANES), struct(CELLS, LANES), struct(len(PAIRS), 8, LANES)],
        in_specs=[SMEM] + [VMEM] * 6,
        out_specs=[VMEM] * 3,
        scratch_shapes=[pltpu.VMEM((2, 4, 2 * HALO, LANES), F32), pltpu.VMEM((2 * POOL * 16, POOL * CELLS), F32),
                        pltpu.VMEM((2, POOL, FULL, LANES), F32), pltpu.VMEM((TERMS, CELLS, LANES), F32)],
        compiler_params=PARAMS,
        name="main_columns",
    )(ocean_mask, parts, early, weights, above, below, own)
    blocks = pl.pallas_call(
        base_kernel,
        out_shape=struct(tiles, BLOCK_ROWS, LANES),
        in_specs=[VMEM] * 9,
        out_specs=VMEM,
        scratch_shapes=[pltpu.VMEM((2, FULL, LANES), F32), pltpu.VMEM((TERMS * TERMS, LANES), F32),
                        pltpu.VMEM((17, BLOCK_ROWS, LANES), F32), pltpu.SMEM((tiles + 1,), jnp.int32),
                        pltpu.VMEM((LANES, CELLS), F32), pltpu.SMEM(ocean_mask.shape, jnp.int32),
                        pltpu.SMEM(tile_owner.shape, jnp.int32), pltpu.SemaphoreType.DMA((2,))],
        compiler_params=PARAMS,
        name="base_fields",
    )(ocean_mask, tile_owner, main, live, inner, own, from_left, from_right, jnp.asarray(place_matrix()))
    blocks = lax.all_to_all(blocks, "tile", split_axis=0, concat_axis=0, tiled=True)
    gram = jnp.sum(blocks[:, GRAM : GRAM + 2], axis=0)
    gram = lax.all_to_all(jnp.broadcast_to(gram, (columns, 2, LANES)), "col", split_axis=0, concat_axis=0, tiled=True)
    library = pl.pallas_call(
        library_kernel,
        out_shape=struct(tiles * TERMS, SIDE * SIDE),
        in_specs=[VMEM],
        out_specs=HBM,
        scratch_shapes=[pltpu.VMEM((8, tiles * TERMS, LANES), F32), pltpu.SemaphoreType.DMA((8,))],
        compiler_params=PARAMS,
        cost_estimate=pl.CostEstimate(flops=2 * tiles * TERMS * SIDE * SIDE, transcendentals=0,
                                      bytes_accessed=5 * tiles * TERMS * SIDE * SIDE),
        name="library_terms",
    )(blocks.reshape(tiles * BLOCK_ROWS, LANES))
    gram = jnp.sum(gram, axis=0).reshape(TERMS, TERMS)
    return library.reshape(1, 1, tiles, TERMS, SIDE * SIDE), gram


def solution(mesh):
    in_specs = (P("tile", "col"), P("tile", "col"), P("tile", "col"), P("tile", "col"), P())
    out_specs = (P("tile", "col", None, None, None), P())
    return jax.shard_map(
        per_device, mesh=mesh, in_specs=in_specs, out_specs=out_specs, check_vma=False
    )
```

```python
import math

import jax
import jax.numpy as jnp
import ml_dtypes
import numpy as np
from jax import lax
from jax.experimental import pallas as pl
from jax.experimental.pallas import tpu as pltpu
from jax.sharding import PartitionSpec as P

PASSES = 8
KAPPA = 0.2
POOL = 4
CELLS = 128
HALO = 12
SIDE = 32
TERMS = 16
PAD = 8
FULL = CELLS + 2 * PAD
LANES = 128
BASES = 5
BLOCK_ROWS = 24
SIDES, ENDS, GRAM = 16, 17, 18
F32 = jnp.float32
BF16 = jnp.bfloat16

SCALE = KAPPA**PASSES / (POOL * POOL)
RIM_COLS = (-2, -1, 0, CELLS - 1, CELLS, CELLS + 1)


def across(power, fine, coarse):
    total = 0
    for inner in range(POOL):
        offset = fine - (POOL * coarse + inner)
        if abs(offset) <= power and (power + offset) % 2 == 0:
            total += math.comb(power, (power + offset) // 2)
    return total


def column_weights():
    fine = CELLS * POOL
    main = np.zeros((fine, 9 * LANES), np.float32)
    rim = np.zeros((fine, LANES), np.float32)
    for j in range(PASSES + 1):
        for coarse in range(-2, CELLS + 2):
            for f in range(max(0, POOL * coarse - PASSES), min(fine, POOL * coarse + POOL + PASSES)):
                value = math.comb(PASSES, j) * across(PASSES - j, f, coarse)
                if 0 <= coarse < CELLS:
                    main[f, (PASSES - j) * LANES + coarse] = value
                if coarse in RIM_COLS:
                    rim[f, 6 * j + RIM_COLS.index(coarse)] = value
    assert not rim[64 : fine - 64].any()
    rim[LANES - 64 : LANES] = rim[fine - 64 :]
    rim[LANES : 2 * LANES] = rim[:LANES]
    weights = np.concatenate([main, rim], axis=1)
    out = weights.astype(ml_dtypes.bfloat16)
    assert (out.astype(np.float32) == weights).all()
    return out


def rim_selector():
    row = lax.broadcasted_iota(jnp.int32, (32, 1), 0)
    source = jnp.full((32, 1), -1, jnp.int32)
    for f in range(2):
        for c in range(3):
            source = jnp.where(row == 3 * f + c, 64 * f + c, source)
            source = jnp.where(row == 8 + 3 * f + c, 64 * f + 3 + c, source)
        source = jnp.where(row == 16 + 2 * f, 64 * f + 1, source)
        source = jnp.where(row == 17 + 2 * f, 64 * f + 4, source)
    lane = lax.broadcasted_iota(jnp.int32, (32, 3 * LANES), 1) % LANES
    return jnp.where(lane == source, 1.0, 0.0).astype(BF16)


def place_matrix():
    place = np.zeros((3, 32, 4 * LANES), np.float32)
    for f in range(2):
        add, rim = 2 * f * LANES, (2 * f + 1) * LANES
        place[:, 3 * f + 0, rim + 0] = 1.0
        place[:, 3 * f + 1, add + 0] = 1.0
        place[:, 3 * f + 2, add + 1] = 1.0
        place[:, 8 + 3 * f + 0, add + CELLS - 2] = 1.0
        place[:, 8 + 3 * f + 1, add + CELLS - 1] = 1.0
        place[:, 8 + 3 * f + 2, rim + CELLS - 1] = 1.0
        place[:, 16 + 2 * f, rim + 0] = 1.0
        place[:, 17 + 2 * f, rim + CELLS - 1] = 1.0
    return place.reshape(96, 4 * LANES).astype(ml_dtypes.bfloat16)


def head(x):
    scaled = x * 65537.0
    return scaled - (scaled - x)


def two_parts(x):
    high = head(x)
    return high.astype(BF16), (x - high).astype(BF16)


def three_parts(x):
    high = head(x)
    rest = x - high
    mid = head(rest)
    return high.astype(BF16), mid.astype(BF16), (rest - mid).astype(BF16)


def dot(a, b, dims=(((1,), (0,)), ((), ()))):
    return lax.dot_general(a, b, dims, preferred_element_type=F32)


def three_rows(t):
    rows = t[0].shape[0]
    up = pltpu.roll(t[3], 1, 0)
    down = pltpu.roll(t[0], rows - 1, 0)
    left, middle, right = t[0] + t[1], t[1] + t[2], t[2] + t[3]
    return [left + up, t[0] + middle, middle + t[3], right + down]


def turn(first, second, k):
    cosine = jnp.where(k == 0, 1.0, jnp.where(k == 2, -1.0, 0.0)).astype(F32)
    sine = jnp.where(k == 1, 1.0, jnp.where(k == 3, -1.0, 0.0)).astype(F32)
    return cosine * first - sine * second, sine * first + cosine * second


def send_kernel(here_ref, turns_hbm, u_hbm, v_hbm, up_ref, down_ref, x_ref, turns_ref, sem, turns_sem):
    rows = u_hbm.shape[0]
    copies = [pltpu.make_async_copy(hbm.at[pl.ds(start, 16)], x_ref.at[side, f], sem.at[side, f])
              for side, start in enumerate((0, rows - 16)) for f, hbm in enumerate((u_hbm, v_hbm))]
    table = pltpu.make_async_copy(turns_hbm, turns_ref, turns_sem)
    table.start()
    for copy in copies:
        copy.start()
    table.wait()
    tiles = turns_ref.shape[0]
    here = here_ref[0]
    k_up = lax.rem(4 - turns_ref[here], 4)
    k_down = turns_ref[lax.rem(here + 1, tiles)]
    for copy in copies:
        copy.wait()
    for side, (to_ref, k, start) in enumerate(((up_ref, k_up, 0), (down_ref, k_down, 16 - HALO))):
        for f, x in enumerate(turn(x_ref[side, 0], x_ref[side, 1], k)):
            to_ref[f * HALO : (f + 1) * HALO] = x[start : start + HALO]


EARLY = 6


def prepare_kernel(*refs):
    w_hbm, parts_ref, w_out, rim_ref, early_ref, rim_parts_ref, first_ref, last_ref, sem = refs[8:]
    copy = pltpu.make_async_copy(w_hbm, w_out, sem)
    copy.start()
    lane = lax.broadcasted_iota(jnp.int32, (1, LANES), 1)
    fine = POOL * CELLS
    for f in range(2):
        for p in range(POOL):
            spot = slice((f * POOL + p) * CELLS, (f * POOL + p + 1) * CELLS)
            pieces = [two_parts(refs[4 * f + c][pl.ds(p, CELLS, stride=POOL), :]) for c in range(4)]
            for part in range(2):
                for c in range(4):
                    parts_ref[spot, part * fine + c * LANES : part * fine + (c + 1) * LANES] = pieces[c][part]
                rim_parts_ref[spot, part * LANES : (part + 1) * LANES] = jnp.where(
                    lane < 64, pieces[0][part], pieces[3][part])
    copy.wait()
    z = dot(rim_parts_ref[...], w_out[: 2 * LANES, 9 * LANES :])
    for p in range(POOL):
        u, v = [z[(f * POOL + p) * CELLS : (f * POOL + p + 1) * CELLS] for f in range(2)]
        both = jnp.where(lane < 64, u, pltpu.roll(v, 64, 1))
        for to_ref in (first_ref, last_ref):
            to_ref[p, :PAD] = jnp.zeros((PAD, LANES), F32)
            to_ref[p, PAD:] = both
    for _ in range(PASSES):
        new = three_rows([pltpu.roll(last_ref[p], LANES - 6, 1) for p in range(POOL)])
        for p in range(POOL):
            last_ref[p] = new[p] + first_ref[p]
    pooled = ((last_ref[0] + last_ref[1]) + (last_ref[2] + last_ref[3])) * SCALE
    rim_ref[: PAD + CELLS] = pooled
    rim_ref[PAD + CELLS :] = pooled[:PAD]
    for start in range(0, EARLY, 2):
        cut = slice(start * LANES, (start + 2) * LANES)
        early_ref[:, cut] = dot(parts_ref[:, :fine], w_out[:, cut]) + dot(parts_ref[:, fine:], w_out[:, cut])


def rim_kernel(above_ref, below_ref, w_ref, rim_in, left_ref, right_ref, own_ref, rows_ref, strip_ref, rim_ref):
    lane = lax.broadcasted_iota(jnp.int32, (1, LANES), 1)
    strip_ref[...] = jnp.zeros_like(strip_ref)
    for s, (x_ref, start) in enumerate(((above_ref, 1), (below_ref, 4))):
        ends = jnp.where(lane < 64, x_ref[:, :LANES], x_ref[:, 3 * LANES :])
        rows_ref[s] = ends
        for f in range(2):
            for p in range(POOL):
                spot = ((f * 2 + s) * POOL + p) * 8 + start
                strip_ref[spot : spot + 3] = rows_ref[s, pl.ds(f * HALO + p, 3, stride=POOL), :]
    z = dot(jnp.concatenate(two_parts(strip_ref[...]), axis=1), w_ref[: 2 * LANES, 9 * LANES :])
    rim_ref[...] = rim_in[...]
    for s, (spot, start) in enumerate(((7, 3), (PAD + CELLS - 2, 2))):
        first = []
        for p in range(POOL):
            u, v = [z[((f * 2 + s) * POOL + p) * 8 : ((f * 2 + s) * POOL + p + 1) * 8] for f in range(2)]
            first.append(jnp.where(lane < 64, u, pltpu.roll(v, 64, 1)))
        powers = [first] + [[pltpu.roll(x, LANES - 6 * j, 1) for x in first] for j in range(1, PASSES + 1)]
        last = powers[PASSES]
        for j in range(PASSES - 1, -1, -1):
            last = [a + b for a, b in zip(three_rows(last), powers[j])]
        pooled = ((last[0] + last[1]) + (last[2] + last[3])) * SCALE
        rim_ref[spot : spot + 3] = rim_ref[spot : spot + 3] + pooled[start : start + 3]
    turned = jnp.transpose(rim_ref[...])
    for to_ref, columns in ((left_ref, (0, 1, 2)), (right_ref, (3, 4, 5)), (own_ref, (1, 4))):
        to_ref[...] = jnp.zeros_like(to_ref)
        for f in range(2):
            for place, c in enumerate(columns):
                spot = len(columns) * f + place
                to_ref[spot : spot + 1] = turned[64 * f + c : 64 * f + c + 1]


PAIRS = [(n, m) for n in range(TERMS) for m in range(n, TERMS)]
REACH = 3


def slopes_of(ref, f, left, right):
    up = ref[f, PAD - 1 : PAD - 1 + CELLS]
    down = ref[f, PAD + 1 : PAD + 1 + CELLS]
    return (right - left) * 0.5, (down - up) * 0.5


def main_kernel(mask_ref, parts_ref, early_ref, w_ref, above_ref, below_ref, _, main_ref, live_ref, inner_ref, rows_ref,
                strip_ref, sum_ref, term_ref):
    strip_ref[...] = jnp.zeros_like(strip_ref)
    for s, (x_ref, start) in enumerate(((above_ref, 5), (below_ref, 8))):
        for c in range(4):
            cut = slice(c * LANES, (c + 1) * LANES)
            rows_ref[s, c] = x_ref[:, cut]
            for f in range(2):
                for p in range(POOL):
                    spot = (f * POOL + p) * 16 + start
                    strip_ref[spot : spot + 3, cut] = rows_ref[s, c, pl.ds(f * HALO + p, 3, stride=POOL), :]
    strips = jnp.concatenate(two_parts(strip_ref[...]), axis=0)
    fine = POOL * CELLS
    for start in range(0, 9, 2):
        wide = min(2, 9 - start)
        w = w_ref[:, start * LANES : (start + wide) * LANES]
        if start < EARLY:
            z = early_ref[:, start * LANES : (start + wide) * LANES]
        else:
            z = dot(parts_ref[:, :fine], w) + dot(parts_ref[:, fine:], w)
        both = dot(strips, w)
        z_strip = both[: both.shape[0] // 2] + both[both.shape[0] // 2 :]
        for stage in range(start, start + wide):
            cut = slice((stage - start) * LANES, (stage - start + 1) * LANES)
            for f in range(2):
                own = []
                for p in range(POOL):
                    block = f * POOL + p
                    own.append(jnp.concatenate([
                        z_strip[block * 16 : block * 16 + 8, cut], z[block * CELLS : (block + 1) * CELLS, cut],
                        z_strip[block * 16 + 8 : block * 16 + 16, cut]], axis=0))
                if stage:
                    own = [a + b for a, b in zip(three_rows([sum_ref[f, p] for p in range(POOL)]), own)]
                for p in range(POOL):
                    sum_ref[f, p] = own[p]
    for f in range(2):
        main_ref[f] = ((sum_ref[f, 0] + sum_ref[f, 1]) + (sum_ref[f, 2] + sum_ref[f, 3])) * SCALE
    lane = lax.broadcasted_iota(jnp.int32, (1, LANES), 1)
    grid = CELLS // SIDE
    for a in range(grid):
        row = jnp.zeros((1, LANES), F32)
        for e in range(grid):
            row = jnp.where(lane // SIDE == e, (mask_ref[a, e] == 1).astype(F32), row)
        live_ref[a * SIDE : (a + 1) * SIDE] = jnp.broadcast_to(row, (SIDE, LANES))
    keep = (live_ref[...] > 0.5) & (lane >= REACH) & (lane < LANES - REACH)
    u, v = [main_ref[f, PAD : PAD + CELLS] for f in range(2)]
    (u_dx, u_dy), (v_dx, v_dy) = [slopes_of(main_ref, f, pltpu.roll(x, 1, 1), pltpu.roll(x, LANES - 1, 1))
                                  for f, x in enumerate((u, v))]
    for n, x in enumerate((u, v, v_dx - u_dy, u_dy + v_dx, u_dx - v_dy)):
        term_ref[n] = jnp.where(keep, x, 0.0)
    for n, x in enumerate(terms_of([term_ref[n] for n in range(BASES)])):
        if n >= BASES:
            term_ref[n] = x
    for place, (n, m) in enumerate(PAIRS):
        product = (term_ref[n] * term_ref[m]).reshape(CELLS // 8, 8, LANES)
        inner_ref[place] = jnp.sum(product, axis=0)


def base_kernel(mask_vmem, owner_vmem, main_ref, live_ref, inner_ref, own_ref, from_left_ref, from_right_ref, place_ref,
                out_ref, field_ref, gram_ref, pack_ref, tile_ref, side_ref, mask_ref, owner_ref, sem):
    tables = [pltpu.make_async_copy(mask_vmem, mask_ref, sem.at[0]),
              pltpu.make_async_copy(owner_vmem, owner_ref, sem.at[1])]
    for table in tables:
        table.start()
    lane = lax.broadcasted_iota(jnp.int32, (1, LANES), 1)
    received = jnp.concatenate([from_left_ref[...], from_right_ref[...], own_ref[...]], axis=0)
    placed = dot(jnp.concatenate(three_parts(received), axis=0), place_ref[...], (((0,), (0,)), ((), ())))
    inner = slice(PAD, PAD + CELLS)
    slopes, beside = [], []
    for f in range(2):
        full = main_ref[f] + placed[:, 2 * f * LANES : (2 * f + 1) * LANES]
        field_ref[f] = full
        rim = placed[inner, (2 * f + 1) * LANES : (2 * f + 2) * LANES]
        centre = full[inner]
        left = jnp.where(lane == 0, rim, pltpu.roll(centre, 1, 1))
        right = jnp.where(lane == LANES - 1, rim, pltpu.roll(centre, LANES - 1, 1))
        beside.append((left, right))
        slopes.append((centre, *slopes_of(field_ref, f, left, right)))
    (u, u_dx, u_dy), (v, v_dx, v_dy) = slopes
    live = live_ref[...] > 0.5
    outer = []
    for x in (u, v, v_dx - u_dy, u_dy + v_dx, u_dx - v_dy):
        x = jnp.where(live, x, 0.0)
        tile = jnp.zeros((8, LANES), F32)
        for b in range(CELLS // 8):
            tile = jnp.where(lane // 8 == b, pltpu.roll(x[8 * b : 8 * b + 8], (REACH + 8 * b) % LANES, 1), tile)
        outer.append(jnp.where(lane % 8 < 2 * REACH, tile, 0.0))
    outer = terms_of(outer)
    for place, (n, m) in enumerate(PAIRS):
        total = jnp.sum(inner_ref[place] + outer[n] * outer[m], axis=0, keepdims=True)
        gram_ref[n * TERMS + m : n * TERMS + m + 1] = total
        if m > n:
            gram_ref[m * TERMS + n : m * TERMS + n + 1] = total
    totals = jnp.sum(gram_ref[...], axis=1, keepdims=True) * (1.0 / (CELLS * CELLS))
    row = lax.broadcasted_iota(jnp.int32, (TERMS * TERMS, 1), 0)
    spread = jnp.where(row % LANES == lane, totals, 0.0)
    halves = [jnp.sum(spread[h * LANES : (h + 1) * LANES], axis=0, keepdims=True) for h in range(2)]
    owners = out_ref.shape[0]
    grid = CELLS // SIDE
    nothing = grid * grid
    for table in tables:
        table.wait()
    for o in range(owners + 1):
        tile_ref[o] = nothing
    for a in range(grid):
        for e in range(grid):
            tile_ref[jnp.where(mask_ref[a, e] == 1, owner_ref[a, e], owners)] = a * grid + e
    pack_ref[nothing] = jnp.zeros((BLOCK_ROWS, LANES), F32)
    group = lane // SIDE
    rims = jnp.where(lane % SIDE == 0, beside[0][0], pltpu.roll(beside[1][0], 1, 1))
    rims = jnp.where(lane % SIDE == SIDE - 1, beside[0][1], rims)
    side_ref[...] = jnp.transpose(jnp.where(lane % SIDE == SIDE - 2, pltpu.roll(beside[1][1], LANES - 1, 1), rims))
    for a in range(grid):
        ends = []
        for f in range(2):
            pieces = [field_ref[f, pl.ds(PAD + a * SIDE + q, 8, stride=4), :] for q in range(grid)]
            for e in range(grid):
                block = None
                for q in range(grid):
                    x = pltpu.roll(pieces[q], (q - e) % grid * SIDE, 1) if q != e else pieces[q]
                    block = x if block is None else jnp.where(group == q, x, block)
                pack_ref[a * grid + e, 8 * f : 8 * f + 8] = block
            for side in range(2):
                ends.append(field_ref[f, PAD + a * SIDE - 1 + side * (SIDE + 1) : PAD + a * SIDE + side * (SIDE + 1)])
        for e in range(grid):
            sides = [side_ref[e * SIDE + at : e * SIDE + at + 1] for at in (0, SIDE - 1, 1, SIDE - 2)]
            for spot, parts, own in ((SIDES, sides, a), (ENDS, ends, e)):
                row = None
                for q in range(4):
                    x = pltpu.roll(parts[q], (q - own) % 4 * SIDE, 1) if q != own else parts[q]
                    row = x if row is None else jnp.where(group == q, x, row)
                pack_ref[a * grid + e, spot : spot + 1] = row
    for o in range(owners):
        out_ref[o] = pack_ref[tile_ref[o]]
        for h in range(2):
            out_ref[o, GRAM + h : GRAM + h + 1] = halves[h]


def terms_of(base):
    u, v, vort, strain, stretch = base
    return [u, v, vort, strain, stretch, vort * vort, vort * strain, vort * stretch, strain * strain, stretch * stretch,
            strain * stretch, u * vort, v * vort, u * strain, v * stretch, u * v]


def library_kernel(x_ref, out_hbm, out_ref, sem):
    slots = x_ref.shape[0] // BLOCK_ROWS
    rows = lambda at: x_ref[pl.ds(at, slots, stride=BLOCK_ROWS), :]
    turn_by = lambda x, count: pltpu.roll(x, count % LANES, 1) if count % LANES else x
    lane = lax.broadcasted_iota(jnp.int32, (1, LANES), 1)
    sides, ends = rows(SIDES), rows(ENDS)
    fields = [[rows(8 * f + k) for k in range(8)] for f in range(2)]
    lower = [[turn_by(x, SIDE) for x in field] for field in fields]
    higher = [[turn_by(x, -SIDE) for x in field] for field in fields]

    def slopes(f, k):
        x = fields[f][k]
        left, right = turn_by(x, 1), turn_by(x, -1)
        for q in range(4):
            start = 64 * f + 4 * k + q
            left = jnp.where(lane == SIDE * q, turn_by(sides, SIDE * q - start), left)
            right = jnp.where(lane == SIDE * (q + 1) - 1, turn_by(sides, SIDE * q - 1 - start), right)
        before = lower[f][k - 1] if k else turn_by(ends, -64 * f)
        after = higher[f][k + 1] if k < 7 else turn_by(ends, 64 - 64 * f)
        up = jnp.where(lane < SIDE, before, lower[f][k])
        down = jnp.where(lane >= LANES - SIDE, after, higher[f][k])
        return (right - left) * 0.5, (down - up) * 0.5

    copies = []
    for k in range(8):
        (u_dx, u_dy), (v_dx, v_dy) = slopes(0, k), slopes(1, k)
        base = [fields[0][k], fields[1][k], v_dx - u_dy, u_dy + v_dx, u_dx - v_dy]
        for n, x in enumerate(terms_of(base)):
            out_ref[k, pl.ds(n, slots, stride=TERMS), :] = x
        copies.append(pltpu.make_async_copy(out_ref.at[k], out_hbm.at[:, pl.ds(k * LANES, LANES)], sem.at[k]))
        copies[k].start()
    for copy in copies:
        copy.wait()


VMEM = pl.BlockSpec(memory_space=pltpu.VMEM)
HBM = pl.BlockSpec(memory_space=pltpu.HBM)
SMEM = pl.BlockSpec(memory_space=pltpu.SMEM)
PARAMS = pltpu.CompilerParams(vmem_limit_bytes=24 << 20)


def struct(*shape):
    return jax.ShapeDtypeStruct(shape, F32)


def per_device(u_velocity, v_velocity, ocean_mask, tile_owner, lower_edge_quarter_turns):
    tiles, columns = lax.axis_size("tile"), lax.axis_size("col")
    onward = lambda count: [(i, (i + 1) % count) for i in range(count)]
    back = lambda count: [((i + 1) % count, i) for i in range(count)]
    here = lax.axis_index("tile").astype(jnp.int32)[None]
    in_hbm = lambda x: pltpu.with_memory_space_constraint(x, pltpu.HBM)
    up, down = pl.pallas_call(
        send_kernel,
        out_shape=[struct(2 * HALO, POOL * CELLS)] * 2,
        in_specs=[SMEM] + [HBM] * 3,
        out_specs=[VMEM] * 2,
        scratch_shapes=[pltpu.VMEM((2, 2, 16, POOL * CELLS), F32), pltpu.SMEM((tiles,), jnp.int32),
                        pltpu.SemaphoreType.DMA((2, 2)), pltpu.SemaphoreType.DMA],
        compiler_params=PARAMS,
        name="send_rows",
    )(here, *[in_hbm(x) for x in (lower_edge_quarter_turns, u_velocity, v_velocity)])
    up, down, u_velocity, v_velocity = lax.optimization_barrier((up, down, u_velocity, v_velocity))
    above = lax.ppermute(down, "tile", onward(tiles))
    below = lax.ppermute(up, "tile", back(tiles))
    column = lambda c: pl.BlockSpec((POOL * CELLS, LANES), lambda i: (0, c))
    rows = 2 * POOL * CELLS
    parts, weights, rim, early = pl.pallas_call(
        prepare_kernel,
        out_shape=[jax.ShapeDtypeStruct((rows, 2 * POOL * CELLS), BF16),
                   jax.ShapeDtypeStruct((POOL * CELLS, 10 * LANES), BF16), struct(FULL, LANES),
                   struct(rows, EARLY * LANES)],
        grid=(1,),
        in_specs=[column(c) for c in range(4)] * 2 + [HBM],
        out_specs=[VMEM] * 4,
        scratch_shapes=[pltpu.VMEM((rows, 2 * LANES), BF16)] + [pltpu.VMEM((POOL, PAD + CELLS, LANES), F32)] * 2
        + [pltpu.SemaphoreType.DMA],
        compiler_params=PARAMS,
        name="prepare_rows",
    )(*[u_velocity] * 4, *[v_velocity] * 4, in_hbm(jnp.asarray(column_weights())))
    to_left, to_right, own = pl.pallas_call(
        rim_kernel,
        out_shape=[struct(8, FULL), struct(8, FULL), struct(16, FULL)],
        in_specs=[VMEM] * 4,
        out_specs=[VMEM] * 3,
        scratch_shapes=[pltpu.VMEM((2, 2 * HALO, LANES), F32), pltpu.VMEM((2 * 2 * POOL * 8, LANES), F32),
                        pltpu.VMEM((FULL, LANES), F32)],
        compiler_params=PARAMS,
        name="rim_columns",
    )(above, below, weights, rim)
    from_right = lax.ppermute(to_left, "col", back(columns))
    from_left = lax.ppermute(to_right, "col", onward(columns))
    main, live, inner = pl.pallas_call(
        main_kernel,
        out_shape=[struct(2, FULL, LANES), struct(CELLS, LANES), struct(len(PAIRS), 8, LANES)],
        in_specs=[SMEM] + [VMEM] * 6,
        out_specs=[VMEM] * 3,
        scratch_shapes=[pltpu.VMEM((2, 4, 2 * HALO, LANES), F32), pltpu.VMEM((2 * POOL * 16, POOL * CELLS), F32),
                        pltpu.VMEM((2, POOL, FULL, LANES), F32), pltpu.VMEM((TERMS, CELLS, LANES), F32)],
        compiler_params=PARAMS,
        name="main_columns",
    )(ocean_mask, parts, early, weights, above, below, own)
    blocks = pl.pallas_call(
        base_kernel,
        out_shape=struct(tiles, BLOCK_ROWS, LANES),
        in_specs=[VMEM] * 9,
        out_specs=VMEM,
        scratch_shapes=[pltpu.VMEM((2, FULL, LANES), F32), pltpu.VMEM((TERMS * TERMS, LANES), F32),
                        pltpu.VMEM((17, BLOCK_ROWS, LANES), F32), pltpu.SMEM((tiles + 1,), jnp.int32),
                        pltpu.VMEM((LANES, CELLS), F32), pltpu.SMEM(ocean_mask.shape, jnp.int32),
                        pltpu.SMEM(tile_owner.shape, jnp.int32), pltpu.SemaphoreType.DMA((2,))],
        compiler_params=PARAMS,
        name="base_fields",
    )(ocean_mask, tile_owner, main, live, inner, own, from_left, from_right, jnp.asarray(place_matrix()))
    blocks = lax.all_to_all(blocks, "tile", split_axis=0, concat_axis=0, tiled=True)
    gram = jnp.sum(blocks[:, GRAM : GRAM + 2], axis=0)
    gram = lax.all_to_all(jnp.broadcast_to(gram, (columns, 2, LANES)), "col", split_axis=0, concat_axis=0, tiled=True)
    library = pl.pallas_call(
        library_kernel,
        out_shape=struct(tiles * TERMS, SIDE * SIDE),
        in_specs=[VMEM],
        out_specs=HBM,
        scratch_shapes=[pltpu.VMEM((8, tiles * TERMS, LANES), F32), pltpu.SemaphoreType.DMA((8,))],
        compiler_params=PARAMS,
        cost_estimate=pl.CostEstimate(flops=2 * tiles * TERMS * SIDE * SIDE, transcendentals=0,
                                      bytes_accessed=5 * tiles * TERMS * SIDE * SIDE),
        name="library_terms",
    )(blocks.reshape(tiles * BLOCK_ROWS, LANES))
    gram = jnp.sum(gram, axis=0).reshape(TERMS, TERMS)
    return library.reshape(1, 1, tiles, TERMS, SIDE * SIDE), gram


def solution(mesh):
    in_specs = (P("tile", "col"), P("tile", "col"), P("tile", "col"), P("tile", "col"), P())
    out_specs = (P("tile", "col", None, None, None), P())
    return jax.shard_map(
        per_device, mesh=mesh, in_specs=in_specs, out_specs=out_specs, check_vma=False
    )
```
